32 devices in a mesh: row: 8 (over z, core), col: 4 (over y, x).
Axes of the slice: x: 2, y: 2, z: 4, core: 2. Of those that a mesh axis runs over, the one named last changes fastest.
Arguments:
- hidden: bfloat16 [1024, 2560], P('row'), may hold values from -4 to 4
- rel_bins: int32 [1024, 1024], P('row', 'col'), may hold values from 0 to 64, as said below
- attn_gain: float32 [2560], replicated, may hold values from 0.25 to 1.75
- w_query: bfloat16 [2560, 2560], P(None, 'col'), may hold values from -0.25 to 0.25
- w_key: bfloat16 [2560, 2560], P(None, 'col'), may hold values from -0.25 to 0.25
- w_value: bfloat16 [2560, 2560], P(None, 'col'), may hold values from -0.125 to 0.125
- w_out: bfloat16 [2560, 2560], P('col'), may hold values from -0.125 to 0.125
- final_gain: float32 [2560], P('col'), may hold values from 0.25 to 1.75
- w_single: bfloat16 [2560, 1024], P('col'), may hold values from -0.125 to 0.125
- w_second: bfloat16 [1024, 1024], replicated, may hold values from -0.1875 to 0.1875
- w_left: bfloat16 [1024, 128], replicated, may hold values from -0.1875 to 0.1875
- w_right: bfloat16 [1024, 128], replicated, may hold values from -0.1875 to 0.1875
- rel_table: bfloat16 [65, 128], replicated, may hold values from -6 to 6
- pair_gain: float32 [128], replicated, may hold values from 0.25 to 1.75
- w_expand: bfloat16 [128, 512], replicated, may hold values from -0.5 to 0.5
- w_contract: bfloat16 [512, 128], replicated, may hold values from -0.25 to 0.25
Outputs:
- pair_rep: bfloat16 [1024, 1024, 128], P('row', 'col')
The draws below stay inside these ranges and needn't reach their ends.
Inputs may be any that keep to these rules, and one draw needn't show every extreme that they name: rel_bins[i, j] is the difference of the residue numbers of j and i, clipped to plus or minus (64) // 2 and shifted by (64) // 2.
All inputs are finite; a program needn't handle non-finite values.
Results may differ from the reference program's by a relative error of at most 0.013.
Values may be sent and summed in bfloat16 or wider, within the bound.
A program may use at most 128 MiB of HBM per device.

```python
import math
import jax
import jax.numpy as jnp
from jax import lax

D = 2560
H = 40
HD = 64
CS = 1024
CZ = 128
CH = 512
NB = 65
L = 1024


def draw_hidden(key, part):
    place = jnp.arange(D, dtype=jnp.float32) / (D - 1)
    base = jnp.clip(jax.random.normal(key, (L, D), jnp.float32), -3.0, 3.0)
    result = base * (4.0 / 9.0) * 3.0 ** place[None, :]
    return result.astype(jnp.bfloat16)


def draw_rel_bins(key, part):
    first_key, second_key = jax.random.split(jax.random.fold_in(key, 17), 2)
    breaks = jax.random.randint(first_key, (L,), 0, 48, dtype=jnp.int32) == 0
    jumps = jax.random.randint(second_key, (L,), 1, 200, dtype=jnp.int32)
    strides = 1 + jnp.where(breaks, jumps, 0)
    numbers = jnp.cumsum(strides).astype(jnp.int32)
    reach = (NB - 1) // 2
    difference = numbers[None, :] - numbers[:, None]
    return (jnp.clip(difference, -reach, reach) + reach).astype(jnp.int32)


def level_of(stream_key, dims, shards, low, top_value):
    def one(position, shards_of):
        steps = jax.random.uniform(jax.random.fold_in(jax.random.fold_in(stream_key, 6), position), (shards_of,), jnp.float32, low / len(shards), top_value / len(shards))
        return jnp.repeat(jnp.exp(steps), dims[position] // shards_of).reshape((-1,) + (1,) * (len(dims) - position - 1))

    level = one(*shards[0])
    for cut in shards[1:]:
        level = level * one(*cut)
    return level


def centred(key, dims, spread, limit, cuts=(), kind=jnp.bfloat16):
    values = spread * jax.random.normal(key, dims, jnp.float32)
    if cuts:
        values = values * level_of(key, dims, cuts, -0.22, 0.18)
    return jnp.clip(values, -limit, limit).astype(kind)


def setup_inputs(seed: int = 0) -> dict:
    key_list = jax.random.split(jax.random.key(seed), 17)
    hidden = draw_hidden(jax.random.fold_in(key_list[16], 71), 0)
    rel_bins = draw_rel_bins(jax.random.fold_in(key_list[16], 71), 0)
    attn_gain = jnp.clip(1.0 + 0.15 * jax.random.normal(key_list[2], (D,), jnp.float32), 0.25, 1.75)
    w_query = centred(key_list[3], (D, D), (D // 4) ** -0.5, 0.25, ((1, 4),))
    w_key = centred(key_list[4], (D, D), (D // 4) ** -0.5, 0.25, ((1, 4),))
    w_value = centred(key_list[5], (D, D), D ** -0.5, 0.125, ((1, 4),))
    w_out = centred(key_list[6], (D, D), D ** -0.5, 0.125, ((0, 4),))
    final_gain = jnp.clip(1.0 + 0.15 * jax.random.normal(key_list[7], (D,), jnp.float32), 0.25, 1.75)
    w_single = centred(key_list[8], (D, CS), D ** -0.5, 0.125, ((0, 4),))
    w_second = centred(key_list[9], (CS, CS), CS ** -0.5, 0.1875)
    w_left = centred(key_list[10], (CS, CZ), CS ** -0.5, 0.1875)
    w_right = centred(key_list[11], (CS, CZ), CS ** -0.5, 0.1875)
    rel_table = centred(key_list[12], (NB, CZ), 1.0, 6.0)
    pair_gain = jnp.clip(1.0 + 0.15 * jax.random.normal(key_list[13], (CZ,), jnp.float32), 0.25, 1.75)
    w_expand = centred(key_list[14], (CZ, CH), CZ ** -0.5, 0.5)
    w_contract = centred(key_list[15], (CH, CZ), CH ** -0.5, 0.25)
    return dict(hidden=hidden, rel_bins=rel_bins, attn_gain=attn_gain, w_query=w_query, w_key=w_key, w_value=w_value, w_out=w_out, final_gain=final_gain, w_single=w_single, w_second=w_second, w_left=w_left, w_right=w_right, rel_table=rel_table, pair_gain=pair_gain, w_expand=w_expand, w_contract=w_contract)


epsilon = 1e-05

def layer_norm(values, gain):
    count = values.shape[-1]
    average = lax.optimization_barrier(jnp.sum(values, -1, keepdims=True)) / count
    variance = lax.optimization_barrier(jnp.sum(values * values, -1, keepdims=True)) / count - average * average
    return (values - average) * lax.rsqrt(variance + epsilon) * gain

def rotary(vectors, positions):
    half_size = vectors.shape[-1] // 2
    frequency = jnp.exp(jnp.arange(half_size, dtype=jnp.float32) * (-2.0 * math.log(10000.0) / vectors.shape[-1]))
    angles = positions.astype(jnp.float32)[:, None] * frequency[None, :]
    angles = jnp.concatenate([angles, angles], -1)[:, None, :]
    turned = jnp.concatenate([-vectors[..., half_size:], vectors[..., :half_size]], -1)
    return vectors * jnp.cos(angles) + turned * jnp.sin(angles)

def one_head(entries):
    query_head, key_head, value_head = entries
    scores = jnp.dot(query_head, key_head.T, preferred_element_type=jnp.float32)
    weights = jnp.exp(scores)
    totals = lax.optimization_barrier(jnp.sum(weights, -1, keepdims=True))
    numerator = jnp.dot(weights.astype(jnp.bfloat16), value_head, preferred_element_type=jnp.float32)
    return (numerator / totals).astype(jnp.bfloat16)

def reference(hidden, rel_bins, attn_gain, w_query, w_key, w_value, w_out, final_gain, w_single, w_second, w_left, w_right, rel_table, pair_gain, w_expand, w_contract):
    residues = hidden.shape[0]
    positions = jnp.arange(residues, dtype=jnp.int32)
    stream = hidden.astype(jnp.float32)
    attn_in = layer_norm(stream, attn_gain).astype(jnp.bfloat16)
    query = jnp.dot(attn_in, w_query, preferred_element_type=jnp.float32) * HD ** (-0.5)
    query = rotary(query.reshape(residues, H, HD), positions).astype(jnp.bfloat16)
    keys = jnp.dot(attn_in, w_key, preferred_element_type=jnp.float32)
    keys = rotary(keys.reshape(residues, H, HD), positions).astype(jnp.bfloat16)
    values = jnp.dot(attn_in, w_value, preferred_element_type=jnp.float32).astype(jnp.bfloat16).reshape(residues, H, HD)
    context = lax.map(one_head, (jnp.transpose(query, (1, 0, 2)), jnp.transpose(keys, (1, 0, 2)), jnp.transpose(values, (1, 0, 2))))
    context = jnp.transpose(context, (1, 0, 2)).reshape(residues, H * HD)
    resid = stream + jnp.dot(context, w_out, preferred_element_type=jnp.float32)
    final = layer_norm(resid, final_gain).astype(jnp.bfloat16)
    lifted = jnp.maximum(jnp.dot(final, w_single, preferred_element_type=jnp.float32), 0.0).astype(jnp.bfloat16)
    single = jnp.dot(lifted, w_second, preferred_element_type=jnp.float32).astype(jnp.bfloat16)
    left = jnp.dot(single, w_left, preferred_element_type=jnp.float32).astype(jnp.bfloat16)
    right = jnp.dot(single, w_right, preferred_element_type=jnp.float32).astype(jnp.bfloat16)
    left_wide = left.astype(jnp.float32)
    right_wide = right.astype(jnp.float32)
    block_rows = math.gcd(residues, 128)

    def pair_tile(entries):
        bin_block, left_block = entries
        pair_in = left_block[:, None, :] + right_wide[None, :, :] + jnp.take(rel_table, bin_block, axis=0).astype(jnp.float32)
        normed = layer_norm(pair_in, pair_gain).astype(jnp.bfloat16)
        flat = normed.reshape(-1, normed.shape[-1])
        expanded = jnp.maximum(jnp.dot(flat, w_expand, preferred_element_type=jnp.float32), 0.0).astype(jnp.bfloat16)
        update = jnp.dot(expanded, w_contract, preferred_element_type=jnp.float32).reshape(pair_in.shape)
        return (pair_in + update).astype(jnp.bfloat16)
    pair_rep = lax.map(pair_tile, (rel_bins.reshape(residues // block_rows, block_rows, residues), left_wide.reshape(residues // block_rows, block_rows, -1)))
    return pair_rep.reshape(residues, residues, -1)
```

```python
import functools
import math

import jax
import jax.numpy as jnp
import numpy as np
from jax import lax
from jax.experimental import pallas as pl
from jax.experimental.pallas import tpu as pltpu
from jax.sharding import PartitionSpec as P

HD = 64
MESH = pl.DeviceIdType.MESH


epsilon = 1e-05


def pair_kernel(bins_ref, left_ref, right_ref, table_ref, gain_ref, expand_ref, contract_ref, out_ref, table):
    block_rows, col_count = bins_ref.shape
    channels = right_ref.shape[1]
    right = right_ref[...].astype(jnp.float32)
    bins = table_ref.shape[0]

    @pl.when(pl.program_id(0) == 0)
    def _():
        table[...] = jnp.zeros_like(table)
        table[:bins] = table_ref[...]

    codes = lax.broadcasted_iota(jnp.int32, (table.shape[0], col_count), 0)
    hot = jnp.concatenate(
        [
            jnp.where(bins_ref[i : i + 1, :] == codes, 1.0, 0.0).astype(jnp.bfloat16)
            for i in range(block_rows)
        ],
        1,
    )
    part = lax.dot_general(
        hot, table[...], (((0,), (0,)), ((), ())), preferred_element_type=jnp.float32
    )
    pair_in = jnp.concatenate(
        [
            part[i * col_count : (i + 1) * col_count]
            + (right + left_ref[i : i + 1, :].astype(jnp.float32))
            for i in range(block_rows)
        ],
        0,
    )
    average = jnp.sum(pair_in, -1, keepdims=True) / channels
    variance = jnp.sum(pair_in * pair_in, -1, keepdims=True) / channels - average * average
    normed = ((pair_in - average) * lax.rsqrt(variance + epsilon) * gain_ref[...]).astype(
        jnp.bfloat16
    )
    expanded = jnp.dot(normed, expand_ref[...], preferred_element_type=jnp.float32)
    expanded = jnp.maximum(expanded.astype(jnp.bfloat16), 0)
    update = jnp.dot(expanded, contract_ref[...], preferred_element_type=jnp.float32)
    out_ref[...] = (pair_in + update).astype(out_ref.dtype).reshape(out_ref.shape)


def pair_stage(rel_bins, left, right, rel_table, pair_gain, w_expand, w_contract):
    row_count, col_count = rel_bins.shape
    channels = right.shape[1]
    block_rows = math.gcd(row_count, 32)
    bins_padded = -(-rel_table.shape[0] // 128) * 128
    whole = lambda array: pl.BlockSpec(array.shape, lambda i: (0, 0))
    gain = pair_gain.reshape(1, channels)
    return pl.pallas_call(
        pair_kernel,
        grid=(row_count // block_rows,),
        in_specs=[
            pl.BlockSpec((block_rows, col_count), lambda i: (i, 0)),
            pl.BlockSpec((block_rows, channels), lambda i: (i, 0)),
            whole(right),
            whole(rel_table),
            whole(gain),
            whole(w_expand),
            whole(w_contract),
        ],
        out_specs=pl.BlockSpec((block_rows, col_count, channels), lambda i: (i, 0, 0)),
        out_shape=jax.ShapeDtypeStruct((row_count, col_count, channels), jnp.bfloat16),
        scratch_shapes=[pltpu.VMEM((bins_padded, channels), jnp.bfloat16)],
        compiler_params=pltpu.CompilerParams(
            dimension_semantics=("arbitrary",), vmem_limit_bytes=56 << 20
        ),
    )(rel_bins, left, right, rel_table, gain, w_expand, w_contract)


def front_kernel(
    rows,
    cols,
    model_width,
    hidden_ref,
    own_hbm,
    attn_gain_ref,
    cos_ref,
    sin_ref,
    final_gain_ref,
    w_query_hbm,
    w_key_hbm,
    w_value_hbm,
    w_out_hbm,
    w_single_hbm,
    w_second_hbm,
    w_left_ref,
    w_right_ref,
    left_ref,
    right_ref,
    w_query,
    w_key,
    w_value,
    w_out,
    w_single,
    w_second,
    own,
    kv,
    query,
    totals,
    numerator,
    context,
    out_send,
    out_recv,
    stat_send,
    stat_recv,
    single_own,
    single_send,
    single_recv,
    sides,
    right_own,
    right_all,
    weight_sem,
    kv_send_sem,
    kv_recv_sem,
    out_send_sem,
    out_recv_sem,
    stat_send_sem,
    stat_recv_sem,
    single_send_sem,
    single_recv_sem,
    sides_send_sem,
    sides_recv_sem,
    right_send_sem,
    right_recv_sem,
):
    row = lax.axis_index("row")
    col = lax.axis_index("col")
    count = hidden_ref.shape[0]
    pairs = query.shape[0]
    features = w_single.shape[0]
    piece = single_own.shape[1]
    owners = rows // cols
    chips = rows // 2
    chip = row // 2
    core = row % 2
    partner = row + 1 - 2 * core

    own_columns = pl.ds(pl.multiple_of(col * features, 128), features)
    loads = []
    for index, (source, target) in enumerate(
        (
            (w_key_hbm, w_key),
            (w_value_hbm, w_value),
            (w_query_hbm, w_query),
            (w_out_hbm, w_out),
            (w_single_hbm, w_single),
            (w_second_hbm, w_second),
            (own_hbm.at[:, own_columns], own),
        )
    ):
        load = pltpu.make_async_copy(source, target, weight_sem.at[index])
        load.start()
        loads.append(load)

    barrier = pltpu.get_barrier_semaphore()
    is_owner = row // owners == col

    def greet(target_row, target_col):
        pl.semaphore_signal(
            barrier, inc=1, device_id=(target_row, target_col), device_id_type=MESH
        )

    greet(partner, col)

    @pl.when(chip + 1 < chips)
    def _():
        greet(row + 2, col)

    @pl.when(chip >= 1)
    def _():
        greet(row - 2, col)

    for slot in range(owners):
        for index in range(cols):

            @pl.when(jnp.logical_or(row != col * owners + slot, col != index))
            def _():
                greet(col * owners + slot, index)

    greetings = cols + rows
    greetings += jnp.where(chip + 1 < chips, 1, 0) + jnp.where(chip >= 1, 1, 0)
    greetings -= jnp.where(is_owner, 1, 0)
    for step in range(1, cols):
        pl.semaphore_signal(
            barrier, inc=1, device_id=(row, (col + step) % cols), device_id_type=MESH
        )

    stream = hidden_ref[...].astype(jnp.float32)
    average = jnp.sum(stream, -1, keepdims=True) / model_width
    variance = jnp.sum(stream * stream, -1, keepdims=True) / model_width - average * average
    attn_in = (
        (stream - average) * lax.rsqrt(variance + epsilon) * attn_gain_ref[...].reshape(1, -1)
    ).astype(jnp.bfloat16)
    cosine = cos_ref[...]
    sine = sin_ref[...]
    lane = lax.broadcasted_iota(jnp.int32, (count, 128), 1)
    first_half = lane % HD < HD // 2
    first_head = lane < HD

    def rope(vectors):
        turned = jnp.where(
            first_half,
            pltpu.roll(vectors, 128 - HD // 2, 1),
            pltpu.roll(vectors, HD // 2, 1),
        )
        return vectors * cosine + turned * sine

    def kv_copy(source, chunk, way, target):
        return pltpu.make_async_remote_copy(
            src_ref=kv.at[source, chunk],
            dst_ref=kv.at[source, chunk],
            send_sem=kv_send_sem.at[way, source, chunk],
            recv_sem=kv_recv_sem.at[source, chunk],
            device_id=(target, col),
            device_id_type=MESH,
        )

    def pass_on(source, chunk, right, left, act):
        if right:

            @pl.when(chip + 1 < chips)
            def _():
                act(kv_copy(source, chunk, 0, row + 2))

        if left:

            @pl.when(chip >= 1)
            def _():
                act(kv_copy(source, chunk, 1, row - 2))

        act(kv_copy(source, chunk, 2, partner))

    def start(copy):
        copy.start()

    def finish(copy):
        copy.wait_send()

    loads[0].wait()
    projected = jnp.dot(attn_in, w_key[...], preferred_element_type=jnp.float32)
    for pair in range(pairs):
        kv[row, 0, pair] = rope(projected[:, pair * 128 : pair * 128 + 128]).astype(jnp.bfloat16)
    pl.semaphore_wait(barrier, greetings)
    pass_on(row, 0, True, True, start)
    loads[1].wait()
    projected = jnp.dot(attn_in, w_value[...], preferred_element_type=jnp.float32)
    for pair in range(pairs):
        kv[row, 1, pair] = projected[:, pair * 128 : pair * 128 + 128].astype(jnp.bfloat16)
    pass_on(row, 1, True, True, start)
    loads[2].wait()
    projected = jnp.dot(attn_in, w_query[...], preferred_element_type=jnp.float32) * HD ** (-0.5)
    for pair in range(pairs):
        turned = rope(projected[:, pair * 128 : pair * 128 + 128])
        query[pair, :count] = jnp.where(first_head, turned, 0.0).astype(jnp.bfloat16)
        query[pair, count:] = jnp.where(first_head, 0.0, turned).astype(jnp.bfloat16)
    totals[...] = jnp.zeros_like(totals)
    numerator[...] = jnp.zeros_like(numerator)

    def attend(source):
        for pair in range(pairs):
            scores = lax.dot_general(
                query[pair],
                kv[source, 0, pair],
                (((1,), (1,)), ((), ())),
                preferred_element_type=jnp.float32,
            )
            weights = jnp.exp(scores)
            totals[pair] += weights
            numerator[pair] += jnp.dot(
                weights.astype(jnp.bfloat16),
                kv[source, 1, pair],
                preferred_element_type=jnp.float32,
            )

    def arrive(source):
        for chunk in range(2):
            kv_copy(source, chunk, 2, partner).wait_recv()

    attend(row)
    arrive(partner)
    attend(partner)

    @pl.loop(1, chips)
    def _(step):
        from_left = chip - step >= 0
        from_right = chip + step < chips
        for chunk in range(2):

            @pl.when(from_left)
            def _():
                source = row - 2 * step
                kv_copy(source, chunk, 2, partner).wait_recv()
                pass_on(source, chunk, True, False, start)

            @pl.when(from_right)
            def _():
                source = row + 2 * step
                kv_copy(source, chunk, 2, partner).wait_recv()
                pass_on(source, chunk, False, True, start)

        @pl.when(from_left)
        def _():
            attend(row - 2 * step)
            arrive(partner - 2 * step)
            attend(partner - 2 * step)

        @pl.when(from_right)
        def _():
            attend(row + 2 * step)
            arrive(partner + 2 * step)
            attend(partner + 2 * step)

    for pair in range(pairs):
        shares = numerator[pair] / jnp.sum(totals[pair], -1, keepdims=True)
        context[:, pair * 128 : pair * 128 + 128] = jnp.where(
            first_head, shares[:count], shares[count:]
        ).astype(jnp.bfloat16)

    def out_copy(source, target):
        return pltpu.make_async_remote_copy(
            src_ref=out_send.at[target],
            dst_ref=out_recv.at[source],
            send_sem=out_send_sem.at[target],
            recv_sem=out_recv_sem.at[source],
            device_id=(row, target),
            device_id_type=MESH,
        )

    def out_part(target):
        columns = pl.ds(pl.multiple_of(target * features, 128), features)
        return jnp.dot(context[...], w_out[:, columns], preferred_element_type=jnp.float32)

    others = [(col + step) % cols for step in range(1, cols)]
    loads[3].wait()
    for target in others:
        out_send[target] = out_part(target).astype(jnp.bfloat16)
        out_copy(col, target).start()
    loads[6].wait()
    resid = own[...].astype(jnp.float32) + out_part(col)
    for source in others:
        out_copy(source, source).wait_recv()
        resid += out_recv[source].astype(jnp.float32)

    def stat_copy(source, target):
        return pltpu.make_async_remote_copy(
            src_ref=stat_send,
            dst_ref=stat_recv.at[source],
            send_sem=stat_send_sem.at[target],
            recv_sem=stat_recv_sem.at[source],
            device_id=(row, target),
            device_id_type=MESH,
        )

    sum_first = jnp.sum(resid, -1, keepdims=True)
    sum_second = jnp.sum(resid * resid, -1, keepdims=True)
    sums = jnp.transpose(jnp.where(lane < 4, sum_first, sum_second))[:8]
    stat_send[...] = sums
    for target in others:
        stat_copy(col, target).start()
    for source in others:
        stat_copy(source, source).wait_recv()
        sums += stat_recv[source]
    sums = jnp.transpose(jnp.concatenate([sums] * 16, 0))
    average = sums[:, 0:1] / model_width
    variance = sums[:, 4:5] / model_width - average * average
    final = (
        (resid - average) * lax.rsqrt(variance + epsilon) * final_gain_ref[...].reshape(1, -1)
    ).astype(jnp.bfloat16)

    def single_copy(source, target):
        return pltpu.make_async_remote_copy(
            src_ref=single_send.at[target],
            dst_ref=single_recv.at[source],
            send_sem=single_send_sem.at[target],
            recv_sem=single_recv_sem.at[source],
            device_id=(row, target),
            device_id_type=MESH,
        )

    loads[4].wait()
    part = jnp.dot(final, w_single[...], preferred_element_type=jnp.float32)
    for index in range(cols):
        block = part[index * piece : (index + 1) * piece]
        single_own[index] = block
        single_send[index] = block.astype(jnp.bfloat16)
    for target in others:
        single_copy(col, target).start()
    summed = single_own[col]
    for source in others:
        single_copy(source, source).wait_recv()
        summed += single_recv[source].astype(jnp.float32)
    lifted = jnp.maximum(summed, 0.0).astype(jnp.bfloat16)
    loads[5].wait()
    single = jnp.dot(lifted, w_second[...], preferred_element_type=jnp.float32)
    single = single.astype(jnp.bfloat16)

    def sides_copy(source, target):
        return pltpu.make_async_remote_copy(
            src_ref=sides.at[source],
            dst_ref=sides.at[source],
            send_sem=sides_send_sem.at[target],
            recv_sem=sides_recv_sem.at[source],
            device_id=(row, target),
            device_id_type=MESH,
        )

    def right_copy(slot, index, step):
        return pltpu.make_async_remote_copy(
            src_ref=right_own,
            dst_ref=right_all.at[slot, index],
            send_sem=right_send_sem.at[step],
            recv_sem=right_recv_sem.at[slot, index],
            device_id=((row + step) % rows, row // owners),
            device_id_type=MESH,
        )

    right_own[...] = jnp.dot(
        single, w_right_ref[...], preferred_element_type=jnp.float32
    ).astype(jnp.bfloat16)
    for step in range(1, rows):
        right_copy(row % owners, col, step).start()

    @pl.when(jnp.logical_not(is_owner))
    def _():
        right_copy(row % owners, col, 0).start()

    sides[col] = jnp.dot(single, w_left_ref[...], preferred_element_type=jnp.float32).astype(
        jnp.bfloat16
    )
    for target in others:
        sides_copy(col, target).start()

    @pl.when(is_owner)
    def _():
        right_all[row % owners, col] = right_own[...]

    for source in others:
        sides_copy(source, source).wait_recv()
    for index in range(cols):
        left_ref[index * piece : (index + 1) * piece] = sides[index]
    for slot in range(owners):
        for index in range(cols):

            @pl.when(jnp.logical_or(row != col * owners + slot, col != index))
            def _():
                right_copy(slot, index, 1).wait_recv()

            start_row = slot * count + index * piece
            right_ref[start_row : start_row + piece] = right_all[slot, index]

    for chunk in range(2):
        pass_on(row, chunk, True, True, finish)

    @pl.loop(1, chips)
    def _(step):
        for chunk in range(2):

            @pl.when(chip - step >= 0)
            def _():
                pass_on(row - 2 * step, chunk, True, False, finish)

            @pl.when(chip + step < chips)
            def _():
                pass_on(row + 2 * step, chunk, False, True, finish)

    for target in others:
        out_copy(col, target).wait_send()
        stat_copy(col, target).wait_send()
        single_copy(col, target).wait_send()
        sides_copy(col, target).wait_send()

    for step in range(1, rows):
        right_copy(row % owners, col, step).wait_send()

    @pl.when(jnp.logical_not(is_owner))
    def _():
        right_copy(row % owners, col, 0).wait_send()


def plane_kernel(
    rows,
    cols,
    model_width,
    hidden_ref,
    own_hbm,
    attn_gain_ref,
    cos_ref,
    sin_ref,
    cos_step_ref,
    sin_step_ref,
    final_gain_ref,
    w_query_hbm,
    w_key_hbm,
    w_value_hbm,
    w_out_hbm,
    w_single_hbm,
    w_second_hbm,
    w_left_ref,
    w_right_ref,
    bins_ref,
    table_ref,
    left_ref,
    right_ref,
    rel_hbm,
    w_query,
    w_key,
    w_value,
    w_out,
    w_single,
    w_second,
    own,
    piece_send,
    far,
    kv,
    query,
    totals,
    numerator,
    context,
    out_send,
    out_recv,
    stat_send,
    stat_recv,
    gain_sums,
    single_own,
    single_send,
    single_recv,
    sides,
    right_own,
    right_all,
    table,
    rel_slots,
    weight_sem,
    far_out_sem,
    far_send_sem,
    far_recv_sem,
    kv_send_sem,
    kv_recv_sem,
    out_send_sem,
    out_recv_sem,
    stat_send_sem,
    stat_recv_sem,
    single_send_sem,
    single_recv_sem,
    sides_send_sem,
    sides_recv_sem,
    right_send_sem,
    right_recv_sem,
    gain_send_sem,
    gain_recv_sem,
    rel_sem,
):
    row = lax.axis_index("row")
    col = lax.axis_index("col")
    count = hidden_ref.shape[0]
    pairs = query.shape[0]
    features = w_single.shape[0]
    piece = single_own.shape[1]
    owners = rows // cols
    chips = rows // 2
    chip = row // 2
    core = row % 2
    partner = row + 1 - 2 * core
    outer = jnp.logical_or(chip == 0, chip == chips - 1)
    farthest = (chips - 1 - chip) * 2 + core
    side = col + 1 - 2 * (col % 2)
    across = (col + 2) % cols
    corner = cols - 1 - col

    own_columns = pl.ds(pl.multiple_of(col * features, 128), features)
    loads = []
    for index, (source, target) in enumerate(
        (
            (w_key_hbm, w_key),
            (w_value_hbm, w_value),
            (w_query_hbm, w_query),
            (w_out_hbm, w_out),
            (w_single_hbm, w_single),
            (w_second_hbm, w_second),
            (own_hbm.at[:, own_columns], own),
        )
    ):
        load = pltpu.make_async_copy(source, target, weight_sem.at[index])
        load.start()
        loads.append(load)

    barrier = pltpu.get_barrier_semaphore()
    is_owner = row // owners == col

    def greet(target_row, target_col):
        pl.semaphore_signal(
            barrier, inc=1, device_id=(target_row, target_col), device_id_type=MESH
        )

    greet(partner, col)

    @pl.when(outer)
    def _():
        greet(farthest, col)

    @pl.when(chip + 1 < chips)
    def _():
        greet(row + 2, col)

    @pl.when(chip >= 1)
    def _():
        greet(row - 2, col)

    for slot in range(owners):
        for index in range(cols):

            @pl.when(jnp.logical_or(row != col * owners + slot, col != index))
            def _():
                greet(col * owners + slot, index)

    greetings = cols + rows + jnp.where(outer, 1, 0)
    greetings += jnp.where(chip + 1 < chips, 1, 0) + jnp.where(chip >= 1, 1, 0)
    greetings -= jnp.where(is_owner, 1, 0)
    for step in range(1, cols):
        pl.semaphore_signal(
            barrier, inc=1, device_id=(row, (col + step) % cols), device_id_type=MESH
        )

    def normalize(values):
        stream = values.astype(jnp.float32)
        average = jnp.sum(stream, -1, keepdims=True) / model_width
        variance = jnp.sum(stream * stream, -1, keepdims=True) / model_width - average * average
        return (
            (stream - average) * lax.rsqrt(variance + epsilon) * attn_gain_ref[...].reshape(1, -1)
        ).astype(jnp.bfloat16)

    half = piece // 2

    @pl.when(outer)
    def _():
        for part in range(2):
            first = pl.multiple_of(col * piece + part * half, half)
            piece_send[part] = normalize(hidden_ref[pl.ds(first, half)])

    lane = lax.broadcasted_iota(jnp.int32, (count, 128), 1)
    first_half = lane % HD < HD // 2
    first_head = lane < HD

    def tables(source):
        cosine = cos_ref[...]
        sine = sin_ref[...]
        cos_step = cos_step_ref[pl.ds(source, 1), :]
        sin_step = sin_step_ref[pl.ds(source, 1), :]
        turned = sine * cos_step + cosine * sin_step
        return cosine * cos_step - sine * sin_step, jnp.where(first_half, -turned, turned)

    def rope(vectors, cosine, sine):
        turned = jnp.where(
            first_half,
            pltpu.roll(vectors, 128 - HD // 2, 1),
            pltpu.roll(vectors, HD // 2, 1),
        )
        return vectors * cosine + turned * sine

    def far_copy(owner, part, way, target):
        return pltpu.make_async_remote_copy(
            src_ref=far.at[owner, part],
            dst_ref=far.at[owner, part],
            send_sem=far_send_sem.at[way, part],
            recv_sem=far_recv_sem.at[owner, part],
            device_id=(row, target),
            device_id_type=MESH,
        )

    def far_out(part):
        return pltpu.make_async_remote_copy(
            src_ref=piece_send.at[part],
            dst_ref=far.at[col, part],
            send_sem=far_out_sem.at[part],
            recv_sem=far_recv_sem.at[col, part],
            device_id=(farthest, col),
            device_id_type=MESH,
        )

    def share(part, act):
        act(far_copy(col, part, 0, side))
        act(far_copy(col, part, 1, across))

    def share_corner(part, act):
        if part == 0:
            act(far_copy(side, part, 2, across))
        else:
            act(far_copy(across, part, 2, side))

    def far_wait(owner, part):
        far_copy(owner, part, 0, side).wait_recv()

    def kv_copy(source, chunk, way, target):
        return pltpu.make_async_remote_copy(
            src_ref=kv.at[source, chunk],
            dst_ref=kv.at[source, chunk],
            send_sem=kv_send_sem.at[way, source, chunk],
            recv_sem=kv_recv_sem.at[source, chunk],
            device_id=(target, col),
            device_id_type=MESH,
        )

    def pass_on(source, chunk, right, left, act):
        if right:

            @pl.when(chip + 1 < chips)
            def _():
                act(kv_copy(source, chunk, 0, row + 2))

        if left:

            @pl.when(chip >= 1)
            def _():
                act(kv_copy(source, chunk, 1, row - 2))

        act(kv_copy(source, chunk, 2, partner))

    def start(copy):
        copy.start()

    def finish(copy):
        copy.wait_send()

    pl.semaphore_wait(barrier, greetings)

    @pl.when(outer)
    def _():
        for part in range(2):
            far_out(part).start()

    def keys_of(rows_in, source):
        cosine, sine = tables(source)
        projected = jnp.dot(rows_in, w_key[...], preferred_element_type=jnp.float32)
        for pair in range(pairs):
            kv[source, 0, pair] = rope(
                projected[:, pair * 128 : pair * 128 + 128], cosine, sine
            ).astype(jnp.bfloat16)

    def values_of(rows_in, source):
        projected = jnp.dot(rows_in, w_value[...], preferred_element_type=jnp.float32)
        for pair in range(pairs):
            kv[source, 1, pair] = projected[:, pair * 128 : pair * 128 + 128].astype(jnp.bfloat16)

    attn_in = normalize(hidden_ref[...])
    loads[0].wait()
    keys_of(attn_in, row)
    pass_on(row, 0, True, True, start)
    loads[1].wait()
    values_of(attn_in, row)
    pass_on(row, 1, True, True, start)

    @pl.when(outer)
    def _():
        for part in range(2):
            far_wait(col, part)
            share(part, start)

    def gain_copy(source, target):
        return pltpu.make_async_remote_copy(
            src_ref=gain_sums.at[source],
            dst_ref=gain_sums.at[source],
            send_sem=gain_send_sem.at[target],
            recv_sem=gain_recv_sem.at[source],
            device_id=(row, target),
            device_id_type=MESH,
        )

    others = [(col + step) % cols for step in range(1, cols)]
    loads[2].wait()
    cosine, sine = tables(row)
    projected = jnp.dot(attn_in, w_query[...], preferred_element_type=jnp.float32) * HD ** (-0.5)
    for pair in range(pairs):
        turned = rope(projected[:, pair * 128 : pair * 128 + 128], cosine, sine)
        query[pair, :count] = jnp.where(first_head, turned, 0.0).astype(jnp.bfloat16)
        query[pair, count:] = jnp.where(first_head, 0.0, turned).astype(jnp.bfloat16)
    bins = table_ref.shape[0]
    table[...] = jnp.zeros_like(table)
    table[:bins] = table_ref[...]
    slot_rows = rel_slots.shape[1]
    col_count = bins_ref.shape[1]
    slots = bins_ref.shape[0] // slot_rows

    def rel_copy(index):
        return pltpu.make_async_copy(
            rel_slots.at[index % 2],
            rel_hbm.at[pl.ds(pl.multiple_of(index * slot_rows, slot_rows), slot_rows)],
            rel_sem.at[index % 2],
        )

    def spell(begin, end):
        @pl.loop(begin, end)
        def _(index):
            @pl.when(index >= 2)
            def _():
                rel_copy(index - 2).wait()

            picked = bins_ref[pl.ds(pl.multiple_of(index * slot_rows, slot_rows), slot_rows)]
            codes = lax.broadcasted_iota(jnp.int32, (table.shape[0], col_count), 0)
            hot = jnp.concatenate(
                [
                    jnp.where(picked[i : i + 1, :] == codes, 1.0, 0.0).astype(jnp.bfloat16)
                    for i in range(slot_rows)
                ],
                1,
            )
            chosen = lax.dot_general(
                hot, table[...], (((0,), (0,)), ((), ())), preferred_element_type=jnp.float32
            )
            rel_slots[index % 2] = chosen.astype(jnp.bfloat16).reshape(rel_slots.shape[1:])
            rel_copy(index).start()

    totals[...] = jnp.zeros_like(totals)
    numerator[...] = jnp.zeros_like(numerator)

    def attend(source):
        for pair in range(pairs):
            scores = lax.dot_general(
                query[pair],
                kv[source, 0, pair],
                (((1,), (1,)), ((), ())),
                preferred_element_type=jnp.float32,
            )
            weights = jnp.exp(scores)
            totals[pair] += weights
            numerator[pair] += jnp.dot(
                weights.astype(jnp.bfloat16),
                kv[source, 1, pair],
                preferred_element_type=jnp.float32,
            )

    def arrive(source):
        for chunk in range(2):
            kv_copy(source, chunk, 2, partner).wait_recv()

    attend(row)
    loads[4].wait()
    gain = final_gain_ref[...].reshape(1, -1)
    coarse = gain.astype(jnp.bfloat16)
    fine = (gain - coarse.astype(jnp.float32)).astype(jnp.bfloat16)
    gains = jnp.concatenate([jnp.broadcast_to(part, (16, features)) for part in (coarse, fine)], 0)
    gained = jnp.dot(gains, w_single[...], preferred_element_type=jnp.float32)
    gain_sums[col] = gained[:8] + gained[16:24]
    for target in others:
        gain_copy(col, target).start()

    @pl.when(outer)
    def _():
        far_wait(side, 0)
        share_corner(0, start)
        far_wait(across, 1)
        share_corner(1, start)

    arrive(partner)
    attend(partner)
    spell(0, slots // 2)

    def near(step, onward):
        from_left = chip - step >= 0
        from_right = chip + step < chips
        for chunk in range(2):

            @pl.when(from_left)
            def _():
                source = row - 2 * step
                kv_copy(source, chunk, 2, partner).wait_recv()
                pass_on(source, chunk, onward, False, start)

            @pl.when(from_right)
            def _():
                source = row + 2 * step
                kv_copy(source, chunk, 2, partner).wait_recv()
                pass_on(source, chunk, False, onward, start)

        @pl.when(from_left)
        def _():
            attend(row - 2 * step)
            arrive(partner - 2 * step)
            attend(partner - 2 * step)

        @pl.when(from_right)
        def _():
            attend(row + 2 * step)
            arrive(partner + 2 * step)
            attend(partner + 2 * step)

    for step in range(1, chips - 1):
        near(step, step < chips - 2)
        if step == 1:
            spell(slots // 2, slots)

            @pl.when(outer)
            def _():
                far_wait(side, 1)
                far_wait(across, 0)
                for part in range(2):
                    far_wait(corner, part)
                rows_in = far[...].reshape(count, model_width)
                keys_of(rows_in, farthest)
                pass_on(farthest, 0, False, False, start)
                values_of(rows_in, farthest)
                pass_on(farthest, 1, False, False, start)
                other = farthest + partner - row
                attend(farthest)
                arrive(other)
                attend(other)

    for pair in range(pairs):
        shares = numerator[pair] / jnp.sum(totals[pair], -1, keepdims=True)
        context[:, pair * 128 : pair * 128 + 128] = jnp.where(
            first_head, shares[:count], shares[count:]
        ).astype(jnp.bfloat16)

    def out_copy(source, target):
        return pltpu.make_async_remote_copy(
            src_ref=out_send.at[target],
            dst_ref=out_recv.at[source],
            send_sem=out_send_sem.at[target],
            recv_sem=out_recv_sem.at[source],
            device_id=(row, target),
            device_id_type=MESH,
        )

    def out_part(target):
        columns = pl.ds(pl.multiple_of(target * features, 128), features)
        return jnp.dot(context[...], w_out[:, columns], preferred_element_type=jnp.float32)

    loads[3].wait()
    for target in others:
        out_send[target] = out_part(target).astype(jnp.bfloat16)
        out_copy(col, target).start()
    loads[6].wait()
    resid = own[...].astype(jnp.float32) + out_part(col)
    for source in others:
        out_copy(source, source).wait_recv()
        resid += out_recv[source].astype(jnp.float32)

    def stat_copy(source, target):
        return pltpu.make_async_remote_copy(
            src_ref=stat_send.at[target],
            dst_ref=stat_recv.at[source],
            send_sem=stat_send_sem.at[target],
            recv_sem=stat_recv_sem.at[source],
            device_id=(row, target),
            device_id_type=MESH,
        )

    middle = jnp.sum(resid, -1, keepdims=True) / features
    centred = resid - middle
    spread_sum = jnp.sum(centred * centred, -1, keepdims=True)
    stats = jnp.where(lane < 1, middle, spread_sum)
    for index in range(cols):
        stat_send[index] = stats[index * piece : (index + 1) * piece]
    for target in others:
        stat_copy(col, target).start()
    final = (centred * final_gain_ref[...].reshape(1, -1)).astype(jnp.bfloat16)

    def single_copy(source, target):
        return pltpu.make_async_remote_copy(
            src_ref=single_send.at[target],
            dst_ref=single_recv.at[source],
            send_sem=single_send_sem.at[target],
            recv_sem=single_recv_sem.at[source],
            device_id=(row, target),
            device_id_type=MESH,
        )

    part = jnp.dot(final, w_single[...], preferred_element_type=jnp.float32)
    for index in range(cols):
        block = part[index * piece : (index + 1) * piece]
        single_own[index] = block
        single_send[index] = block.astype(jnp.bfloat16)
    for target in others:
        single_copy(col, target).start()
    for source in others:
        stat_copy(source, source).wait_recv()
        gain_copy(source, source).wait_recv()
    stat_recv[col] = stat_send[col]
    middles = [stat_recv[index][:, 0:1] for index in range(cols)]
    average = sum(middles) / cols
    variance = sum(stat_recv[index][:, 1:2] for index in range(cols)) / model_width
    variance += sum((middles[index] - average) * (middles[index] - average) for index in range(cols)) / cols
    scale = lax.rsqrt(variance + epsilon)
    summed = single_own[col]
    for index in range(cols):
        summed += (middles[index] - average) * gain_sums[index][0:1]
    for source in others:
        single_copy(source, source).wait_recv()
        summed += single_recv[source].astype(jnp.float32)
    lifted = jnp.maximum(summed * scale, 0.0).astype(jnp.bfloat16)
    loads[5].wait()
    single = jnp.dot(lifted, w_second[...], preferred_element_type=jnp.float32)
    single = single.astype(jnp.bfloat16)

    def sides_copy(source, target):
        return pltpu.make_async_remote_copy(
            src_ref=sides.at[source],
            dst_ref=sides.at[source],
            send_sem=sides_send_sem.at[target],
            recv_sem=sides_recv_sem.at[source],
            device_id=(row, target),
            device_id_type=MESH,
        )

    def right_copy(slot, index, step):
        return pltpu.make_async_remote_copy(
            src_ref=right_own,
            dst_ref=right_all.at[slot, index],
            send_sem=right_send_sem.at[step],
            recv_sem=right_recv_sem.at[slot, index],
            device_id=((row + step) % rows, row // owners),
            device_id_type=MESH,
        )

    right_own[...] = jnp.dot(
        single, w_right_ref[...], preferred_element_type=jnp.float32
    ).astype(jnp.bfloat16)
    for step in range(1, rows):
        right_copy(row % owners, col, step).start()

    @pl.when(jnp.logical_not(is_owner))
    def _():
        right_copy(row % owners, col, 0).start()

    sides[col] = jnp.dot(single, w_left_ref[...], preferred_element_type=jnp.float32).astype(
        jnp.bfloat16
    )
    for target in others:
        sides_copy(col, target).start()

    @pl.when(is_owner)
    def _():
        right_all[row % owners, col] = right_own[...]

    for source in others:
        sides_copy(source, source).wait_recv()
    for index in range(cols):
        left_ref[index * piece : (index + 1) * piece] = sides[index]
    for slot in range(owners):
        for index in range(cols):

            @pl.when(jnp.logical_or(row != col * owners + slot, col != index))
            def _():
                right_copy(slot, index, 1).wait_recv()

            start_row = slot * count + index * piece
            right_ref[start_row : start_row + piece] = right_all[slot, index]

    for chunk in range(2):
        pass_on(row, chunk, True, True, finish)
        for step in range(1, chips - 1):

            @pl.when(chip - step >= 0)
            def _():
                pass_on(row - 2 * step, chunk, step < chips - 2, False, finish)

            @pl.when(chip + step < chips)
            def _():
                pass_on(row + 2 * step, chunk, False, step < chips - 2, finish)

    @pl.when(outer)
    def _():
        for part in range(2):
            pass_on(farthest, part, False, False, finish)
            far_out(part).wait_send()
            share(part, finish)
            share_corner(part, finish)

    rel_copy(slots - 2).wait()
    rel_copy(slots - 1).wait()
    for target in others:
        out_copy(col, target).wait_send()
        stat_copy(col, target).wait_send()
        single_copy(col, target).wait_send()
        sides_copy(col, target).wait_send()
        gain_copy(col, target).wait_send()

    for step in range(1, rows):
        right_copy(row % owners, col, step).wait_send()

    @pl.when(jnp.logical_not(is_owner))
    def _():
        right_copy(row % owners, col, 0).wait_send()


def padded(array, axis, size, groups=1):
    width = array.shape[axis] // groups
    if width == size:
        return array
    shape = array.shape
    array = array.reshape(shape[:axis] + (groups, width) + shape[axis + 1 :])
    pads = [(0, 0)] * array.ndim
    pads[axis + 1] = (0, size - width)
    array = jnp.pad(array, pads)
    return array.reshape(shape[:axis] + (groups * size,) + shape[axis + 1 :])


def front_general(
    hidden,
    attn_gain,
    w_query,
    w_key,
    w_value,
    w_out,
    final_gain,
    w_single,
    w_second,
    w_left,
    w_right,
):
    rows = lax.axis_size("row")
    cols = lax.axis_size("col")
    count, model_width = hidden.shape
    width = -(-w_query.shape[1] // 128) * 128
    features = -(-w_single.shape[0] // 128) * 128
    pairs = width // 128
    piece = count // cols
    owners = rows // cols
    single_width = w_second.shape[0]
    channels = w_left.shape[1]
    positions = lax.axis_index("row") * count + jnp.arange(count, dtype=jnp.int32)
    frequency = jnp.exp(
        jnp.arange(HD // 2, dtype=jnp.float32) * (-2.0 * math.log(10000.0) / HD)
    )
    angles = positions.astype(jnp.float32)[:, None] * frequency[None, :]
    cosine = jnp.cos(angles)
    sine = jnp.sin(angles)
    cosine = jnp.concatenate([cosine] * 4, -1)
    sine = jnp.concatenate([-sine, sine, -sine, sine], -1)
    weights = (
        padded(w_query, 1, width),
        padded(w_key, 1, width),
        padded(w_value, 1, width),
        padded(padded(w_out, 0, width), 1, features, cols),
        padded(w_single, 0, features),
        w_second,
    )
    vmem = pl.BlockSpec(memory_space=pltpu.VMEM)
    anywhere = pl.BlockSpec(memory_space=pl.ANY)
    bf16 = jnp.bfloat16
    f32 = jnp.float32
    dma = pltpu.SemaphoreType.DMA
    return pl.pallas_call(
        functools.partial(front_kernel, rows, cols, model_width),
        out_shape=(
            jax.ShapeDtypeStruct((count, channels), bf16),
            jax.ShapeDtypeStruct((owners * count, channels), bf16),
        ),
        in_specs=[vmem, anywhere] + [vmem] * 4 + [anywhere] * 6 + [vmem] * 2,
        out_specs=(vmem, vmem),
        scratch_shapes=[pltpu.VMEM(weight.shape, bf16) for weight in weights]
        + [
            pltpu.VMEM((count, features), bf16),
            pltpu.VMEM((rows, 2, pairs, count, 128), bf16),
            pltpu.VMEM((pairs, 2 * count, 128), bf16),
            pltpu.VMEM((pairs, 2 * count, count), f32),
            pltpu.VMEM((pairs, 2 * count, 128), f32),
            pltpu.VMEM((count, width), bf16),
            pltpu.VMEM((cols, count, features), bf16),
            pltpu.VMEM((cols, count, features), bf16),
            pltpu.VMEM((8, count), f32),
            pltpu.VMEM((cols, 8, count), f32),
            pltpu.VMEM((cols, piece, single_width), f32),
            pltpu.VMEM((cols, piece, single_width), bf16),
            pltpu.VMEM((cols, piece, single_width), bf16),
            pltpu.VMEM((cols, piece, channels), bf16),
            pltpu.VMEM((piece, channels), bf16),
            pltpu.VMEM((owners, cols, piece, channels), bf16),
            dma((7,)),
            dma((3, rows, 2)),
            dma((rows, 2)),
            dma((cols,)),
            dma((cols,)),
            dma((cols,)),
            dma((cols,)),
            dma((cols,)),
            dma((cols,)),
            dma((cols,)),
            dma((cols,)),
            dma((rows,)),
            dma((owners, cols)),
        ],
        compiler_params=pltpu.CompilerParams(
            collective_id=0, has_side_effects=True, vmem_limit_bytes=56 << 20
        ),
    )(
        hidden,
        padded(hidden, 1, features, cols),
        attn_gain,
        cosine,
        sine,
        padded(final_gain, 0, features),
        *weights,
        w_left,
        w_right,
    )


def spelled_kernel(rel_ref, left_ref, right_ref, gain_ref, expand_ref, contract_ref, out_ref):
    block_rows, col_count, channels = rel_ref.shape
    right = right_ref[...].astype(jnp.float32)
    pair_in = jnp.concatenate(
        [
            rel_ref[i].astype(jnp.float32) + (right + left_ref[i : i + 1, :].astype(jnp.float32))
            for i in range(block_rows)
        ],
        0,
    )
    average = jnp.sum(pair_in, -1, keepdims=True) / channels
    variance = jnp.sum(pair_in * pair_in, -1, keepdims=True) / channels - average * average
    normed = ((pair_in - average) * lax.rsqrt(variance + epsilon) * gain_ref[...]).astype(
        jnp.bfloat16
    )
    expanded = jnp.dot(normed, expand_ref[...], preferred_element_type=jnp.float32)
    expanded = jnp.maximum(expanded.astype(jnp.bfloat16), 0)
    update = jnp.dot(expanded, contract_ref[...], preferred_element_type=jnp.float32)
    out_ref[...] = (pair_in + update).astype(out_ref.dtype).reshape(out_ref.shape)


def spelled_stage(rel, left, right, pair_gain, w_expand, w_contract):
    row_count, col_count, channels = rel.shape
    block_rows = math.gcd(row_count, 32)
    whole = lambda array: pl.BlockSpec(array.shape, lambda i: (0, 0))
    gain = pair_gain.reshape(1, channels)
    tile = pl.BlockSpec((block_rows, col_count, channels), lambda i: (i, 0, 0))
    return pl.pallas_call(
        spelled_kernel,
        grid=(row_count // block_rows,),
        in_specs=[
            tile,
            pl.BlockSpec((block_rows, channels), lambda i: (i, 0)),
            whole(right),
            whole(gain),
            whole(w_expand),
            whole(w_contract),
        ],
        out_specs=tile,
        out_shape=jax.ShapeDtypeStruct(rel.shape, jnp.bfloat16),
        compiler_params=pltpu.CompilerParams(
            dimension_semantics=("arbitrary",), vmem_limit_bytes=56 << 20
        ),
    )(rel, left, right, gain, w_expand, w_contract)


def front_plane(
    hidden,
    attn_gain,
    w_query,
    w_key,
    w_value,
    w_out,
    final_gain,
    w_single,
    w_second,
    w_left,
    w_right,
    rel_bins,
    rel_table,
):
    rows = lax.axis_size("row")
    cols = lax.axis_size("col")
    count, model_width = hidden.shape
    width = -(-w_query.shape[1] // 128) * 128
    features = -(-w_single.shape[0] // 128) * 128
    pairs = width // 128
    piece = count // cols
    owners = rows // cols
    single_width = w_second.shape[0]
    channels = w_left.shape[1]
    frequency = np.exp(np.arange(HD // 2) * (-2.0 * math.log(10000.0) / HD))
    frequency = np.concatenate([frequency] * 4)[None, :]
    offsets = np.arange(count)[:, None] * frequency
    steps = (np.arange(rows) * count)[:, None] * frequency
    angles = [
        jnp.asarray(turn(angle), jnp.float32)
        for angle in (offsets, steps)
        for turn in (np.cos, np.sin)
    ]
    weights = (w_query, w_key, w_value, w_out, w_single, w_second)
    vmem = pl.BlockSpec(memory_space=pltpu.VMEM)
    anywhere = pl.BlockSpec(memory_space=pl.ANY)
    bf16 = jnp.bfloat16
    f32 = jnp.float32
    dma = pltpu.SemaphoreType.DMA
    return pl.pallas_call(
        functools.partial(plane_kernel, rows, cols, model_width),
        out_shape=(
            jax.ShapeDtypeStruct((count, channels), bf16),
            jax.ShapeDtypeStruct((owners * count, channels), bf16),
            jax.ShapeDtypeStruct(rel_bins.shape + (channels,), bf16),
        ),
        in_specs=[vmem, anywhere] + [vmem] * 6 + [anywhere] * 6 + [vmem] * 4,
        out_specs=(vmem, vmem, anywhere),
        scratch_shapes=[pltpu.VMEM(weight.shape, bf16) for weight in weights]
        + [
            pltpu.VMEM((count, features), bf16),
            pltpu.VMEM((2, piece // 2, model_width), bf16),
            pltpu.VMEM((cols, 2, piece // 2, model_width), bf16),
            pltpu.VMEM((rows, 2, pairs, count, 128), bf16),
            pltpu.VMEM((pairs, 2 * count, 128), bf16),
            pltpu.VMEM((pairs, 2 * count, count), f32),
            pltpu.VMEM((pairs, 2 * count, 128), f32),
            pltpu.VMEM((count, width), bf16),
            pltpu.VMEM((cols, count, features), bf16),
            pltpu.VMEM((cols, count, features), bf16),
            pltpu.VMEM((cols, piece, 128), f32),
            pltpu.VMEM((cols, piece, 128), f32),
            pltpu.VMEM((cols, 8, single_width), f32),
            pltpu.VMEM((cols, piece, single_width), f32),
            pltpu.VMEM((cols, piece, single_width), bf16),
            pltpu.VMEM((cols, piece, single_width), bf16),
            pltpu.VMEM((cols, piece, channels), bf16),
            pltpu.VMEM((piece, channels), bf16),
            pltpu.VMEM((owners, cols, piece, channels), bf16),
            pltpu.VMEM((-(-rel_table.shape[0] // 128) * 128, channels), bf16),
            pltpu.VMEM((2, rel_bins.shape[0] // 8, rel_bins.shape[1], channels), bf16),
            dma((7,)),
            dma((2,)),
            dma((3, 2)),
            dma((cols, 2)),
            dma((3, rows, 2)),
            dma((rows, 2)),
            dma((cols,)),
            dma((cols,)),
            dma((cols,)),
            dma((cols,)),
            dma((cols,)),
            dma((cols,)),
            dma((cols,)),
            dma((cols,)),
            dma((rows,)),
            dma((owners, cols)),
            dma((cols,)),
            dma((cols,)),
            dma((2,)),
        ],
        compiler_params=pltpu.CompilerParams(
            collective_id=0, has_side_effects=True, vmem_limit_bytes=56 << 20
        ),
    )(
        hidden,
        hidden,
        attn_gain,
        *angles,
        final_gain,
        *weights,
        w_left,
        w_right,
        rel_bins,
        rel_table,
    )


def local(
    hidden,
    rel_bins,
    attn_gain,
    w_query,
    w_key,
    w_value,
    w_out,
    final_gain,
    w_single,
    w_second,
    w_left,
    w_right,
    rel_table,
    pair_gain,
    w_expand,
    w_contract,
):
    rows = lax.axis_size("row")
    cols = lax.axis_size("col")
    aligned = w_query.shape[1] % 128 == 0 and hidden.shape[0] % (32 * cols) == 0
    operands = (
        hidden,
        attn_gain,
        w_query,
        w_key,
        w_value,
        w_out,
        final_gain,
        w_single,
        w_second,
        w_left,
        w_right,
    )
    if rows == 2 * cols and cols == 4 and aligned:
        left, right, rel = front_plane(*operands, rel_bins, rel_table)
        return spelled_stage(rel, left, right, pair_gain, w_expand, w_contract)
    left, right = front_general(*operands)
    return pair_stage(rel_bins, left, right, rel_table, pair_gain, w_expand, w_contract)


def solution(mesh):
    in_specs = (
        P("row", None),
        P("row", "col"),
        P(),
        P(None, "col"),
        P(None, "col"),
        P(None, "col"),
        P("col", None),
        P("col"),
        P("col", None),
        P(),
        P(),
        P(),
        P(),
        P(),
        P(),
        P(),
    )
    out_specs = P("row", "col", None)
    return jax.shard_map(local, mesh=mesh, in_specs=in_specs, out_specs=out_specs, check_vma=False)
```

```python
import functools
import math

import jax
import jax.numpy as jnp
import numpy as np
from jax import lax
from jax.experimental import pallas as pl
from jax.experimental.pallas import tpu as pltpu
from jax.sharding import PartitionSpec as P

HD = 64
MESH = pl.DeviceIdType.MESH


epsilon = 1e-05


def pair_kernel(bins_ref, left_ref, right_ref, table_ref, gain_ref, expand_ref, contract_ref, out_ref, table):
    block_rows, col_count = bins_ref.shape
    channels = right_ref.shape[1]
    right = right_ref[...].astype(jnp.float32)
    bins = table_ref.shape[0]

    @pl.when(pl.program_id(0) == 0)
    def _():
        table[...] = jnp.zeros_like(table)
        table[:bins] = table_ref[...]

    codes = lax.broadcasted_iota(jnp.int32, (table.shape[0], col_count), 0)
    hot = jnp.concatenate(
        [
            jnp.where(bins_ref[i : i + 1, :] == codes, 1.0, 0.0).astype(jnp.bfloat16)
            for i in range(block_rows)
        ],
        1,
    )
    part = lax.dot_general(
        hot, table[...], (((0,), (0,)), ((), ())), preferred_element_type=jnp.float32
    )
    pair_in = jnp.concatenate(
        [
            part[i * col_count : (i + 1) * col_count]
            + (right + left_ref[i : i + 1, :].astype(jnp.float32))
            for i in range(block_rows)
        ],
        0,
    )
    average = jnp.sum(pair_in, -1, keepdims=True) / channels
    variance = jnp.sum(pair_in * pair_in, -1, keepdims=True) / channels - average * average
    normed = ((pair_in - average) * lax.rsqrt(variance + epsilon) * gain_ref[...]).astype(
        jnp.bfloat16
    )
    expanded = jnp.dot(normed, expand_ref[...], preferred_element_type=jnp.float32)
    expanded = jnp.maximum(expanded.astype(jnp.bfloat16), 0)
    update = jnp.dot(expanded, contract_ref[...], preferred_element_type=jnp.float32)
    out_ref[...] = (pair_in + update).astype(out_ref.dtype).reshape(out_ref.shape)


def pair_stage(rel_bins, left, right, rel_table, pair_gain, w_expand, w_contract):
    row_count, col_count = rel_bins.shape
    channels = right.shape[1]
    block_rows = math.gcd(row_count, 32)
    bins_padded = -(-rel_table.shape[0] // 128) * 128
    whole = lambda array: pl.BlockSpec(array.shape, lambda i: (0, 0))
    gain = pair_gain.reshape(1, channels)
    return pl.pallas_call(
        pair_kernel,
        grid=(row_count // block_rows,),
        in_specs=[
            pl.BlockSpec((block_rows, col_count), lambda i: (i, 0)),
            pl.BlockSpec((block_rows, channels), lambda i: (i, 0)),
            whole(right),
            whole(rel_table),
            whole(gain),
            whole(w_expand),
            whole(w_contract),
        ],
        out_specs=pl.BlockSpec((block_rows, col_count, channels), lambda i: (i, 0, 0)),
        out_shape=jax.ShapeDtypeStruct((row_count, col_count, channels), jnp.bfloat16),
        scratch_shapes=[pltpu.VMEM((bins_padded, channels), jnp.bfloat16)],
        compiler_params=pltpu.CompilerParams(
            dimension_semantics=("arbitrary",), vmem_limit_bytes=56 << 20
        ),
    )(rel_bins, left, right, rel_table, gain, w_expand, w_contract)


def front_kernel(
    rows,
    cols,
    model_width,
    hidden_ref,
    own_hbm,
    attn_gain_ref,
    cos_ref,
    sin_ref,
    final_gain_ref,
    w_query_hbm,
    w_key_hbm,
    w_value_hbm,
    w_out_hbm,
    w_single_hbm,
    w_second_hbm,
    w_left_ref,
    w_right_ref,
    left_ref,
    right_ref,
    w_query,
    w_key,
    w_value,
    w_out,
    w_single,
    w_second,
    own,
    kv,
    query,
    totals,
    numerator,
    context,
    out_send,
    out_recv,
    stat_send,
    stat_recv,
    single_own,
    single_send,
    single_recv,
    sides,
    right_own,
    right_all,
    weight_sem,
    kv_send_sem,
    kv_recv_sem,
    out_send_sem,
    out_recv_sem,
    stat_send_sem,
    stat_recv_sem,
    single_send_sem,
    single_recv_sem,
    sides_send_sem,
    sides_recv_sem,
    right_send_sem,
    right_recv_sem,
):
    row = lax.axis_index("row")
    col = lax.axis_index("col")
    count = hidden_ref.shape[0]
    pairs = query.shape[0]
    features = w_single.shape[0]
    piece = single_own.shape[1]
    owners = rows // cols
    chips = rows // 2
    chip = row // 2
    core = row % 2
    partner = row + 1 - 2 * core

    own_columns = pl.ds(pl.multiple_of(col * features, 128), features)
    loads = []
    for index, (source, target) in enumerate(
        (
            (w_key_hbm, w_key),
            (w_value_hbm, w_value),
            (w_query_hbm, w_query),
            (w_out_hbm, w_out),
            (w_single_hbm, w_single),
            (w_second_hbm, w_second),
            (own_hbm.at[:, own_columns], own),
        )
    ):
        load = pltpu.make_async_copy(source, target, weight_sem.at[index])
        load.start()
        loads.append(load)

    barrier = pltpu.get_barrier_semaphore()
    is_owner = row // owners == col

    def greet(target_row, target_col):
        pl.semaphore_signal(
            barrier, inc=1, device_id=(target_row, target_col), device_id_type=MESH
        )

    greet(partner, col)

    @pl.when(chip + 1 < chips)
    def _():
        greet(row + 2, col)

    @pl.when(chip >= 1)
    def _():
        greet(row - 2, col)

    for slot in range(owners):
        for index in range(cols):

            @pl.when(jnp.logical_or(row != col * owners + slot, col != index))
            def _():
                greet(col * owners + slot, index)

    greetings = cols + rows
    greetings += jnp.where(chip + 1 < chips, 1, 0) + jnp.where(chip >= 1, 1, 0)
    greetings -= jnp.where(is_owner, 1, 0)
    for step in range(1, cols):
        pl.semaphore_signal(
            barrier, inc=1, device_id=(row, (col + step) % cols), device_id_type=MESH
        )

    stream = hidden_ref[...].astype(jnp.float32)
    average = jnp.sum(stream, -1, keepdims=True) / model_width
    variance = jnp.sum(stream * stream, -1, keepdims=True) / model_width - average * average
    attn_in = (
        (stream - average) * lax.rsqrt(variance + epsilon) * attn_gain_ref[...].reshape(1, -1)
    ).astype(jnp.bfloat16)
    cosine = cos_ref[...]
    sine = sin_ref[...]
    lane = lax.broadcasted_iota(jnp.int32, (count, 128), 1)
    first_half = lane % HD < HD // 2
    first_head = lane < HD

    def rope(vectors):
        turned = jnp.where(
            first_half,
            pltpu.roll(vectors, 128 - HD // 2, 1),
            pltpu.roll(vectors, HD // 2, 1),
        )
        return vectors * cosine + turned * sine

    def kv_copy(source, chunk, way, target):
        return pltpu.make_async_remote_copy(
            src_ref=kv.at[source, chunk],
            dst_ref=kv.at[source, chunk],
            send_sem=kv_send_sem.at[way, source, chunk],
            recv_sem=kv_recv_sem.at[source, chunk],
            device_id=(target, col),
            device_id_type=MESH,
        )

    def pass_on(source, chunk, right, left, act):
        if right:

            @pl.when(chip + 1 < chips)
            def _():
                act(kv_copy(source, chunk, 0, row + 2))

        if left:

            @pl.when(chip >= 1)
            def _():
                act(kv_copy(source, chunk, 1, row - 2))

        act(kv_copy(source, chunk, 2, partner))

    def start(copy):
        copy.start()

    def finish(copy):
        copy.wait_send()

    loads[0].wait()
    projected = jnp.dot(attn_in, w_key[...], preferred_element_type=jnp.float32)
    for pair in range(pairs):
        kv[row, 0, pair] = rope(projected[:, pair * 128 : pair * 128 + 128]).astype(jnp.bfloat16)
    pl.semaphore_wait(barrier, greetings)
    pass_on(row, 0, True, True, start)
    loads[1].wait()
    projected = jnp.dot(attn_in, w_value[...], preferred_element_type=jnp.float32)
    for pair in range(pairs):
        kv[row, 1, pair] = projected[:, pair * 128 : pair * 128 + 128].astype(jnp.bfloat16)
    pass_on(row, 1, True, True, start)
    loads[2].wait()
    projected = jnp.dot(attn_in, w_query[...], preferred_element_type=jnp.float32) * HD ** (-0.5)
    for pair in range(pairs):
        turned = rope(projected[:, pair * 128 : pair * 128 + 128])
        query[pair, :count] = jnp.where(first_head, turned, 0.0).astype(jnp.bfloat16)
        query[pair, count:] = jnp.where(first_head, 0.0, turned).astype(jnp.bfloat16)
    totals[...] = jnp.zeros_like(totals)
    numerator[...] = jnp.zeros_like(numerator)

    def attend(source):
        for pair in range(pairs):
            scores = lax.dot_general(
                query[pair],
                kv[source, 0, pair],
                (((1,), (1,)), ((), ())),
                preferred_element_type=jnp.float32,
            )
            weights = jnp.exp(scores)
            totals[pair] += weights
            numerator[pair] += jnp.dot(
                weights.astype(jnp.bfloat16),
                kv[source, 1, pair],
                preferred_element_type=jnp.float32,
            )

    def arrive(source):
        for chunk in range(2):
            kv_copy(source, chunk, 2, partner).wait_recv()

    attend(row)
    arrive(partner)
    attend(partner)

    @pl.loop(1, chips)
    def _(step):
        from_left = chip - step >= 0
        from_right = chip + step < chips
        for chunk in range(2):

            @pl.when(from_left)
            def _():
                source = row - 2 * step
                kv_copy(source, chunk, 2, partner).wait_recv()
                pass_on(source, chunk, True, False, start)

            @pl.when(from_right)
            def _():
                source = row + 2 * step
                kv_copy(source, chunk, 2, partner).wait_recv()
                pass_on(source, chunk, False, True, start)

        @pl.when(from_left)
        def _():
            attend(row - 2 * step)
            arrive(partner - 2 * step)
            attend(partner - 2 * step)

        @pl.when(from_right)
        def _():
            attend(row + 2 * step)
            arrive(partner + 2 * step)
            attend(partner + 2 * step)

    for pair in range(pairs):
        shares = numerator[pair] / jnp.sum(totals[pair], -1, keepdims=True)
        context[:, pair * 128 : pair * 128 + 128] = jnp.where(
            first_head, shares[:count], shares[count:]
        ).astype(jnp.bfloat16)

    def out_copy(source, target):
        return pltpu.make_async_remote_copy(
            src_ref=out_send.at[target],
            dst_ref=out_recv.at[source],
            send_sem=out_send_sem.at[target],
            recv_sem=out_recv_sem.at[source],
            device_id=(row, target),
            device_id_type=MESH,
        )

    def out_part(target):
        columns = pl.ds(pl.multiple_of(target * features, 128), features)
        return jnp.dot(context[...], w_out[:, columns], preferred_element_type=jnp.float32)

    others = [(col + step) % cols for step in range(1, cols)]
    loads[3].wait()
    for target in others:
        out_send[target] = out_part(target).astype(jnp.bfloat16)
        out_copy(col, target).start()
    loads[6].wait()
    resid = own[...].astype(jnp.float32) + out_part(col)
    for source in others:
        out_copy(source, source).wait_recv()
        resid += out_recv[source].astype(jnp.float32)

    def stat_copy(source, target):
        return pltpu.make_async_remote_copy(
            src_ref=stat_send,
            dst_ref=stat_recv.at[source],
            send_sem=stat_send_sem.at[target],
            recv_sem=stat_recv_sem.at[source],
            device_id=(row, target),
            device_id_type=MESH,
        )

    sum_first = jnp.sum(resid, -1, keepdims=True)
    sum_second = jnp.sum(resid * resid, -1, keepdims=True)
    sums = jnp.transpose(jnp.where(lane < 4, sum_first, sum_second))[:8]
    stat_send[...] = sums
    for target in others:
        stat_copy(col, target).start()
    for source in others:
        stat_copy(source, source).wait_recv()
        sums += stat_recv[source]
    sums = jnp.transpose(jnp.concatenate([sums] * 16, 0))
    average = sums[:, 0:1] / model_width
    variance = sums[:, 4:5] / model_width - average * average
    final = (
        (resid - average) * lax.rsqrt(variance + epsilon) * final_gain_ref[...].reshape(1, -1)
    ).astype(jnp.bfloat16)

    def single_copy(source, target):
        return pltpu.make_async_remote_copy(
            src_ref=single_send.at[target],
            dst_ref=single_recv.at[source],
            send_sem=single_send_sem.at[target],
            recv_sem=single_recv_sem.at[source],
            device_id=(row, target),
            device_id_type=MESH,
        )

    loads[4].wait()
    part = jnp.dot(final, w_single[...], preferred_element_type=jnp.float32)
    for index in range(cols):
        block = part[index * piece : (index + 1) * piece]
        single_own[index] = block
        single_send[index] = block.astype(jnp.bfloat16)
    for target in others:
        single_copy(col, target).start()
    summed = single_own[col]
    for source in others:
        single_copy(source, source).wait_recv()
        summed += single_recv[source].astype(jnp.float32)
    lifted = jnp.maximum(summed, 0.0).astype(jnp.bfloat16)
    loads[5].wait()
    single = jnp.dot(lifted, w_second[...], preferred_element_type=jnp.float32)
    single = single.astype(jnp.bfloat16)

    def sides_copy(source, target):
        return pltpu.make_async_remote_copy(
            src_ref=sides.at[source],
            dst_ref=sides.at[source],
            send_sem=sides_send_sem.at[target],
            recv_sem=sides_recv_sem.at[source],
            device_id=(row, target),
            device_id_type=MESH,
        )

    def right_copy(slot, index, step):
        return pltpu.make_async_remote_copy(
            src_ref=right_own,
            dst_ref=right_all.at[slot, index],
            send_sem=right_send_sem.at[step],
            recv_sem=right_recv_sem.at[slot, index],
            device_id=((row + step) % rows, row // owners),
            device_id_type=MESH,
        )

    right_own[...] = jnp.dot(
        single, w_right_ref[...], preferred_element_type=jnp.float32
    ).astype(jnp.bfloat16)
    for step in range(1, rows):
        right_copy(row % owners, col, step).start()

    @pl.when(jnp.logical_not(is_owner))
    def _():
        right_copy(row % owners, col, 0).start()

    sides[col] = jnp.dot(single, w_left_ref[...], preferred_element_type=jnp.float32).astype(
        jnp.bfloat16
    )
    for target in others:
        sides_copy(col, target).start()

    @pl.when(is_owner)
    def _():
        right_all[row % owners, col] = right_own[...]

    for source in others:
        sides_copy(source, source).wait_recv()
    for index in range(cols):
        left_ref[index * piece : (index + 1) * piece] = sides[index]
    for slot in range(owners):
        for index in range(cols):

            @pl.when(jnp.logical_or(row != col * owners + slot, col != index))
            def _():
                right_copy(slot, index, 1).wait_recv()

            start_row = slot * count + index * piece
            right_ref[start_row : start_row + piece] = right_all[slot, index]

    for chunk in range(2):
        pass_on(row, chunk, True, True, finish)

    @pl.loop(1, chips)
    def _(step):
        for chunk in range(2):

            @pl.when(chip - step >= 0)
            def _():
                pass_on(row - 2 * step, chunk, True, False, finish)

            @pl.when(chip + step < chips)
            def _():
                pass_on(row + 2 * step, chunk, False, True, finish)

    for target in others:
        out_copy(col, target).wait_send()
        stat_copy(col, target).wait_send()
        single_copy(col, target).wait_send()
        sides_copy(col, target).wait_send()

    for step in range(1, rows):
        right_copy(row % owners, col, step).wait_send()

    @pl.when(jnp.logical_not(is_owner))
    def _():
        right_copy(row % owners, col, 0).wait_send()


def plane_kernel(
    rows,
    cols,
    model_width,
    hidden_ref,
    own_hbm,
    attn_gain_ref,
    cos_ref,
    sin_ref,
    cos_step_ref,
    sin_step_ref,
    final_gain_ref,
    w_query_hbm,
    w_key_hbm,
    w_value_hbm,
    w_out_hbm,
    w_single_hbm,
    w_second_hbm,
    w_left_ref,
    w_right_ref,
    bins_ref,
    table_ref,
    left_ref,
    right_ref,
    rel_hbm,
    w_query,
    w_key,
    w_value,
    w_out,
    w_single,
    w_second,
    own,
    piece_send,
    far,
    kv,
    query,
    totals,
    shares,
    numerator,
    w_sides,
    context,
    out_send,
    out_recv,
    stat_send,
    stat_recv,
    gain_sums,
    single_own,
    single_send,
    single_recv,
    sides,
    right_own,
    right_all,
    table,
    rel_slots,
    weight_sem,
    far_out_sem,
    far_send_sem,
    far_recv_sem,
    kv_send_sem,
    kv_recv_sem,
    out_send_sem,
    out_recv_sem,
    stat_send_sem,
    stat_recv_sem,
    single_send_sem,
    single_recv_sem,
    sides_send_sem,
    sides_recv_sem,
    right_send_sem,
    right_recv_sem,
    gain_send_sem,
    gain_recv_sem,
    rel_sem,
):
    row = lax.axis_index("row")
    col = lax.axis_index("col")
    count = hidden_ref.shape[0]
    pairs = query.shape[0]
    features = w_single.shape[0]
    piece = single_own.shape[1]
    owners = rows // cols
    chips = rows // 2
    chip = row // 2
    core = row % 2
    partner = row + 1 - 2 * core
    outer = jnp.logical_or(chip == 0, chip == chips - 1)
    farthest = (chips - 1 - chip) * 2 + core
    side = col + 1 - 2 * (col % 2)
    across = (col + 2) % cols
    corner = cols - 1 - col

    own_columns = pl.ds(pl.multiple_of(col * features, 128), features)
    loads = []
    for index, (source, target) in enumerate(
        (
            (w_key_hbm, w_key),
            (w_value_hbm, w_value),
            (w_query_hbm, w_query),
            (w_out_hbm, w_out),
            (w_single_hbm, w_single),
            (w_second_hbm, w_second),
            (own_hbm.at[:, own_columns], own),
        )
    ):
        load = pltpu.make_async_copy(source, target, weight_sem.at[index])
        load.start()
        loads.append(load)

    barrier = pltpu.get_barrier_semaphore()
    is_owner = row // owners == col

    def greet(target_row, target_col):
        pl.semaphore_signal(
            barrier, inc=1, device_id=(target_row, target_col), device_id_type=MESH
        )

    greet(partner, col)

    @pl.when(outer)
    def _():
        greet(farthest, col)

    @pl.when(chip + 1 < chips)
    def _():
        greet(row + 2, col)

    @pl.when(chip >= 1)
    def _():
        greet(row - 2, col)

    for slot in range(owners):
        for index in range(cols):

            @pl.when(jnp.logical_or(row != col * owners + slot, col != index))
            def _():
                greet(col * owners + slot, index)

    greetings = cols + rows + jnp.where(outer, 1, 0)
    greetings += jnp.where(chip + 1 < chips, 1, 0) + jnp.where(chip >= 1, 1, 0)
    greetings -= jnp.where(is_owner, 1, 0)
    for step in range(1, cols):
        pl.semaphore_signal(
            barrier, inc=1, device_id=(row, (col + step) % cols), device_id_type=MESH
        )

    def normalize(values):
        stream = values.astype(jnp.float32)
        average = jnp.sum(stream, -1, keepdims=True) / model_width
        variance = jnp.sum(stream * stream, -1, keepdims=True) / model_width - average * average
        return (
            (stream - average) * lax.rsqrt(variance + epsilon) * attn_gain_ref[...].reshape(1, -1)
        ).astype(jnp.bfloat16)

    half = piece // 2

    @pl.when(outer)
    def _():
        for part in range(2):
            first = pl.multiple_of(col * piece + part * half, half)
            piece_send[part] = normalize(hidden_ref[pl.ds(first, half)])

    lane = lax.broadcasted_iota(jnp.int32, (count, 128), 1)
    first_half = lane % HD < HD // 2
    first_head = lane < HD

    def tables(source):
        cosine = cos_ref[...]
        sine = sin_ref[...]
        cos_step = cos_step_ref[pl.ds(source, 1), :]
        sin_step = sin_step_ref[pl.ds(source, 1), :]
        turned = sine * cos_step + cosine * sin_step
        return cosine * cos_step - sine * sin_step, jnp.where(first_half, -turned, turned)

    def rope(vectors, cosine, sine):
        turned = jnp.where(
            first_half,
            pltpu.roll(vectors, 128 - HD // 2, 1),
            pltpu.roll(vectors, HD // 2, 1),
        )
        return vectors * cosine + turned * sine

    def far_copy(owner, part, way, target):
        return pltpu.make_async_remote_copy(
            src_ref=far.at[owner, part],
            dst_ref=far.at[owner, part],
            send_sem=far_send_sem.at[way, part],
            recv_sem=far_recv_sem.at[owner, part],
            device_id=(row, target),
            device_id_type=MESH,
        )

    def far_out(part):
        return pltpu.make_async_remote_copy(
            src_ref=piece_send.at[part],
            dst_ref=far.at[col, part],
            send_sem=far_out_sem.at[part],
            recv_sem=far_recv_sem.at[col, part],
            device_id=(farthest, col),
            device_id_type=MESH,
        )

    def share(part, act):
        act(far_copy(col, part, 0, side))
        act(far_copy(col, part, 1, across))

    def share_corner(part, act):
        if part == 0:
            act(far_copy(side, part, 2, across))
        else:
            act(far_copy(across, part, 2, side))

    def far_wait(owner, part):
        far_copy(owner, part, 0, side).wait_recv()

    def kv_copy(source, chunk, way, target):
        return pltpu.make_async_remote_copy(
            src_ref=kv.at[source, chunk],
            dst_ref=kv.at[source, chunk],
            send_sem=kv_send_sem.at[way, source, chunk],
            recv_sem=kv_recv_sem.at[source, chunk],
            device_id=(target, col),
            device_id_type=MESH,
        )

    def pass_on(source, chunk, right, left, act):
        if right:

            @pl.when(chip + 1 < chips)
            def _():
                act(kv_copy(source, chunk, 0, row + 2))

        if left:

            @pl.when(chip >= 1)
            def _():
                act(kv_copy(source, chunk, 1, row - 2))

        act(kv_copy(source, chunk, 2, partner))

    def start(copy):
        copy.start()

    def finish(copy):
        copy.wait_send()

    def keys_of(rows_in, source):
        cosine, sine = tables(source)
        projected = jnp.dot(rows_in, w_key[...], preferred_element_type=jnp.float32)
        for pair in range(pairs):
            kv[source, 0, pair] = rope(
                projected[:, pair * 128 : pair * 128 + 128], cosine, sine
            ).astype(jnp.bfloat16)

    def values_of(rows_in, source):
        projected = jnp.dot(rows_in, w_value[...], preferred_element_type=jnp.float32)
        for pair in range(pairs):
            kv[source, 1, pair] = projected[:, pair * 128 : pair * 128 + 128].astype(jnp.bfloat16)

    pl.semaphore_wait(barrier, greetings)

    @pl.when(outer)
    def _():
        for part in range(2):
            far_out(part).start()

    attn_in = normalize(hidden_ref[...])
    loads[0].wait()
    keys_of(attn_in, row)
    pass_on(row, 0, True, True, start)
    loads[1].wait()
    values_of(attn_in, row)
    pass_on(row, 1, True, True, start)

    def gain_copy(source, target):
        return pltpu.make_async_remote_copy(
            src_ref=gain_sums.at[source],
            dst_ref=gain_sums.at[source],
            send_sem=gain_send_sem.at[target],
            recv_sem=gain_recv_sem.at[source],
            device_id=(row, target),
            device_id_type=MESH,
        )

    others = [(col + step) % cols for step in range(1, cols)]
    loads[2].wait()
    cosine, sine = tables(row)
    projected = jnp.dot(attn_in, w_query[...], preferred_element_type=jnp.float32) * HD ** (-0.5)
    for pair in range(pairs):
        turned = rope(projected[:, pair * 128 : pair * 128 + 128], cosine, sine)
        query[pair, :count] = jnp.where(first_head, turned, 0.0).astype(jnp.bfloat16)
        query[pair, count:] = jnp.where(first_head, 0.0, turned).astype(jnp.bfloat16)
    bins = table_ref.shape[0]
    table[...] = jnp.zeros_like(table)
    table[:bins] = table_ref[...]
    slot_rows = rel_slots.shape[1]
    col_count = bins_ref.shape[1]
    slots = bins_ref.shape[0] // slot_rows

    def rel_copy(index):
        return pltpu.make_async_copy(
            rel_slots.at[index % 2],
            rel_hbm.at[pl.ds(pl.multiple_of(index * slot_rows, slot_rows), slot_rows)],
            rel_sem.at[index % 2],
        )

    def spell(begin, end):
        @pl.loop(begin, end)
        def _(index):
            @pl.when(index >= 2)
            def _():
                rel_copy(index - 2).wait()

            picked = bins_ref[pl.ds(pl.multiple_of(index * slot_rows, slot_rows), slot_rows)]
            codes = lax.broadcasted_iota(jnp.int32, (table.shape[0], col_count), 0)
            hot = jnp.concatenate(
                [
                    jnp.where(picked[i : i + 1, :] == codes, 1.0, 0.0).astype(jnp.bfloat16)
                    for i in range(slot_rows)
                ],
                1,
            )
            chosen = lax.dot_general(
                hot, table[...], (((0,), (0,)), ((), ())), preferred_element_type=jnp.float32
            )
            rel_slots[index % 2] = chosen.astype(jnp.bfloat16).reshape(rel_slots.shape[1:])
            rel_copy(index).start()

    totals[...] = jnp.zeros_like(totals)
    numerator[...] = jnp.zeros_like(numerator)

    def score(source, slot):
        for pair in range(pairs):
            keys = kv[pl.ds(2 * source, 2), 0, pair].reshape(2 * count, 128)
            weights = jnp.exp(
                lax.dot_general(
                    query[pair],
                    keys,
                    (((1,), (1,)), ((), ())),
                    preferred_element_type=jnp.float32,
                )
            )
            totals[pair] += weights[:, :count] + weights[:, count:]
            shares[slot, pair] = weights.astype(jnp.bfloat16)

    def mix(source, slot):
        for pair in range(pairs):
            values = kv[pl.ds(2 * source, 2), 1, pair].reshape(2 * count, 128)
            numerator[pair] += jnp.dot(
                shares[slot, pair], values, preferred_element_type=jnp.float32
            )

    def arrive(source, chunk):
        kv_copy(source, chunk, 2, partner).wait_recv()

    arrive(partner, 0)
    score(chip, 0)
    loads[4].wait()
    gain = final_gain_ref[...].reshape(1, -1)
    coarse = gain.astype(jnp.bfloat16)
    fine = (gain - coarse.astype(jnp.float32)).astype(jnp.bfloat16)
    gains = jnp.concatenate([jnp.broadcast_to(part, (16, features)) for part in (coarse, fine)], 0)
    gained = jnp.dot(gains, w_single[...], preferred_element_type=jnp.float32)
    gain_sums[col] = gained[:8] + gained[16:24]
    for target in others:
        gain_copy(col, target).start()

    arrive(partner, 1)
    mix(chip, 0)

    early = jnp.where(outer, slots, 4)
    spell(0, 2)

    @pl.when(outer)
    def _():
        for part in range(2):
            far_wait(col, part)
            share(part, start)

    spell(2, early)

    @pl.when(outer)
    def _():
        far_wait(side, 0)
        share_corner(0, start)
        far_wait(across, 1)
        share_corner(1, start)


    def near(step, onward):
        from_left = chip - step >= 0
        from_right = chip + step < chips

        def receive(chunk):
            @pl.when(from_left)
            def _():
                arrive(row - 2 * step, chunk)
                pass_on(row - 2 * step, chunk, onward, False, start)

            @pl.when(from_right)
            def _():
                arrive(row + 2 * step, chunk)
                pass_on(row + 2 * step, chunk, False, onward, start)

        def use(chunk):
            @pl.when(from_left)
            def _():
                arrive(partner - 2 * step, chunk)
                (mix if chunk else score)(chip - step, 0)

            @pl.when(from_right)
            def _():
                arrive(partner + 2 * step, chunk)
                (mix if chunk else score)(chip + step, 1)

        receive(0)
        if onward:
            receive(1)
        use(0)
        if not onward:
            receive(1)
        use(1)

    for step in range(1, chips - 1):
        near(step, step < chips - 2)
        if step == 1:
            loads[5].wait()
            w_sides[...] = jnp.dot(
                w_second[...],
                jnp.concatenate([w_left_ref[...], w_right_ref[...]], 1),
                preferred_element_type=jnp.float32,
            ).astype(jnp.bfloat16)
            spell(early, slots)

            @pl.when(outer)
            def _():
                far_wait(side, 1)
                far_wait(across, 0)
                for part in range(2):
                    far_wait(corner, part)
                rows_in = far[...].reshape(count, model_width)
                keys_of(rows_in, farthest)
                pass_on(farthest, 0, False, False, start)
                values_of(rows_in, farthest)
                pass_on(farthest, 1, False, False, start)
                for chunk in range(2):
                    arrive(farthest + partner - row, chunk)
                    (mix if chunk else score)(chips - 1 - chip, 0)


    for pair in range(pairs):
        mixed = numerator[pair] / jnp.sum(totals[pair], -1, keepdims=True)
        context[:, pair * 128 : pair * 128 + 128] = jnp.where(
            first_head, mixed[:count], mixed[count:]
        ).astype(jnp.bfloat16)

    split = count // 2
    halves = [slice(0, split), slice(split, count)]
    firsts = (side, across)
    seconds = (across, side)

    def out_copy(slot, target):
        return pltpu.make_async_remote_copy(
            src_ref=out_send.at[slot],
            dst_ref=out_recv.at[slot],
            send_sem=out_send_sem.at[slot],
            recv_sem=out_recv_sem.at[slot],
            device_id=(row, target),
            device_id_type=MESH,
        )

    def out_part(target):
        columns = pl.ds(pl.multiple_of(target * features, 128), features)
        return jnp.dot(context[...], w_out[:, columns], preferred_element_type=jnp.float32)

    loads[3].wait()
    passing = out_part(corner).astype(jnp.bfloat16)
    for half in range(2):
        out_send[half] = passing[halves[half]]
        out_copy(half, firsts[half]).start()
    kept = [None, None]
    for half in range(2):
        passing = out_part(firsts[half])
        out_send[2 + half] = passing[halves[half]].astype(jnp.bfloat16)
        out_copy(2 + half, firsts[half]).start()
        kept[1 - half] = passing[halves[1 - half]]
    for half in range(2):
        out_copy(half, firsts[half]).wait_recv()
        out_send[4 + half] = (kept[half] + out_recv[half].astype(jnp.float32)).astype(jnp.bfloat16)
        out_copy(4 + half, seconds[half]).start()
    loads[6].wait()
    resid = own[...].astype(jnp.float32) + out_part(col)
    collected = []
    for half in range(2):
        out_copy(2 + half, firsts[half]).wait_recv()
        out_copy(4 + half, seconds[half]).wait_recv()
        collected.append(
            resid[halves[half]]
            + out_recv[2 + half].astype(jnp.float32)
            + out_recv[4 + half].astype(jnp.float32)
        )
    resid = jnp.concatenate(collected, 0)

    def stat_copy(source, target):
        return pltpu.make_async_remote_copy(
            src_ref=stat_send.at[target],
            dst_ref=stat_recv.at[source],
            send_sem=stat_send_sem.at[target],
            recv_sem=stat_recv_sem.at[source],
            device_id=(row, target),
            device_id_type=MESH,
        )

    middle = jnp.sum(resid, -1, keepdims=True) / features
    centred = resid - middle
    spread_sum = jnp.sum(centred * centred, -1, keepdims=True)
    stats = jnp.where(lane < 1, middle, spread_sum)
    for index in range(cols):
        stat_send[index] = stats[index * piece : (index + 1) * piece]
    for target in others:
        stat_copy(col, target).start()
    final = (centred * final_gain_ref[...].reshape(1, -1)).astype(jnp.bfloat16)

    def single_copy(source, target):
        return pltpu.make_async_remote_copy(
            src_ref=single_send.at[target],
            dst_ref=single_recv.at[source],
            send_sem=single_send_sem.at[target],
            recv_sem=single_recv_sem.at[source],
            device_id=(row, target),
            device_id_type=MESH,
        )

    part = jnp.dot(final, w_single[...], preferred_element_type=jnp.float32)
    for index in range(cols):
        block = part[index * piece : (index + 1) * piece]
        single_own[index] = block
        single_send[index] = block.astype(jnp.bfloat16)
    for target in others:
        single_copy(col, target).start()
    for source in others:
        stat_copy(source, source).wait_recv()
        gain_copy(source, source).wait_recv()
    stat_recv[col] = stat_send[col]
    middles = [stat_recv[index][:, 0:1] for index in range(cols)]
    average = sum(middles) / cols
    variance = sum(stat_recv[index][:, 1:2] for index in range(cols)) / model_width
    variance += sum((middles[index] - average) * (middles[index] - average) for index in range(cols)) / cols
    scale = lax.rsqrt(variance + epsilon)
    summed = single_own[col]
    for index in range(cols):
        summed += (middles[index] - average) * gain_sums[index][0:1]
    for source in others:
        single_copy(source, source).wait_recv()
        summed += single_recv[source].astype(jnp.float32)
    lifted = jnp.maximum(summed * scale, 0.0).astype(jnp.bfloat16)
    channels = w_left_ref.shape[1]
    both = jnp.dot(lifted, w_sides[...], preferred_element_type=jnp.float32).astype(jnp.bfloat16)

    def sides_copy(source, target):
        return pltpu.make_async_remote_copy(
            src_ref=sides.at[source],
            dst_ref=sides.at[source],
            send_sem=sides_send_sem.at[target],
            recv_sem=sides_recv_sem.at[source],
            device_id=(row, target),
            device_id_type=MESH,
        )

    def right_copy(slot, index, step):
        return pltpu.make_async_remote_copy(
            src_ref=right_own,
            dst_ref=right_all.at[slot, index],
            send_sem=right_send_sem.at[step],
            recv_sem=right_recv_sem.at[slot, index],
            device_id=((row + step) % rows, row // owners),
            device_id_type=MESH,
        )

    right_own[...] = both[:, channels:]
    for step in range(1, rows):
        right_copy(row % owners, col, step).start()

    @pl.when(jnp.logical_not(is_owner))
    def _():
        right_copy(row % owners, col, 0).start()

    sides[col] = both[:, :channels]
    for target in others:
        sides_copy(col, target).start()

    @pl.when(is_owner)
    def _():
        right_all[row % owners, col] = right_own[...]

    for source in others:
        sides_copy(source, source).wait_recv()
    for index in range(cols):
        left_ref[index * piece : (index + 1) * piece] = sides[index]
    for slot in range(owners):
        for index in range(cols):

            @pl.when(jnp.logical_or(row != col * owners + slot, col != index))
            def _():
                right_copy(slot, index, 1).wait_recv()

            start_row = slot * count + index * piece
            right_ref[start_row : start_row + piece] = right_all[slot, index]

    for chunk in range(2):
        pass_on(row, chunk, True, True, finish)
        for step in range(1, chips - 1):

            @pl.when(chip - step >= 0)
            def _():
                pass_on(row - 2 * step, chunk, step < chips - 2, False, finish)

            @pl.when(chip + step < chips)
            def _():
                pass_on(row + 2 * step, chunk, False, step < chips - 2, finish)

    @pl.when(outer)
    def _():
        for part in range(2):
            pass_on(farthest, part, False, False, finish)
            far_out(part).wait_send()
            share(part, finish)
            share_corner(part, finish)

    rel_copy(slots - 2).wait()
    rel_copy(slots - 1).wait()
    for half in range(2):
        out_copy(half, firsts[half]).wait_send()
        out_copy(2 + half, firsts[half]).wait_send()
        out_copy(4 + half, seconds[half]).wait_send()
    for target in others:
        stat_copy(col, target).wait_send()
        single_copy(col, target).wait_send()
        sides_copy(col, target).wait_send()
        gain_copy(col, target).wait_send()

    for step in range(1, rows):
        right_copy(row % owners, col, step).wait_send()

    @pl.when(jnp.logical_not(is_owner))
    def _():
        right_copy(row % owners, col, 0).wait_send()


def padded(array, axis, size, groups=1):
    width = array.shape[axis] // groups
    if width == size:
        return array
    shape = array.shape
    array = array.reshape(shape[:axis] + (groups, width) + shape[axis + 1 :])
    pads = [(0, 0)] * array.ndim
    pads[axis + 1] = (0, size - width)
    array = jnp.pad(array, pads)
    return array.reshape(shape[:axis] + (groups * size,) + shape[axis + 1 :])


def front_general(
    hidden,
    attn_gain,
    w_query,
    w_key,
    w_value,
    w_out,
    final_gain,
    w_single,
    w_second,
    w_left,
    w_right,
):
    rows = lax.axis_size("row")
    cols = lax.axis_size("col")
    count, model_width = hidden.shape
    width = -(-w_query.shape[1] // 128) * 128
    features = -(-w_single.shape[0] // 128) * 128
    pairs = width // 128
    piece = count // cols
    owners = rows // cols
    single_width = w_second.shape[0]
    channels = w_left.shape[1]
    positions = lax.axis_index("row") * count + jnp.arange(count, dtype=jnp.int32)
    frequency = jnp.exp(
        jnp.arange(HD // 2, dtype=jnp.float32) * (-2.0 * math.log(10000.0) / HD)
    )
    angles = positions.astype(jnp.float32)[:, None] * frequency[None, :]
    cosine = jnp.cos(angles)
    sine = jnp.sin(angles)
    cosine = jnp.concatenate([cosine] * 4, -1)
    sine = jnp.concatenate([-sine, sine, -sine, sine], -1)
    weights = (
        padded(w_query, 1, width),
        padded(w_key, 1, width),
        padded(w_value, 1, width),
        padded(padded(w_out, 0, width), 1, features, cols),
        padded(w_single, 0, features),
        w_second,
    )
    vmem = pl.BlockSpec(memory_space=pltpu.VMEM)
    anywhere = pl.BlockSpec(memory_space=pl.ANY)
    bf16 = jnp.bfloat16
    f32 = jnp.float32
    dma = pltpu.SemaphoreType.DMA
    return pl.pallas_call(
        functools.partial(front_kernel, rows, cols, model_width),
        out_shape=(
            jax.ShapeDtypeStruct((count, channels), bf16),
            jax.ShapeDtypeStruct((owners * count, channels), bf16),
        ),
        in_specs=[vmem, anywhere] + [vmem] * 4 + [anywhere] * 6 + [vmem] * 2,
        out_specs=(vmem, vmem),
        scratch_shapes=[pltpu.VMEM(weight.shape, bf16) for weight in weights]
        + [
            pltpu.VMEM((count, features), bf16),
            pltpu.VMEM((rows, 2, pairs, count, 128), bf16),
            pltpu.VMEM((pairs, 2 * count, 128), bf16),
            pltpu.VMEM((pairs, 2 * count, count), f32),
            pltpu.VMEM((pairs, 2 * count, 128), f32),
            pltpu.VMEM((count, width), bf16),
            pltpu.VMEM((cols, count, features), bf16),
            pltpu.VMEM((cols, count, features), bf16),
            pltpu.VMEM((8, count), f32),
            pltpu.VMEM((cols, 8, count), f32),
            pltpu.VMEM((cols, piece, single_width), f32),
            pltpu.VMEM((cols, piece, single_width), bf16),
            pltpu.VMEM((cols, piece, single_width), bf16),
            pltpu.VMEM((cols, piece, channels), bf16),
            pltpu.VMEM((piece, channels), bf16),
            pltpu.VMEM((owners, cols, piece, channels), bf16),
            dma((7,)),
            dma((3, rows, 2)),
            dma((rows, 2)),
            dma((cols,)),
            dma((cols,)),
            dma((cols,)),
            dma((cols,)),
            dma((cols,)),
            dma((cols,)),
            dma((cols,)),
            dma((cols,)),
            dma((rows,)),
            dma((owners, cols)),
        ],
        compiler_params=pltpu.CompilerParams(
            collective_id=0, has_side_effects=True, vmem_limit_bytes=56 << 20
        ),
    )(
        hidden,
        padded(hidden, 1, features, cols),
        attn_gain,
        cosine,
        sine,
        padded(final_gain, 0, features),
        *weights,
        w_left,
        w_right,
    )


def spelled_kernel(rel_ref, left_ref, right_ref, gain_ref, expand_ref, contract_ref, out_ref):
    block_rows, col_count, channels = rel_ref.shape
    right = right_ref[...].astype(jnp.float32)
    pair_in = jnp.concatenate(
        [
            rel_ref[i].astype(jnp.float32) + (right + left_ref[i : i + 1, :].astype(jnp.float32))
            for i in range(block_rows)
        ],
        0,
    )
    average = jnp.sum(pair_in, -1, keepdims=True) / channels
    variance = jnp.sum(pair_in * pair_in, -1, keepdims=True) / channels - average * average
    normed = ((pair_in - average) * lax.rsqrt(variance + epsilon) * gain_ref[...]).astype(
        jnp.bfloat16
    )
    expanded = jnp.dot(normed, expand_ref[...], preferred_element_type=jnp.float32)
    expanded = jnp.maximum(expanded.astype(jnp.bfloat16), 0)
    update = jnp.dot(expanded, contract_ref[...], preferred_element_type=jnp.float32)
    out_ref[...] = (pair_in + update).astype(out_ref.dtype).reshape(out_ref.shape)


def spelled_stage(rel, left, right, pair_gain, w_expand, w_contract):
    row_count, col_count, channels = rel.shape
    block_rows = math.gcd(row_count, 32)
    whole = lambda array: pl.BlockSpec(array.shape, lambda i: (0, 0))
    gain = pair_gain.reshape(1, channels)
    tile = pl.BlockSpec((block_rows, col_count, channels), lambda i: (i, 0, 0))
    return pl.pallas_call(
        spelled_kernel,
        grid=(row_count // block_rows,),
        in_specs=[
            tile,
            pl.BlockSpec((block_rows, channels), lambda i: (i, 0)),
            whole(right),
            whole(gain),
            whole(w_expand),
            whole(w_contract),
        ],
        out_specs=tile,
        out_shape=jax.ShapeDtypeStruct(rel.shape, jnp.bfloat16),
        compiler_params=pltpu.CompilerParams(
            dimension_semantics=("arbitrary",), vmem_limit_bytes=56 << 20
        ),
    )(rel, left, right, gain, w_expand, w_contract)


def front_plane(
    hidden,
    attn_gain,
    w_query,
    w_key,
    w_value,
    w_out,
    final_gain,
    w_single,
    w_second,
    w_left,
    w_right,
    rel_bins,
    rel_table,
):
    rows = lax.axis_size("row")
    cols = lax.axis_size("col")
    count, model_width = hidden.shape
    width = -(-w_query.shape[1] // 128) * 128
    features = -(-w_single.shape[0] // 128) * 128
    pairs = width // 128
    piece = count // cols
    owners = rows // cols
    single_width = w_second.shape[0]
    channels = w_left.shape[1]
    frequency = np.exp(np.arange(HD // 2) * (-2.0 * math.log(10000.0) / HD))
    frequency = np.concatenate([frequency] * 4)[None, :]
    offsets = np.arange(count)[:, None] * frequency
    steps = (np.arange(rows) * count)[:, None] * frequency
    angles = [
        jnp.asarray(turn(angle), jnp.float32)
        for angle in (offsets, steps)
        for turn in (np.cos, np.sin)
    ]
    weights = (w_query, w_key, w_value, w_out, w_single, w_second)
    vmem = pl.BlockSpec(memory_space=pltpu.VMEM)
    anywhere = pl.BlockSpec(memory_space=pl.ANY)
    bf16 = jnp.bfloat16
    f32 = jnp.float32
    dma = pltpu.SemaphoreType.DMA
    return pl.pallas_call(
        functools.partial(plane_kernel, rows, cols, model_width),
        out_shape=(
            jax.ShapeDtypeStruct((count, channels), bf16),
            jax.ShapeDtypeStruct((owners * count, channels), bf16),
            jax.ShapeDtypeStruct(rel_bins.shape + (channels,), bf16),
        ),
        in_specs=[vmem, anywhere] + [vmem] * 6 + [anywhere] * 6 + [vmem] * 4,
        out_specs=(vmem, vmem, anywhere),
        scratch_shapes=[pltpu.VMEM(weight.shape, bf16) for weight in weights]
        + [
            pltpu.VMEM((count, features), bf16),
            pltpu.VMEM((2, piece // 2, model_width), bf16),
            pltpu.VMEM((cols, 2, piece // 2, model_width), bf16),
            pltpu.VMEM((rows, 2, pairs, count, 128), bf16),
            pltpu.VMEM((pairs, 2 * count, 128), bf16),
            pltpu.VMEM((pairs, 2 * count, count), f32),
            pltpu.VMEM((2, pairs, 2 * count, 2 * count), bf16),
            pltpu.VMEM((pairs, 2 * count, 128), f32),
            pltpu.VMEM((single_width, 2 * channels), bf16),
            pltpu.VMEM((count, width), bf16),
            pltpu.VMEM((6, count // 2, features), bf16),
            pltpu.VMEM((6, count // 2, features), bf16),
            pltpu.VMEM((cols, piece, 128), f32),
            pltpu.VMEM((cols, piece, 128), f32),
            pltpu.VMEM((cols, 8, single_width), f32),
            pltpu.VMEM((cols, piece, single_width), f32),
            pltpu.VMEM((cols, piece, single_width), bf16),
            pltpu.VMEM((cols, piece, single_width), bf16),
            pltpu.VMEM((cols, piece, channels), bf16),
            pltpu.VMEM((piece, channels), bf16),
            pltpu.VMEM((owners, cols, piece, channels), bf16),
            pltpu.VMEM((-(-rel_table.shape[0] // 16) * 16, channels), bf16),
            pltpu.VMEM((2, rel_bins.shape[0] // 8, rel_bins.shape[1], channels), bf16),
            dma((7,)),
            dma((2,)),
            dma((3, 2)),
            dma((cols, 2)),
            dma((3, rows, 2)),
            dma((rows, 2)),
            dma((6,)),
            dma((6,)),
            dma((cols,)),
            dma((cols,)),
            dma((cols,)),
            dma((cols,)),
            dma((cols,)),
            dma((cols,)),
            dma((rows,)),
            dma((owners, cols)),
            dma((cols,)),
            dma((cols,)),
            dma((2,)),
        ],
        compiler_params=pltpu.CompilerParams(
            collective_id=0, has_side_effects=True, vmem_limit_bytes=56 << 20
        ),
    )(
        hidden,
        hidden,
        attn_gain,
        *angles,
        final_gain,
        *weights,
        w_left,
        w_right,
        rel_bins,
        rel_table,
    )


def local(
    hidden,
    rel_bins,
    attn_gain,
    w_query,
    w_key,
    w_value,
    w_out,
    final_gain,
    w_single,
    w_second,
    w_left,
    w_right,
    rel_table,
    pair_gain,
    w_expand,
    w_contract,
):
    rows = lax.axis_size("row")
    cols = lax.axis_size("col")
    aligned = w_query.shape[1] % 128 == 0 and hidden.shape[0] % (32 * cols) == 0
    operands = (
        hidden,
        attn_gain,
        w_query,
        w_key,
        w_value,
        w_out,
        final_gain,
        w_single,
        w_second,
        w_left,
        w_right,
    )
    if rows == 2 * cols and cols == 4 and aligned:
        left, right, rel = front_plane(*operands, rel_bins, rel_table)
        return spelled_stage(rel, left, right, pair_gain, w_expand, w_contract)
    left, right = front_general(*operands)
    return pair_stage(rel_bins, left, right, rel_table, pair_gain, w_expand, w_contract)


def solution(mesh):
    in_specs = (
        P("row", None),
        P("row", "col"),
        P(),
        P(None, "col"),
        P(None, "col"),
        P(None, "col"),
        P("col", None),
        P("col"),
        P("col", None),
        P(),
        P(),
        P(),
        P(),
        P(),
        P(),
        P(),
    )
    out_specs = P("row", "col", None)
    return jax.shard_map(local, mesh=mesh, in_specs=in_specs, out_specs=out_specs, check_vma=False)
```

```python
import functools
import math

import jax
import jax.numpy as jnp
import numpy as np
from jax import lax
from jax.experimental import pallas as pl
from jax.experimental.pallas import tpu as pltpu
from jax.sharding import PartitionSpec as P

HD = 64
MESH = pl.DeviceIdType.MESH


epsilon = 1e-05


def pair_kernel(bins_ref, left_ref, right_ref, table_ref, gain_ref, expand_ref, contract_ref, out_ref, table):
    block_rows, col_count = bins_ref.shape
    channels = right_ref.shape[1]
    right = right_ref[...].astype(jnp.float32)
    bins = table_ref.shape[0]

    @pl.when(pl.program_id(0) == 0)
    def _():
        table[...] = jnp.zeros_like(table)
        table[:bins] = table_ref[...]

    codes = lax.broadcasted_iota(jnp.int32, (table.shape[0], col_count), 0)
    hot = jnp.concatenate(
        [
            jnp.where(bins_ref[i : i + 1, :] == codes, 1.0, 0.0).astype(jnp.bfloat16)
            for i in range(block_rows)
        ],
        1,
    )
    part = lax.dot_general(
        hot, table[...], (((0,), (0,)), ((), ())), preferred_element_type=jnp.float32
    )
    pair_in = jnp.concatenate(
        [
            part[i * col_count : (i + 1) * col_count]
            + (right + left_ref[i : i + 1, :].astype(jnp.float32))
            for i in range(block_rows)
        ],
        0,
    )
    average = jnp.sum(pair_in, -1, keepdims=True) / channels
    variance = jnp.sum(pair_in * pair_in, -1, keepdims=True) / channels - average * average
    normed = ((pair_in - average) * lax.rsqrt(variance + epsilon) * gain_ref[...]).astype(
        jnp.bfloat16
    )
    expanded = jnp.dot(normed, expand_ref[...], preferred_element_type=jnp.float32)
    expanded = jnp.maximum(expanded.astype(jnp.bfloat16), 0)
    update = jnp.dot(expanded, contract_ref[...], preferred_element_type=jnp.float32)
    out_ref[...] = (pair_in + update).astype(out_ref.dtype).reshape(out_ref.shape)


def pair_stage(rel_bins, left, right, rel_table, pair_gain, w_expand, w_contract):
    row_count, col_count = rel_bins.shape
    channels = right.shape[1]
    block_rows = math.gcd(row_count, 32)
    bins_padded = -(-rel_table.shape[0] // 128) * 128
    whole = lambda array: pl.BlockSpec(array.shape, lambda i: (0, 0))
    gain = pair_gain.reshape(1, channels)
    return pl.pallas_call(
        pair_kernel,
        grid=(row_count // block_rows,),
        in_specs=[
            pl.BlockSpec((block_rows, col_count), lambda i: (i, 0)),
            pl.BlockSpec((block_rows, channels), lambda i: (i, 0)),
            whole(right),
            whole(rel_table),
            whole(gain),
            whole(w_expand),
            whole(w_contract),
        ],
        out_specs=pl.BlockSpec((block_rows, col_count, channels), lambda i: (i, 0, 0)),
        out_shape=jax.ShapeDtypeStruct((row_count, col_count, channels), jnp.bfloat16),
        scratch_shapes=[pltpu.VMEM((bins_padded, channels), jnp.bfloat16)],
        compiler_params=pltpu.CompilerParams(
            dimension_semantics=("arbitrary",), vmem_limit_bytes=56 << 20
        ),
    )(rel_bins, left, right, rel_table, gain, w_expand, w_contract)


def front_kernel(
    rows,
    cols,
    model_width,
    hidden_ref,
    own_hbm,
    attn_gain_ref,
    cos_ref,
    sin_ref,
    final_gain_ref,
    w_query_hbm,
    w_key_hbm,
    w_value_hbm,
    w_out_hbm,
    w_single_hbm,
    w_second_hbm,
    w_left_ref,
    w_right_ref,
    left_ref,
    right_ref,
    w_query,
    w_key,
    w_value,
    w_out,
    w_single,
    w_second,
    own,
    kv,
    query,
    totals,
    numerator,
    context,
    out_send,
    out_recv,
    stat_send,
    stat_recv,
    single_own,
    single_send,
    single_recv,
    sides,
    right_own,
    right_all,
    weight_sem,
    kv_send_sem,
    kv_recv_sem,
    out_send_sem,
    out_recv_sem,
    stat_send_sem,
    stat_recv_sem,
    single_send_sem,
    single_recv_sem,
    sides_send_sem,
    sides_recv_sem,
    right_send_sem,
    right_recv_sem,
):
    row = lax.axis_index("row")
    col = lax.axis_index("col")
    count = hidden_ref.shape[0]
    pairs = query.shape[0]
    features = w_single.shape[0]
    piece = single_own.shape[1]
    owners = rows // cols
    chips = rows // 2
    chip = row // 2
    core = row % 2
    partner = row + 1 - 2 * core

    own_columns = pl.ds(pl.multiple_of(col * features, 128), features)
    loads = []
    for index, (source, target) in enumerate(
        (
            (w_key_hbm, w_key),
            (w_value_hbm, w_value),
            (w_query_hbm, w_query),
            (w_out_hbm, w_out),
            (w_single_hbm, w_single),
            (w_second_hbm, w_second),
            (own_hbm.at[:, own_columns], own),
        )
    ):
        load = pltpu.make_async_copy(source, target, weight_sem.at[index])
        load.start()
        loads.append(load)

    barrier = pltpu.get_barrier_semaphore()
    is_owner = row // owners == col

    def greet(target_row, target_col):
        pl.semaphore_signal(
            barrier, inc=1, device_id=(target_row, target_col), device_id_type=MESH
        )

    greet(partner, col)

    @pl.when(chip + 1 < chips)
    def _():
        greet(row + 2, col)

    @pl.when(chip >= 1)
    def _():
        greet(row - 2, col)

    for slot in range(owners):
        for index in range(cols):

            @pl.when(jnp.logical_or(row != col * owners + slot, col != index))
            def _():
                greet(col * owners + slot, index)

    greetings = cols + rows
    greetings += jnp.where(chip + 1 < chips, 1, 0) + jnp.where(chip >= 1, 1, 0)
    greetings -= jnp.where(is_owner, 1, 0)
    for step in range(1, cols):
        pl.semaphore_signal(
            barrier, inc=1, device_id=(row, (col + step) % cols), device_id_type=MESH
        )

    stream = hidden_ref[...].astype(jnp.float32)
    average = jnp.sum(stream, -1, keepdims=True) / model_width
    variance = jnp.sum(stream * stream, -1, keepdims=True) / model_width - average * average
    attn_in = (
        (stream - average) * lax.rsqrt(variance + epsilon) * attn_gain_ref[...].reshape(1, -1)
    ).astype(jnp.bfloat16)
    cosine = cos_ref[...]
    sine = sin_ref[...]
    lane = lax.broadcasted_iota(jnp.int32, (count, 128), 1)
    first_half = lane % HD < HD // 2
    first_head = lane < HD

    def rope(vectors):
        turned = jnp.where(
            first_half,
            pltpu.roll(vectors, 128 - HD // 2, 1),
            pltpu.roll(vectors, HD // 2, 1),
        )
        return vectors * cosine + turned * sine

    def kv_copy(source, chunk, way, target):
        return pltpu.make_async_remote_copy(
            src_ref=kv.at[source, chunk],
            dst_ref=kv.at[source, chunk],
            send_sem=kv_send_sem.at[way, source, chunk],
            recv_sem=kv_recv_sem.at[source, chunk],
            device_id=(target, col),
            device_id_type=MESH,
        )

    def pass_on(source, chunk, right, left, act):
        if right:

            @pl.when(chip + 1 < chips)
            def _():
                act(kv_copy(source, chunk, 0, row + 2))

        if left:

            @pl.when(chip >= 1)
            def _():
                act(kv_copy(source, chunk, 1, row - 2))

        act(kv_copy(source, chunk, 2, partner))

    def start(copy):
        copy.start()

    def finish(copy):
        copy.wait_send()

    loads[0].wait()
    projected = jnp.dot(attn_in, w_key[...], preferred_element_type=jnp.float32)
    for pair in range(pairs):
        kv[row, 0, pair] = rope(projected[:, pair * 128 : pair * 128 + 128]).astype(jnp.bfloat16)
    pl.semaphore_wait(barrier, greetings)
    pass_on(row, 0, True, True, start)
    loads[1].wait()
    projected = jnp.dot(attn_in, w_value[...], preferred_element_type=jnp.float32)
    for pair in range(pairs):
        kv[row, 1, pair] = projected[:, pair * 128 : pair * 128 + 128].astype(jnp.bfloat16)
    pass_on(row, 1, True, True, start)
    loads[2].wait()
    projected = jnp.dot(attn_in, w_query[...], preferred_element_type=jnp.float32) * HD ** (-0.5)
    for pair in range(pairs):
        turned = rope(projected[:, pair * 128 : pair * 128 + 128])
        query[pair, :count] = jnp.where(first_head, turned, 0.0).astype(jnp.bfloat16)
        query[pair, count:] = jnp.where(first_head, 0.0, turned).astype(jnp.bfloat16)
    totals[...] = jnp.zeros_like(totals)
    numerator[...] = jnp.zeros_like(numerator)

    def attend(source):
        for pair in range(pairs):
            scores = lax.dot_general(
                query[pair],
                kv[source, 0, pair],
                (((1,), (1,)), ((), ())),
                preferred_element_type=jnp.float32,
            )
            weights = jnp.exp(scores)
            totals[pair] += weights
            numerator[pair] += jnp.dot(
                weights.astype(jnp.bfloat16),
                kv[source, 1, pair],
                preferred_element_type=jnp.float32,
            )

    def arrive(source):
        for chunk in range(2):
            kv_copy(source, chunk, 2, partner).wait_recv()

    attend(row)
    arrive(partner)
    attend(partner)

    @pl.loop(1, chips)
    def _(step):
        from_left = chip - step >= 0
        from_right = chip + step < chips
        for chunk in range(2):

            @pl.when(from_left)
            def _():
                source = row - 2 * step
                kv_copy(source, chunk, 2, partner).wait_recv()
                pass_on(source, chunk, True, False, start)

            @pl.when(from_right)
            def _():
                source = row + 2 * step
                kv_copy(source, chunk, 2, partner).wait_recv()
                pass_on(source, chunk, False, True, start)

        @pl.when(from_left)
        def _():
            attend(row - 2 * step)
            arrive(partner - 2 * step)
            attend(partner - 2 * step)

        @pl.when(from_right)
        def _():
            attend(row + 2 * step)
            arrive(partner + 2 * step)
            attend(partner + 2 * step)

    for pair in range(pairs):
        shares = numerator[pair] / jnp.sum(totals[pair], -1, keepdims=True)
        context[:, pair * 128 : pair * 128 + 128] = jnp.where(
            first_head, shares[:count], shares[count:]
        ).astype(jnp.bfloat16)

    def out_copy(source, target):
        return pltpu.make_async_remote_copy(
            src_ref=out_send.at[target],
            dst_ref=out_recv.at[source],
            send_sem=out_send_sem.at[target],
            recv_sem=out_recv_sem.at[source],
            device_id=(row, target),
            device_id_type=MESH,
        )

    def out_part(target):
        columns = pl.ds(pl.multiple_of(target * features, 128), features)
        return jnp.dot(context[...], w_out[:, columns], preferred_element_type=jnp.float32)

    others = [(col + step) % cols for step in range(1, cols)]
    loads[3].wait()
    for target in others:
        out_send[target] = out_part(target).astype(jnp.bfloat16)
        out_copy(col, target).start()
    loads[6].wait()
    resid = own[...].astype(jnp.float32) + out_part(col)
    for source in others:
        out_copy(source, source).wait_recv()
        resid += out_recv[source].astype(jnp.float32)

    def stat_copy(source, target):
        return pltpu.make_async_remote_copy(
            src_ref=stat_send,
            dst_ref=stat_recv.at[source],
            send_sem=stat_send_sem.at[target],
            recv_sem=stat_recv_sem.at[source],
            device_id=(row, target),
            device_id_type=MESH,
        )

    sum_first = jnp.sum(resid, -1, keepdims=True)
    sum_second = jnp.sum(resid * resid, -1, keepdims=True)
    sums = jnp.transpose(jnp.where(lane < 4, sum_first, sum_second))[:8]
    stat_send[...] = sums
    for target in others:
        stat_copy(col, target).start()
    for source in others:
        stat_copy(source, source).wait_recv()
        sums += stat_recv[source]
    sums = jnp.transpose(jnp.concatenate([sums] * 16, 0))
    average = sums[:, 0:1] / model_width
    variance = sums[:, 4:5] / model_width - average * average
    final = (
        (resid - average) * lax.rsqrt(variance + epsilon) * final_gain_ref[...].reshape(1, -1)
    ).astype(jnp.bfloat16)

    def single_copy(source, target):
        return pltpu.make_async_remote_copy(
            src_ref=single_send.at[target],
            dst_ref=single_recv.at[source],
            send_sem=single_send_sem.at[target],
            recv_sem=single_recv_sem.at[source],
            device_id=(row, target),
            device_id_type=MESH,
        )

    loads[4].wait()
    part = jnp.dot(final, w_single[...], preferred_element_type=jnp.float32)
    for index in range(cols):
        block = part[index * piece : (index + 1) * piece]
        single_own[index] = block
        single_send[index] = block.astype(jnp.bfloat16)
    for target in others:
        single_copy(col, target).start()
    summed = single_own[col]
    for source in others:
        single_copy(source, source).wait_recv()
        summed += single_recv[source].astype(jnp.float32)
    lifted = jnp.maximum(summed, 0.0).astype(jnp.bfloat16)
    loads[5].wait()
    single = jnp.dot(lifted, w_second[...], preferred_element_type=jnp.float32)
    single = single.astype(jnp.bfloat16)

    def sides_copy(source, target):
        return pltpu.make_async_remote_copy(
            src_ref=sides.at[source],
            dst_ref=sides.at[source],
            send_sem=sides_send_sem.at[target],
            recv_sem=sides_recv_sem.at[source],
            device_id=(row, target),
            device_id_type=MESH,
        )

    def right_copy(slot, index, step):
        return pltpu.make_async_remote_copy(
            src_ref=right_own,
            dst_ref=right_all.at[slot, index],
            send_sem=right_send_sem.at[step],
            recv_sem=right_recv_sem.at[slot, index],
            device_id=((row + step) % rows, row // owners),
            device_id_type=MESH,
        )

    right_own[...] = jnp.dot(
        single, w_right_ref[...], preferred_element_type=jnp.float32
    ).astype(jnp.bfloat16)
    for step in range(1, rows):
        right_copy(row % owners, col, step).start()

    @pl.when(jnp.logical_not(is_owner))
    def _():
        right_copy(row % owners, col, 0).start()

    sides[col] = jnp.dot(single, w_left_ref[...], preferred_element_type=jnp.float32).astype(
        jnp.bfloat16
    )
    for target in others:
        sides_copy(col, target).start()

    @pl.when(is_owner)
    def _():
        right_all[row % owners, col] = right_own[...]

    for source in others:
        sides_copy(source, source).wait_recv()
    for index in range(cols):
        left_ref[index * piece : (index + 1) * piece] = sides[index]
    for slot in range(owners):
        for index in range(cols):

            @pl.when(jnp.logical_or(row != col * owners + slot, col != index))
            def _():
                right_copy(slot, index, 1).wait_recv()

            start_row = slot * count + index * piece
            right_ref[start_row : start_row + piece] = right_all[slot, index]

    for chunk in range(2):
        pass_on(row, chunk, True, True, finish)

    @pl.loop(1, chips)
    def _(step):
        for chunk in range(2):

            @pl.when(chip - step >= 0)
            def _():
                pass_on(row - 2 * step, chunk, True, False, finish)

            @pl.when(chip + step < chips)
            def _():
                pass_on(row + 2 * step, chunk, False, True, finish)

    for target in others:
        out_copy(col, target).wait_send()
        stat_copy(col, target).wait_send()
        single_copy(col, target).wait_send()
        sides_copy(col, target).wait_send()

    for step in range(1, rows):
        right_copy(row % owners, col, step).wait_send()

    @pl.when(jnp.logical_not(is_owner))
    def _():
        right_copy(row % owners, col, 0).wait_send()


def plane_kernel(
    rows,
    cols,
    model_width,
    hidden_ref,
    own_hbm,
    attn_gain_ref,
    cos_ref,
    sin_ref,
    cos_step_ref,
    sin_step_ref,
    final_gain_ref,
    w_query_hbm,
    w_key_hbm,
    w_value_hbm,
    w_out_hbm,
    w_single_hbm,
    w_second_hbm,
    w_left_ref,
    w_right_ref,
    bins_ref,
    table_ref,
    left_ref,
    right_ref,
    rel_hbm,
    w_query,
    w_key,
    w_value,
    w_out,
    w_single,
    w_second,
    own,
    piece_send,
    far,
    kv,
    query,
    totals,
    shares,
    numerator,
    w_sides,
    context,
    out_send,
    out_recv,
    stat_send,
    stat_recv,
    gain_sums,
    single_own,
    single_send,
    single_recv,
    sides,
    right_own,
    right_all,
    table,
    rel_slots,
    weight_sem,
    far_out_sem,
    far_send_sem,
    far_recv_sem,
    kv_send_sem,
    kv_recv_sem,
    out_send_sem,
    out_recv_sem,
    stat_send_sem,
    stat_recv_sem,
    single_send_sem,
    single_recv_sem,
    sides_send_sem,
    sides_recv_sem,
    right_send_sem,
    right_recv_sem,
    gain_send_sem,
    gain_recv_sem,
    rel_sem,
):
    row = lax.axis_index("row")
    col = lax.axis_index("col")
    count = hidden_ref.shape[0]
    pairs = query.shape[0]
    features = w_single.shape[0]
    piece = single_own.shape[1]
    owners = rows // cols
    chips = rows // 2
    chip = row // 2
    core = row % 2
    partner = row + 1 - 2 * core
    outer = jnp.logical_or(chip == 0, chip == chips - 1)
    farthest = (chips - 1 - chip) * 2 + core
    side = col + 1 - 2 * (col % 2)
    across = (col + 2) % cols
    corner = cols - 1 - col

    own_columns = pl.ds(pl.multiple_of(col * features, 128), features)
    loads = []
    for index, (source, target) in enumerate(
        (
            (w_key_hbm, w_key),
            (w_value_hbm, w_value),
            (w_query_hbm, w_query),
            (w_out_hbm, w_out),
            (w_single_hbm, w_single),
            (w_second_hbm, w_second),
            (own_hbm.at[:, own_columns], own),
        )
    ):
        load = pltpu.make_async_copy(source, target, weight_sem.at[index])
        load.start()
        loads.append(load)

    barrier = pltpu.get_barrier_semaphore()
    is_owner = row // owners == col

    def greet(target_row, target_col):
        pl.semaphore_signal(
            barrier, inc=1, device_id=(target_row, target_col), device_id_type=MESH
        )

    greet(partner, col)

    @pl.when(chip + 1 < chips)
    def _():
        greet(row + 2, col)

    @pl.when(chip >= 1)
    def _():
        greet(row - 2, col)

    @pl.when(outer)
    def _():
        greet(farthest, col)

    greetings = cols + jnp.where(outer, 1, 0)
    greetings += jnp.where(chip + 1 < chips, 1, 0) + jnp.where(chip >= 1, 1, 0)
    for step in range(1, cols):
        pl.semaphore_signal(
            barrier, inc=1, device_id=(row, (col + step) % cols), device_id_type=MESH
        )

    def normalize(values):
        stream = values.astype(jnp.float32)
        average = jnp.sum(stream, -1, keepdims=True) / model_width
        variance = jnp.sum(stream * stream, -1, keepdims=True) / model_width - average * average
        return (
            (stream - average) * lax.rsqrt(variance + epsilon) * attn_gain_ref[...].reshape(1, -1)
        ).astype(jnp.bfloat16)

    half = piece // 2

    @pl.when(outer)
    def _():
        for part in range(2):
            first = pl.multiple_of(col * piece + part * half, half)
            piece_send[part] = normalize(hidden_ref[pl.ds(first, half)])

    lane = lax.broadcasted_iota(jnp.int32, (count, 128), 1)
    first_half = lane % HD < HD // 2
    first_head = lane < HD

    def tables(source):
        cosine = cos_ref[...]
        sine = sin_ref[...]
        cos_step = cos_step_ref[pl.ds(source, 1), :]
        sin_step = sin_step_ref[pl.ds(source, 1), :]
        turned = sine * cos_step + cosine * sin_step
        return cosine * cos_step - sine * sin_step, jnp.where(first_half, -turned, turned)

    def rope(vectors, cosine, sine):
        turned = jnp.where(
            first_half,
            pltpu.roll(vectors, 128 - HD // 2, 1),
            pltpu.roll(vectors, HD // 2, 1),
        )
        return vectors * cosine + turned * sine

    def far_copy(owner, part, way, target):
        return pltpu.make_async_remote_copy(
            src_ref=far.at[owner, part],
            dst_ref=far.at[owner, part],
            send_sem=far_send_sem.at[way, part],
            recv_sem=far_recv_sem.at[owner, part],
            device_id=(row, target),
            device_id_type=MESH,
        )

    def far_out(part):
        return pltpu.make_async_remote_copy(
            src_ref=piece_send.at[part],
            dst_ref=far.at[col, part],
            send_sem=far_out_sem.at[part],
            recv_sem=far_recv_sem.at[col, part],
            device_id=(farthest, col),
            device_id_type=MESH,
        )

    def share(part, act):
        act(far_copy(col, part, 0, side))
        act(far_copy(col, part, 1, across))

    def share_corner(part, act):
        if part == 0:
            act(far_copy(side, part, 2, across))
        else:
            act(far_copy(across, part, 2, side))

    def far_wait(owner, part):
        far_copy(owner, part, 0, side).wait_recv()

    def kv_copy(source, chunk, way, target):
        return pltpu.make_async_remote_copy(
            src_ref=kv.at[source, chunk],
            dst_ref=kv.at[source, chunk],
            send_sem=kv_send_sem.at[way, source, chunk],
            recv_sem=kv_recv_sem.at[source, chunk],
            device_id=(target, col),
            device_id_type=MESH,
        )

    def pass_on(source, chunk, right, left, act):
        if right:

            @pl.when(chip + 1 < chips)
            def _():
                act(kv_copy(source, chunk, 0, row + 2))

        if left:

            @pl.when(chip >= 1)
            def _():
                act(kv_copy(source, chunk, 1, row - 2))

        act(kv_copy(source, chunk, 2, partner))

    def start(copy):
        copy.start()

    def finish(copy):
        copy.wait_send()

    def keys_of(rows_in, source):
        cosine, sine = tables(source)
        projected = jnp.dot(rows_in, w_key[...], preferred_element_type=jnp.float32)
        for pair in range(pairs):
            kv[source, 0, pair] = rope(
                projected[:, pair * 128 : pair * 128 + 128], cosine, sine
            ).astype(jnp.bfloat16)

    def values_of(rows_in, source):
        projected = jnp.dot(rows_in, w_value[...], preferred_element_type=jnp.float32)
        for pair in range(pairs):
            kv[source, 1, pair] = projected[:, pair * 128 : pair * 128 + 128].astype(jnp.bfloat16)

    pl.semaphore_wait(barrier, greetings)

    @pl.when(outer)
    def _():
        for part in range(2):
            far_out(part).start()

    attn_in = normalize(hidden_ref[...])
    loads[0].wait()
    keys_of(attn_in, row)
    pass_on(row, 0, True, True, start)
    loads[1].wait()
    values_of(attn_in, row)
    pass_on(row, 1, True, True, start)

    def gain_copy(source, target):
        return pltpu.make_async_remote_copy(
            src_ref=gain_sums.at[source],
            dst_ref=gain_sums.at[source],
            send_sem=gain_send_sem.at[target],
            recv_sem=gain_recv_sem.at[source],
            device_id=(row, target),
            device_id_type=MESH,
        )

    others = [(col + step) % cols for step in range(1, cols)]
    loads[2].wait()
    cosine, sine = tables(row)
    projected = jnp.dot(attn_in, w_query[...], preferred_element_type=jnp.float32) * HD ** (-0.5)
    for pair in range(pairs):
        turned = rope(projected[:, pair * 128 : pair * 128 + 128], cosine, sine)
        query[pair, :count] = jnp.where(first_head, turned, 0.0).astype(jnp.bfloat16)
        query[pair, count:] = jnp.where(first_head, 0.0, turned).astype(jnp.bfloat16)
    bins = table_ref.shape[0]
    table[...] = jnp.zeros_like(table)
    table[:bins] = table_ref[...]
    slot_rows = rel_slots.shape[1]
    col_count = bins_ref.shape[1]
    slots = bins_ref.shape[0] // slot_rows

    def rel_copy(index):
        return pltpu.make_async_copy(
            rel_slots.at[index % 2],
            rel_hbm.at[pl.ds(pl.multiple_of(index * slot_rows, slot_rows), slot_rows)],
            rel_sem.at[index % 2],
        )

    def spell(begin, end):
        @pl.loop(begin, end)
        def _(index):
            @pl.when(index >= 2)
            def _():
                rel_copy(index - 2).wait()

            picked = bins_ref[pl.ds(pl.multiple_of(index * slot_rows, slot_rows), slot_rows)]
            codes = lax.broadcasted_iota(jnp.int32, (table.shape[0], col_count), 0)
            hot = jnp.concatenate(
                [
                    jnp.where(picked[i : i + 1, :] == codes, 1.0, 0.0).astype(jnp.bfloat16)
                    for i in range(slot_rows)
                ],
                1,
            )
            chosen = lax.dot_general(
                hot, table[...], (((0,), (0,)), ((), ())), preferred_element_type=jnp.float32
            )
            rel_slots[index % 2] = chosen.astype(jnp.bfloat16).reshape(rel_slots.shape[1:])
            rel_copy(index).start()

    totals[...] = jnp.zeros_like(totals)
    numerator[...] = jnp.zeros_like(numerator)

    def score(source, slot):
        for pair in range(pairs):
            keys = kv[pl.ds(2 * source, 2), 0, pair].reshape(2 * count, 128)
            weights = jnp.exp(
                lax.dot_general(
                    query[pair],
                    keys,
                    (((1,), (1,)), ((), ())),
                    preferred_element_type=jnp.float32,
                )
            )
            totals[pair] += weights[:, :count] + weights[:, count:]
            shares[slot, pair] = weights.astype(jnp.bfloat16)

    def mix(source, slot):
        for pair in range(pairs):
            values = kv[pl.ds(2 * source, 2), 1, pair].reshape(2 * count, 128)
            numerator[pair] += jnp.dot(
                shares[slot, pair], values, preferred_element_type=jnp.float32
            )

    def arrive(source, chunk):
        kv_copy(source, chunk, 2, partner).wait_recv()

    arrive(partner, 0)
    score(chip, 0)
    loads[4].wait()
    gain = final_gain_ref[...].reshape(1, -1)
    coarse = gain.astype(jnp.bfloat16)
    fine = (gain - coarse.astype(jnp.float32)).astype(jnp.bfloat16)
    gains = jnp.concatenate([jnp.broadcast_to(part, (16, features)) for part in (coarse, fine)], 0)
    gained = jnp.dot(gains, w_single[...], preferred_element_type=jnp.float32)
    gain_sums[col] = gained[:8] + gained[16:24]
    for target in others:
        gain_copy(col, target).start()

    arrive(partner, 1)
    mix(chip, 0)

    early = jnp.where(outer, slots, 4)
    spell(0, 2)

    @pl.when(outer)
    def _():
        for part in range(2):
            far_wait(col, part)
            share(part, start)

    spell(2, early)

    @pl.when(outer)
    def _():
        far_wait(side, 0)
        share_corner(0, start)
        far_wait(across, 1)
        share_corner(1, start)


    def near(step, onward):
        from_left = chip - step >= 0
        from_right = chip + step < chips

        def receive(chunk):
            @pl.when(from_left)
            def _():
                arrive(row - 2 * step, chunk)
                pass_on(row - 2 * step, chunk, onward, False, start)

            @pl.when(from_right)
            def _():
                arrive(row + 2 * step, chunk)
                pass_on(row + 2 * step, chunk, False, onward, start)

        def use(chunk):
            @pl.when(from_left)
            def _():
                arrive(partner - 2 * step, chunk)
                (mix if chunk else score)(chip - step, 0)

            @pl.when(from_right)
            def _():
                arrive(partner + 2 * step, chunk)
                (mix if chunk else score)(chip + step, 1)

        receive(0)
        if onward:
            receive(1)
        use(0)
        if not onward:
            receive(1)
        use(1)

    for step in range(1, chips - 1):
        near(step, step < chips - 2)
        if step == 1:
            loads[5].wait()
            w_sides[...] = jnp.dot(
                w_second[...],
                jnp.concatenate([w_left_ref[...], w_right_ref[...]], 1),
                preferred_element_type=jnp.float32,
            ).astype(jnp.bfloat16)
            spell(early, slots)

            @pl.when(outer)
            def _():
                far_wait(side, 1)
                far_wait(across, 0)
                for part in range(2):
                    far_wait(corner, part)
                rows_in = far[...].reshape(count, model_width)
                keys_of(rows_in, farthest)
                pass_on(farthest, 0, False, False, start)
                values_of(rows_in, farthest)
                pass_on(farthest, 1, False, False, start)
                for chunk in range(2):
                    arrive(farthest + partner - row, chunk)
                    (mix if chunk else score)(chips - 1 - chip, 0)


    for pair in range(pairs):
        mixed = numerator[pair] / jnp.sum(totals[pair], -1, keepdims=True)
        context[:, pair * 128 : pair * 128 + 128] = jnp.where(
            first_head, mixed[:count], mixed[count:]
        ).astype(jnp.bfloat16)

    split = count // 2
    halves = [slice(0, split), slice(split, count)]
    firsts = (side, across)
    seconds = (across, side)

    def out_copy(slot, target):
        return pltpu.make_async_remote_copy(
            src_ref=out_send.at[slot],
            dst_ref=out_recv.at[slot],
            send_sem=out_send_sem.at[slot],
            recv_sem=out_recv_sem.at[slot],
            device_id=(row, target),
            device_id_type=MESH,
        )

    def out_part(target):
        columns = pl.ds(pl.multiple_of(target * features, 128), features)
        return jnp.dot(context[...], w_out[:, columns], preferred_element_type=jnp.float32)

    loads[3].wait()
    passing = out_part(corner).astype(jnp.bfloat16)
    for half in range(2):
        out_send[half] = passing[halves[half]]
        out_copy(half, firsts[half]).start()
    kept = [None, None]
    for half in range(2):
        passing = out_part(firsts[half])
        out_send[2 + half] = passing[halves[half]].astype(jnp.bfloat16)
        out_copy(2 + half, firsts[half]).start()
        kept[1 - half] = passing[halves[1 - half]]
    for half in range(2):
        out_copy(half, firsts[half]).wait_recv()
        out_send[4 + half] = (kept[half] + out_recv[half].astype(jnp.float32)).astype(jnp.bfloat16)
        out_copy(4 + half, seconds[half]).start()
    loads[6].wait()
    resid = own[...].astype(jnp.float32) + out_part(col)
    collected = []
    for half in range(2):
        out_copy(2 + half, firsts[half]).wait_recv()
        out_copy(4 + half, seconds[half]).wait_recv()
        collected.append(
            resid[halves[half]]
            + out_recv[2 + half].astype(jnp.float32)
            + out_recv[4 + half].astype(jnp.float32)
        )
    resid = jnp.concatenate(collected, 0)

    def stat_copy(source, target):
        return pltpu.make_async_remote_copy(
            src_ref=stat_send.at[target],
            dst_ref=stat_recv.at[source],
            send_sem=stat_send_sem.at[target],
            recv_sem=stat_recv_sem.at[source],
            device_id=(row, target),
            device_id_type=MESH,
        )

    middle = jnp.sum(resid, -1, keepdims=True) / features
    centred = resid - middle
    spread_sum = jnp.sum(centred * centred, -1, keepdims=True)
    stats = jnp.where(lane < 1, middle, spread_sum)
    for index in range(cols):
        stat_send[index] = stats[index * piece : (index + 1) * piece]
    for target in others:
        stat_copy(col, target).start()
    final = (centred * final_gain_ref[...].reshape(1, -1)).astype(jnp.bfloat16)

    def single_copy(source, target):
        return pltpu.make_async_remote_copy(
            src_ref=single_send.at[target],
            dst_ref=single_recv.at[source],
            send_sem=single_send_sem.at[target],
            recv_sem=single_recv_sem.at[source],
            device_id=(row, target),
            device_id_type=MESH,
        )

    part = jnp.dot(final, w_single[...], preferred_element_type=jnp.float32)
    for index in range(cols):
        block = part[index * piece : (index + 1) * piece]
        single_own[index] = block
        single_send[index] = block.astype(jnp.bfloat16)
    for target in others:
        single_copy(col, target).start()
    for source in others:
        stat_copy(source, source).wait_recv()
        gain_copy(source, source).wait_recv()
    stat_recv[col] = stat_send[col]
    middles = [stat_recv[index][:, 0:1] for index in range(cols)]
    average = sum(middles) / cols
    variance = sum(stat_recv[index][:, 1:2] for index in range(cols)) / model_width
    variance += sum((middles[index] - average) * (middles[index] - average) for index in range(cols)) / cols
    scale = lax.rsqrt(variance + epsilon)
    summed = single_own[col]
    for index in range(cols):
        summed += (middles[index] - average) * gain_sums[index][0:1]
    for source in others:
        single_copy(source, source).wait_recv()
        summed += single_recv[source].astype(jnp.float32)
    lifted = jnp.maximum(summed * scale, 0.0).astype(jnp.bfloat16)
    channels = w_left_ref.shape[1]
    both = jnp.dot(lifted, w_sides[...], preferred_element_type=jnp.float32).astype(jnp.bfloat16)

    def sides_copy(source, target):
        return pltpu.make_async_remote_copy(
            src_ref=sides.at[source],
            dst_ref=sides.at[source],
            send_sem=sides_send_sem.at[target],
            recv_sem=sides_recv_sem.at[source],
            device_id=(row, target),
            device_id_type=MESH,
        )

    def right_copy(slot, index, step):
        return pltpu.make_async_remote_copy(
            src_ref=right_own,
            dst_ref=right_all.at[slot, index],
            send_sem=right_send_sem.at[step],
            recv_sem=right_recv_sem.at[slot, index],
            device_id=((row + step) % rows, row // owners),
            device_id_type=MESH,
        )

    right_own[...] = both[:, channels:]
    for step in range(1, rows):
        right_copy(row % owners, col, step).start()

    @pl.when(jnp.logical_not(is_owner))
    def _():
        right_copy(row % owners, col, 0).start()

    sides[col] = both[:, :channels]
    for target in others:
        sides_copy(col, target).start()

    @pl.when(is_owner)
    def _():
        right_all[row % owners, col] = right_own[...]

    for source in others:
        sides_copy(source, source).wait_recv()
    for index in range(cols):
        left_ref[index * piece : (index + 1) * piece] = sides[index]
    for slot in range(owners):
        for index in range(cols):

            @pl.when(jnp.logical_or(row != col * owners + slot, col != index))
            def _():
                right_copy(slot, index, 1).wait_recv()

            start_row = slot * count + index * piece
            right_ref[start_row : start_row + piece] = right_all[slot, index]

    for chunk in range(2):
        pass_on(row, chunk, True, True, finish)
        for step in range(1, chips - 1):

            @pl.when(chip - step >= 0)
            def _():
                pass_on(row - 2 * step, chunk, step < chips - 2, False, finish)

            @pl.when(chip + step < chips)
            def _():
                pass_on(row + 2 * step, chunk, False, step < chips - 2, finish)

    @pl.when(outer)
    def _():
        for part in range(2):
            pass_on(farthest, part, False, False, finish)
            far_out(part).wait_send()
            share(part, finish)
            share_corner(part, finish)

    rel_copy(slots - 2).wait()
    rel_copy(slots - 1).wait()
    for half in range(2):
        out_copy(half, firsts[half]).wait_send()
        out_copy(2 + half, firsts[half]).wait_send()
        out_copy(4 + half, seconds[half]).wait_send()
    for target in others:
        stat_copy(col, target).wait_send()
        single_copy(col, target).wait_send()
        sides_copy(col, target).wait_send()
        gain_copy(col, target).wait_send()

    for step in range(1, rows):
        right_copy(row % owners, col, step).wait_send()

    @pl.when(jnp.logical_not(is_owner))
    def _():
        right_copy(row % owners, col, 0).wait_send()


def padded(array, axis, size, groups=1):
    width = array.shape[axis] // groups
    if width == size:
        return array
    shape = array.shape
    array = array.reshape(shape[:axis] + (groups, width) + shape[axis + 1 :])
    pads = [(0, 0)] * array.ndim
    pads[axis + 1] = (0, size - width)
    array = jnp.pad(array, pads)
    return array.reshape(shape[:axis] + (groups * size,) + shape[axis + 1 :])


def front_general(
    hidden,
    attn_gain,
    w_query,
    w_key,
    w_value,
    w_out,
    final_gain,
    w_single,
    w_second,
    w_left,
    w_right,
):
    rows = lax.axis_size("row")
    cols = lax.axis_size("col")
    count, model_width = hidden.shape
    width = -(-w_query.shape[1] // 128) * 128
    features = -(-w_single.shape[0] // 128) * 128
    pairs = width // 128
    piece = count // cols
    owners = rows // cols
    single_width = w_second.shape[0]
    channels = w_left.shape[1]
    positions = lax.axis_index("row") * count + jnp.arange(count, dtype=jnp.int32)
    frequency = jnp.exp(
        jnp.arange(HD // 2, dtype=jnp.float32) * (-2.0 * math.log(10000.0) / HD)
    )
    angles = positions.astype(jnp.float32)[:, None] * frequency[None, :]
    cosine = jnp.cos(angles)
    sine = jnp.sin(angles)
    cosine = jnp.concatenate([cosine] * 4, -1)
    sine = jnp.concatenate([-sine, sine, -sine, sine], -1)
    weights = (
        padded(w_query, 1, width),
        padded(w_key, 1, width),
        padded(w_value, 1, width),
        padded(padded(w_out, 0, width), 1, features, cols),
        padded(w_single, 0, features),
        w_second,
    )
    vmem = pl.BlockSpec(memory_space=pltpu.VMEM)
    anywhere = pl.BlockSpec(memory_space=pl.ANY)
    bf16 = jnp.bfloat16
    f32 = jnp.float32
    dma = pltpu.SemaphoreType.DMA
    return pl.pallas_call(
        functools.partial(front_kernel, rows, cols, model_width),
        out_shape=(
            jax.ShapeDtypeStruct((count, channels), bf16),
            jax.ShapeDtypeStruct((owners * count, channels), bf16),
        ),
        in_specs=[vmem, anywhere] + [vmem] * 4 + [anywhere] * 6 + [vmem] * 2,
        out_specs=(vmem, vmem),
        scratch_shapes=[pltpu.VMEM(weight.shape, bf16) for weight in weights]
        + [
            pltpu.VMEM((count, features), bf16),
            pltpu.VMEM((rows, 2, pairs, count, 128), bf16),
            pltpu.VMEM((pairs, 2 * count, 128), bf16),
            pltpu.VMEM((pairs, 2 * count, count), f32),
            pltpu.VMEM((pairs, 2 * count, 128), f32),
            pltpu.VMEM((count, width), bf16),
            pltpu.VMEM((cols, count, features), bf16),
            pltpu.VMEM((cols, count, features), bf16),
            pltpu.VMEM((8, count), f32),
            pltpu.VMEM((cols, 8, count), f32),
            pltpu.VMEM((cols, piece, single_width), f32),
            pltpu.VMEM((cols, piece, single_width), bf16),
            pltpu.VMEM((cols, piece, single_width), bf16),
            pltpu.VMEM((cols, piece, channels), bf16),
            pltpu.VMEM((piece, channels), bf16),
            pltpu.VMEM((owners, cols, piece, channels), bf16),
            dma((7,)),
            dma((3, rows, 2)),
            dma((rows, 2)),
            dma((cols,)),
            dma((cols,)),
            dma((cols,)),
            dma((cols,)),
            dma((cols,)),
            dma((cols,)),
            dma((cols,)),
            dma((cols,)),
            dma((rows,)),
            dma((owners, cols)),
        ],
        compiler_params=pltpu.CompilerParams(
            collective_id=0, has_side_effects=True, vmem_limit_bytes=56 << 20
        ),
    )(
        hidden,
        padded(hidden, 1, features, cols),
        attn_gain,
        cosine,
        sine,
        padded(final_gain, 0, features),
        *weights,
        w_left,
        w_right,
    )


def spelled_kernel(rel_ref, left_ref, right_ref, gain_ref, expand_ref, contract_ref, out_ref):
    block_rows, col_count, channels = rel_ref.shape
    right = right_ref[...].astype(jnp.float32)
    pair_in = jnp.concatenate(
        [
            rel_ref[i].astype(jnp.float32) + (right + left_ref[i : i + 1, :].astype(jnp.float32))
            for i in range(block_rows)
        ],
        0,
    )
    average = jnp.sum(pair_in, -1, keepdims=True) / channels
    variance = jnp.sum(pair_in * pair_in, -1, keepdims=True) / channels - average * average
    normed = ((pair_in - average) * lax.rsqrt(variance + epsilon) * gain_ref[...]).astype(
        jnp.bfloat16
    )
    expanded = jnp.dot(normed, expand_ref[...], preferred_element_type=jnp.float32)
    expanded = jnp.maximum(expanded.astype(jnp.bfloat16), 0)
    update = jnp.dot(expanded, contract_ref[...], preferred_element_type=jnp.float32)
    out_ref[...] = (pair_in + update).astype(out_ref.dtype).reshape(out_ref.shape)


def spelled_stage(rel, left, right, pair_gain, w_expand, w_contract):
    row_count, col_count, channels = rel.shape
    block_rows = math.gcd(row_count, 32)
    whole = lambda array: pl.BlockSpec(array.shape, lambda i: (0, 0))
    gain = pair_gain.reshape(1, channels)
    tile = pl.BlockSpec((block_rows, col_count, channels), lambda i: (i, 0, 0))
    return pl.pallas_call(
        spelled_kernel,
        grid=(row_count // block_rows,),
        in_specs=[
            tile,
            pl.BlockSpec((block_rows, channels), lambda i: (i, 0)),
            whole(right),
            whole(gain),
            whole(w_expand),
            whole(w_contract),
        ],
        out_specs=tile,
        out_shape=jax.ShapeDtypeStruct(rel.shape, jnp.bfloat16),
        compiler_params=pltpu.CompilerParams(
            dimension_semantics=("arbitrary",), vmem_limit_bytes=56 << 20
        ),
    )(rel, left, right, gain, w_expand, w_contract)


def front_plane(
    hidden,
    attn_gain,
    w_query,
    w_key,
    w_value,
    w_out,
    final_gain,
    w_single,
    w_second,
    w_left,
    w_right,
    rel_bins,
    rel_table,
):
    rows = lax.axis_size("row")
    cols = lax.axis_size("col")
    count, model_width = hidden.shape
    width = -(-w_query.shape[1] // 128) * 128
    features = -(-w_single.shape[0] // 128) * 128
    pairs = width // 128
    piece = count // cols
    owners = rows // cols
    single_width = w_second.shape[0]
    channels = w_left.shape[1]
    frequency = np.exp(np.arange(HD // 2) * (-2.0 * math.log(10000.0) / HD))
    frequency = np.concatenate([frequency] * 4)[None, :]
    offsets = np.arange(count)[:, None] * frequency
    steps = (np.arange(rows) * count)[:, None] * frequency
    angles = [
        jnp.asarray(turn(angle), jnp.float32)
        for angle in (offsets, steps)
        for turn in (np.cos, np.sin)
    ]
    weights = (w_query, w_key, w_value, w_out, w_single, w_second)
    vmem = pl.BlockSpec(memory_space=pltpu.VMEM)
    anywhere = pl.BlockSpec(memory_space=pl.ANY)
    bf16 = jnp.bfloat16
    f32 = jnp.float32
    dma = pltpu.SemaphoreType.DMA
    return pl.pallas_call(
        functools.partial(plane_kernel, rows, cols, model_width),
        out_shape=(
            jax.ShapeDtypeStruct((count, channels), bf16),
            jax.ShapeDtypeStruct((owners * count, channels), bf16),
            jax.ShapeDtypeStruct(rel_bins.shape + (channels,), bf16),
        ),
        in_specs=[vmem, anywhere] + [vmem] * 6 + [anywhere] * 6 + [vmem] * 4,
        out_specs=(vmem, vmem, anywhere),
        scratch_shapes=[pltpu.VMEM(weight.shape, bf16) for weight in weights]
        + [
            pltpu.VMEM((count, features), bf16),
            pltpu.VMEM((2, piece // 2, model_width), bf16),
            pltpu.VMEM((cols, 2, piece // 2, model_width), bf16),
            pltpu.VMEM((rows, 2, pairs, count, 128), bf16),
            pltpu.VMEM((pairs, 2 * count, 128), bf16),
            pltpu.VMEM((pairs, 2 * count, count), f32),
            pltpu.VMEM((2, pairs, 2 * count, 2 * count), bf16),
            pltpu.VMEM((pairs, 2 * count, 128), f32),
            pltpu.VMEM((single_width, 2 * channels), bf16),
            pltpu.VMEM((count, width), bf16),
            pltpu.VMEM((6, count // 2, features), bf16),
            pltpu.VMEM((6, count // 2, features), bf16),
            pltpu.VMEM((cols, piece, 128), f32),
            pltpu.VMEM((cols, piece, 128), f32),
            pltpu.VMEM((cols, 8, single_width), f32),
            pltpu.VMEM((cols, piece, single_width), f32),
            pltpu.VMEM((cols, piece, single_width), bf16),
            pltpu.VMEM((cols, piece, single_width), bf16),
            pltpu.VMEM((cols, piece, channels), bf16),
            pltpu.VMEM((piece, channels), bf16),
            pltpu.VMEM((owners, cols, piece, channels), bf16),
            pltpu.VMEM((-(-rel_table.shape[0] // 16) * 16, channels), bf16),
            pltpu.VMEM((2, rel_bins.shape[0] // 8, rel_bins.shape[1], channels), bf16),
            dma((7,)),
            dma((2,)),
            dma((3, 2)),
            dma((cols, 2)),
            dma((3, rows, 2)),
            dma((rows, 2)),
            dma((6,)),
            dma((6,)),
            dma((cols,)),
            dma((cols,)),
            dma((cols,)),
            dma((cols,)),
            dma((cols,)),
            dma((cols,)),
            dma((rows,)),
            dma((owners, cols)),
            dma((cols,)),
            dma((cols,)),
            dma((2,)),
        ],
        compiler_params=pltpu.CompilerParams(
            collective_id=0, has_side_effects=True, vmem_limit_bytes=56 << 20
        ),
    )(
        hidden,
        hidden,
        attn_gain,
        *angles,
        final_gain,
        *weights,
        w_left,
        w_right,
        rel_bins,
        rel_table,
    )


def local(
    hidden,
    rel_bins,
    attn_gain,
    w_query,
    w_key,
    w_value,
    w_out,
    final_gain,
    w_single,
    w_second,
    w_left,
    w_right,
    rel_table,
    pair_gain,
    w_expand,
    w_contract,
):
    rows = lax.axis_size("row")
    cols = lax.axis_size("col")
    aligned = w_query.shape[1] % 128 == 0 and hidden.shape[0] % (32 * cols) == 0
    operands = (
        hidden,
        attn_gain,
        w_query,
        w_key,
        w_value,
        w_out,
        final_gain,
        w_single,
        w_second,
        w_left,
        w_right,
    )
    if rows == 2 * cols and cols == 4 and aligned:
        left, right, rel = front_plane(*operands, rel_bins, rel_table)
        return spelled_stage(rel, left, right, pair_gain, w_expand, w_contract)
    left, right = front_general(*operands)
    return pair_stage(rel_bins, left, right, rel_table, pair_gain, w_expand, w_contract)


def solution(mesh):
    in_specs = (
        P("row", None),
        P("row", "col"),
        P(),
        P(None, "col"),
        P(None, "col"),
        P(None, "col"),
        P("col", None),
        P("col"),
        P("col", None),
        P(),
        P(),
        P(),
        P(),
        P(),
        P(),
        P(),
    )
    out_specs = P("row", "col", None)
    return jax.shard_map(local, mesh=mesh, in_specs=in_specs, out_specs=out_specs, check_vma=False)
```

```python
import functools
import math

import jax
import jax.numpy as jnp
import numpy as np
from jax import lax
from jax.experimental import pallas as pl
from jax.experimental.pallas import tpu as pltpu
from jax.sharding import PartitionSpec as P

HD = 64
SUB = 8
CHUNKS = 8
WINDOW = 3
MESH = pl.DeviceIdType.MESH


epsilon = 1e-05


def pair_kernel(bins_ref, left_ref, right_ref, table_ref, gain_ref, expand_ref, contract_ref, out_ref, table):
    block_rows, col_count = bins_ref.shape
    channels = right_ref.shape[1]
    right = right_ref[...].astype(jnp.float32)
    bins = table_ref.shape[0]

    @pl.when(pl.program_id(0) == 0)
    def _():
        table[...] = jnp.zeros_like(table)
        table[:bins] = table_ref[...]

    codes = lax.broadcasted_iota(jnp.int32, (table.shape[0], col_count), 0)
    hot = jnp.concatenate(
        [
            jnp.where(bins_ref[i : i + 1, :] == codes, 1.0, 0.0).astype(jnp.bfloat16)
            for i in range(block_rows)
        ],
        1,
    )
    part = lax.dot_general(
        hot, table[...], (((0,), (0,)), ((), ())), preferred_element_type=jnp.float32
    )
    pair_in = jnp.concatenate(
        [
            part[i * col_count : (i + 1) * col_count]
            + (right + left_ref[i : i + 1, :].astype(jnp.float32))
            for i in range(block_rows)
        ],
        0,
    )
    average = jnp.sum(pair_in, -1, keepdims=True) / channels
    variance = jnp.sum(pair_in * pair_in, -1, keepdims=True) / channels - average * average
    normed = ((pair_in - average) * lax.rsqrt(variance + epsilon) * gain_ref[...]).astype(
        jnp.bfloat16
    )
    expanded = jnp.dot(normed, expand_ref[...], preferred_element_type=jnp.float32)
    expanded = jnp.maximum(expanded.astype(jnp.bfloat16), 0)
    update = jnp.dot(expanded, contract_ref[...], preferred_element_type=jnp.float32)
    out_ref[...] = (pair_in + update).astype(out_ref.dtype).reshape(out_ref.shape)


def pair_stage(rel_bins, left, right, rel_table, pair_gain, w_expand, w_contract):
    row_count, col_count = rel_bins.shape
    channels = right.shape[1]
    block_rows = math.gcd(row_count, 32)
    bins_padded = -(-rel_table.shape[0] // 128) * 128
    whole = lambda array: pl.BlockSpec(array.shape, lambda i: (0, 0))
    gain = pair_gain.reshape(1, channels)
    return pl.pallas_call(
        pair_kernel,
        grid=(row_count // block_rows,),
        in_specs=[
            pl.BlockSpec((block_rows, col_count), lambda i: (i, 0)),
            pl.BlockSpec((block_rows, channels), lambda i: (i, 0)),
            whole(right),
            whole(rel_table),
            whole(gain),
            whole(w_expand),
            whole(w_contract),
        ],
        out_specs=pl.BlockSpec((block_rows, col_count, channels), lambda i: (i, 0, 0)),
        out_shape=jax.ShapeDtypeStruct((row_count, col_count, channels), jnp.bfloat16),
        scratch_shapes=[pltpu.VMEM((bins_padded, channels), jnp.bfloat16)],
        compiler_params=pltpu.CompilerParams(
            dimension_semantics=("arbitrary",), vmem_limit_bytes=56 << 20
        ),
    )(rel_bins, left, right, rel_table, gain, w_expand, w_contract)


def front_kernel(
    rows,
    cols,
    model_width,
    hidden_ref,
    own_hbm,
    attn_gain_ref,
    cos_ref,
    sin_ref,
    final_gain_ref,
    w_query_hbm,
    w_key_hbm,
    w_value_hbm,
    w_out_hbm,
    w_single_hbm,
    w_second_hbm,
    w_left_ref,
    w_right_ref,
    left_ref,
    right_ref,
    w_query,
    w_key,
    w_value,
    w_out,
    w_single,
    w_second,
    own,
    kv,
    query,
    totals,
    numerator,
    context,
    out_send,
    out_recv,
    stat_send,
    stat_recv,
    single_own,
    single_send,
    single_recv,
    sides,
    right_own,
    right_all,
    weight_sem,
    kv_send_sem,
    kv_recv_sem,
    out_send_sem,
    out_recv_sem,
    stat_send_sem,
    stat_recv_sem,
    single_send_sem,
    single_recv_sem,
    sides_send_sem,
    sides_recv_sem,
    right_send_sem,
    right_recv_sem,
):
    row = lax.axis_index("row")
    col = lax.axis_index("col")
    count = hidden_ref.shape[0]
    pairs = query.shape[0]
    features = w_single.shape[0]
    piece = single_own.shape[1]
    owners = rows // cols
    chips = rows // 2
    chip = row // 2
    core = row % 2
    partner = row + 1 - 2 * core

    own_columns = pl.ds(pl.multiple_of(col * features, 128), features)
    loads = []
    for index, (source, target) in enumerate(
        (
            (w_key_hbm, w_key),
            (w_value_hbm, w_value),
            (w_query_hbm, w_query),
            (w_out_hbm, w_out),
            (w_single_hbm, w_single),
            (w_second_hbm, w_second),
            (own_hbm.at[:, own_columns], own),
        )
    ):
        load = pltpu.make_async_copy(source, target, weight_sem.at[index])
        load.start()
        loads.append(load)

    barrier = pltpu.get_barrier_semaphore()
    is_owner = row // owners == col

    def greet(target_row, target_col):
        pl.semaphore_signal(
            barrier, inc=1, device_id=(target_row, target_col), device_id_type=MESH
        )

    greet(partner, col)

    @pl.when(chip + 1 < chips)
    def _():
        greet(row + 2, col)

    @pl.when(chip >= 1)
    def _():
        greet(row - 2, col)

    for slot in range(owners):
        for index in range(cols):

            @pl.when(jnp.logical_or(row != col * owners + slot, col != index))
            def _():
                greet(col * owners + slot, index)

    greetings = cols + rows
    greetings += jnp.where(chip + 1 < chips, 1, 0) + jnp.where(chip >= 1, 1, 0)
    greetings -= jnp.where(is_owner, 1, 0)
    for step in range(1, cols):
        pl.semaphore_signal(
            barrier, inc=1, device_id=(row, (col + step) % cols), device_id_type=MESH
        )

    stream = hidden_ref[...].astype(jnp.float32)
    average = jnp.sum(stream, -1, keepdims=True) / model_width
    variance = jnp.sum(stream * stream, -1, keepdims=True) / model_width - average * average
    attn_in = (
        (stream - average) * lax.rsqrt(variance + epsilon) * attn_gain_ref[...].reshape(1, -1)
    ).astype(jnp.bfloat16)
    cosine = cos_ref[...]
    sine = sin_ref[...]
    lane = lax.broadcasted_iota(jnp.int32, (count, 128), 1)
    first_half = lane % HD < HD // 2
    first_head = lane < HD

    def rope(vectors):
        turned = jnp.where(
            first_half,
            pltpu.roll(vectors, 128 - HD // 2, 1),
            pltpu.roll(vectors, HD // 2, 1),
        )
        return vectors * cosine + turned * sine

    def kv_copy(source, chunk, way, target):
        return pltpu.make_async_remote_copy(
            src_ref=kv.at[source, chunk],
            dst_ref=kv.at[source, chunk],
            send_sem=kv_send_sem.at[way, source, chunk],
            recv_sem=kv_recv_sem.at[source, chunk],
            device_id=(target, col),
            device_id_type=MESH,
        )

    def pass_on(source, chunk, right, left, act):
        if right:

            @pl.when(chip + 1 < chips)
            def _():
                act(kv_copy(source, chunk, 0, row + 2))

        if left:

            @pl.when(chip >= 1)
            def _():
                act(kv_copy(source, chunk, 1, row - 2))

        act(kv_copy(source, chunk, 2, partner))

    def start(copy):
        copy.start()

    def finish(copy):
        copy.wait_send()

    loads[0].wait()
    projected = jnp.dot(attn_in, w_key[...], preferred_element_type=jnp.float32)
    for pair in range(pairs):
        kv[row, 0, pair] = rope(projected[:, pair * 128 : pair * 128 + 128]).astype(jnp.bfloat16)
    pl.semaphore_wait(barrier, greetings)
    pass_on(row, 0, True, True, start)
    loads[1].wait()
    projected = jnp.dot(attn_in, w_value[...], preferred_element_type=jnp.float32)
    for pair in range(pairs):
        kv[row, 1, pair] = projected[:, pair * 128 : pair * 128 + 128].astype(jnp.bfloat16)
    pass_on(row, 1, True, True, start)
    loads[2].wait()
    projected = jnp.dot(attn_in, w_query[...], preferred_element_type=jnp.float32) * HD ** (-0.5)
    for pair in range(pairs):
        turned = rope(projected[:, pair * 128 : pair * 128 + 128])
        query[pair, :count] = jnp.where(first_head, turned, 0.0).astype(jnp.bfloat16)
        query[pair, count:] = jnp.where(first_head, 0.0, turned).astype(jnp.bfloat16)
    totals[...] = jnp.zeros_like(totals)
    numerator[...] = jnp.zeros_like(numerator)

    def attend(source):
        for pair in range(pairs):
            scores = lax.dot_general(
                query[pair],
                kv[source, 0, pair],
                (((1,), (1,)), ((), ())),
                preferred_element_type=jnp.float32,
            )
            weights = jnp.exp(scores)
            totals[pair] += weights
            numerator[pair] += jnp.dot(
                weights.astype(jnp.bfloat16),
                kv[source, 1, pair],
                preferred_element_type=jnp.float32,
            )

    def arrive(source):
        for chunk in range(2):
            kv_copy(source, chunk, 2, partner).wait_recv()

    attend(row)
    arrive(partner)
    attend(partner)

    @pl.loop(1, chips)
    def _(step):
        from_left = chip - step >= 0
        from_right = chip + step < chips
        for chunk in range(2):

            @pl.when(from_left)
            def _():
                source = row - 2 * step
                kv_copy(source, chunk, 2, partner).wait_recv()
                pass_on(source, chunk, True, False, start)

            @pl.when(from_right)
            def _():
                source = row + 2 * step
                kv_copy(source, chunk, 2, partner).wait_recv()
                pass_on(source, chunk, False, True, start)

        @pl.when(from_left)
        def _():
            attend(row - 2 * step)
            arrive(partner - 2 * step)
            attend(partner - 2 * step)

        @pl.when(from_right)
        def _():
            attend(row + 2 * step)
            arrive(partner + 2 * step)
            attend(partner + 2 * step)

    for pair in range(pairs):
        shares = numerator[pair] / jnp.sum(totals[pair], -1, keepdims=True)
        context[:, pair * 128 : pair * 128 + 128] = jnp.where(
            first_head, shares[:count], shares[count:]
        ).astype(jnp.bfloat16)

    def out_copy(source, target):
        return pltpu.make_async_remote_copy(
            src_ref=out_send.at[target],
            dst_ref=out_recv.at[source],
            send_sem=out_send_sem.at[target],
            recv_sem=out_recv_sem.at[source],
            device_id=(row, target),
            device_id_type=MESH,
        )

    def out_part(target):
        columns = pl.ds(pl.multiple_of(target * features, 128), features)
        return jnp.dot(context[...], w_out[:, columns], preferred_element_type=jnp.float32)

    others = [(col + step) % cols for step in range(1, cols)]
    loads[3].wait()
    for target in others:
        out_send[target] = out_part(target).astype(jnp.bfloat16)
        out_copy(col, target).start()
    loads[6].wait()
    resid = own[...].astype(jnp.float32) + out_part(col)
    for source in others:
        out_copy(source, source).wait_recv()
        resid += out_recv[source].astype(jnp.float32)

    def stat_copy(source, target):
        return pltpu.make_async_remote_copy(
            src_ref=stat_send,
            dst_ref=stat_recv.at[source],
            send_sem=stat_send_sem.at[target],
            recv_sem=stat_recv_sem.at[source],
            device_id=(row, target),
            device_id_type=MESH,
        )

    sum_first = jnp.sum(resid, -1, keepdims=True)
    sum_second = jnp.sum(resid * resid, -1, keepdims=True)
    sums = jnp.transpose(jnp.where(lane < 4, sum_first, sum_second))[:8]
    stat_send[...] = sums
    for target in others:
        stat_copy(col, target).start()
    for source in others:
        stat_copy(source, source).wait_recv()
        sums += stat_recv[source]
    sums = jnp.transpose(jnp.concatenate([sums] * 16, 0))
    average = sums[:, 0:1] / model_width
    variance = sums[:, 4:5] / model_width - average * average
    final = (
        (resid - average) * lax.rsqrt(variance + epsilon) * final_gain_ref[...].reshape(1, -1)
    ).astype(jnp.bfloat16)

    def single_copy(source, target):
        return pltpu.make_async_remote_copy(
            src_ref=single_send.at[target],
            dst_ref=single_recv.at[source],
            send_sem=single_send_sem.at[target],
            recv_sem=single_recv_sem.at[source],
            device_id=(row, target),
            device_id_type=MESH,
        )

    loads[4].wait()
    part = jnp.dot(final, w_single[...], preferred_element_type=jnp.float32)
    for index in range(cols):
        block = part[index * piece : (index + 1) * piece]
        single_own[index] = block
        single_send[index] = block.astype(jnp.bfloat16)
    for target in others:
        single_copy(col, target).start()
    summed = single_own[col]
    for source in others:
        single_copy(source, source).wait_recv()
        summed += single_recv[source].astype(jnp.float32)
    lifted = jnp.maximum(summed, 0.0).astype(jnp.bfloat16)
    loads[5].wait()
    single = jnp.dot(lifted, w_second[...], preferred_element_type=jnp.float32)
    single = single.astype(jnp.bfloat16)

    def sides_copy(source, target):
        return pltpu.make_async_remote_copy(
            src_ref=sides.at[source],
            dst_ref=sides.at[source],
            send_sem=sides_send_sem.at[target],
            recv_sem=sides_recv_sem.at[source],
            device_id=(row, target),
            device_id_type=MESH,
        )

    def right_copy(slot, index, step):
        return pltpu.make_async_remote_copy(
            src_ref=right_own,
            dst_ref=right_all.at[slot, index],
            send_sem=right_send_sem.at[step],
            recv_sem=right_recv_sem.at[slot, index],
            device_id=((row + step) % rows, row // owners),
            device_id_type=MESH,
        )

    right_own[...] = jnp.dot(
        single, w_right_ref[...], preferred_element_type=jnp.float32
    ).astype(jnp.bfloat16)
    for step in range(1, rows):
        right_copy(row % owners, col, step).start()

    @pl.when(jnp.logical_not(is_owner))
    def _():
        right_copy(row % owners, col, 0).start()

    sides[col] = jnp.dot(single, w_left_ref[...], preferred_element_type=jnp.float32).astype(
        jnp.bfloat16
    )
    for target in others:
        sides_copy(col, target).start()

    @pl.when(is_owner)
    def _():
        right_all[row % owners, col] = right_own[...]

    for source in others:
        sides_copy(source, source).wait_recv()
    for index in range(cols):
        left_ref[index * piece : (index + 1) * piece] = sides[index]
    for slot in range(owners):
        for index in range(cols):

            @pl.when(jnp.logical_or(row != col * owners + slot, col != index))
            def _():
                right_copy(slot, index, 1).wait_recv()

            start_row = slot * count + index * piece
            right_ref[start_row : start_row + piece] = right_all[slot, index]

    for chunk in range(2):
        pass_on(row, chunk, True, True, finish)

    @pl.loop(1, chips)
    def _(step):
        for chunk in range(2):

            @pl.when(chip - step >= 0)
            def _():
                pass_on(row - 2 * step, chunk, True, False, finish)

            @pl.when(chip + step < chips)
            def _():
                pass_on(row + 2 * step, chunk, False, True, finish)

    for target in others:
        out_copy(col, target).wait_send()
        stat_copy(col, target).wait_send()
        single_copy(col, target).wait_send()
        sides_copy(col, target).wait_send()

    for step in range(1, rows):
        right_copy(row % owners, col, step).wait_send()

    @pl.when(jnp.logical_not(is_owner))
    def _():
        right_copy(row % owners, col, 0).wait_send()


def plane_kernel(
    rows,
    cols,
    model_width,
    hidden_ref,
    own_hbm,
    attn_gain_ref,
    cos_ref,
    sin_ref,
    cos_step_ref,
    sin_step_ref,
    final_gain_ref,
    w_query_hbm,
    w_key_hbm,
    w_value_hbm,
    w_out_hbm,
    w_single_hbm,
    w_second_hbm,
    w_left_ref,
    w_right_ref,
    bins_ref,
    table_ref,
    left_ref,
    right_ref,
    rel_hbm,
    flags_ref,
    w_query,
    w_key,
    w_value,
    w_out,
    w_single,
    w_second,
    own,
    piece_send,
    far,
    kv,
    query,
    totals,
    shares,
    numerator,
    w_sides,
    context,
    out_send,
    out_recv,
    stat_send,
    stat_recv,
    gain_sums,
    single_own,
    single_send,
    single_recv,
    sides,
    right_own,
    right_all,
    table,
    rel_slots,
    weight_sem,
    far_out_sem,
    far_send_sem,
    far_recv_sem,
    kv_send_sem,
    kv_recv_sem,
    out_send_sem,
    out_recv_sem,
    stat_send_sem,
    stat_recv_sem,
    single_send_sem,
    single_recv_sem,
    sides_send_sem,
    sides_recv_sem,
    right_send_sem,
    right_recv_sem,
    gain_send_sem,
    gain_recv_sem,
    rel_sem,
):
    row = lax.axis_index("row")
    col = lax.axis_index("col")
    count = hidden_ref.shape[0]
    pairs = query.shape[0]
    features = w_single.shape[0]
    piece = single_own.shape[1]
    owners = rows // cols
    chips = rows // 2
    chip = row // 2
    core = row % 2
    partner = row + 1 - 2 * core
    outer = jnp.logical_or(chip == 0, chip == chips - 1)
    farthest = (chips - 1 - chip) * 2 + core
    side = col + 1 - 2 * (col % 2)
    across = (col + 2) % cols
    corner = cols - 1 - col

    own_columns = pl.ds(pl.multiple_of(col * features, 128), features)
    loads = []
    for index, (source, target) in enumerate(
        (
            (w_key_hbm, w_key),
            (w_value_hbm, w_value),
            (w_query_hbm, w_query),
            (w_out_hbm, w_out),
            (w_single_hbm, w_single),
            (w_second_hbm, w_second),
            (own_hbm.at[:, own_columns], own),
        )
    ):
        load = pltpu.make_async_copy(source, target, weight_sem.at[index])
        load.start()
        loads.append(load)

    barrier = pltpu.get_barrier_semaphore()
    is_owner = row // owners == col

    def greet(target_row, target_col):
        pl.semaphore_signal(
            barrier, inc=1, device_id=(target_row, target_col), device_id_type=MESH
        )

    greet(partner, col)

    @pl.when(chip + 1 < chips)
    def _():
        greet(row + 2, col)

    @pl.when(chip >= 1)
    def _():
        greet(row - 2, col)

    @pl.when(outer)
    def _():
        greet(farthest, col)

    greetings = cols + jnp.where(outer, 1, 0)
    greetings += jnp.where(chip + 1 < chips, 1, 0) + jnp.where(chip >= 1, 1, 0)
    for step in range(1, cols):
        pl.semaphore_signal(
            barrier, inc=1, device_id=(row, (col + step) % cols), device_id_type=MESH
        )

    def normalize(values):
        stream = values.astype(jnp.float32)
        average = jnp.sum(stream, -1, keepdims=True) / model_width
        variance = jnp.sum(stream * stream, -1, keepdims=True) / model_width - average * average
        return (
            (stream - average) * lax.rsqrt(variance + epsilon) * attn_gain_ref[...].reshape(1, -1)
        ).astype(jnp.bfloat16)

    half = piece // 2

    @pl.when(outer)
    def _():
        for part in range(2):
            first = pl.multiple_of(col * piece + part * half, half)
            piece_send[part] = normalize(hidden_ref[pl.ds(first, half)])

    lane = lax.broadcasted_iota(jnp.int32, (count, 128), 1)
    first_half = lane % HD < HD // 2
    first_head = lane < HD

    def tables(source):
        cosine = cos_ref[...]
        sine = sin_ref[...]
        cos_step = cos_step_ref[pl.ds(source, 1), :]
        sin_step = sin_step_ref[pl.ds(source, 1), :]
        turned = sine * cos_step + cosine * sin_step
        return cosine * cos_step - sine * sin_step, jnp.where(first_half, -turned, turned)

    def rope(vectors, cosine, sine):
        turned = jnp.where(
            first_half,
            pltpu.roll(vectors, 128 - HD // 2, 1),
            pltpu.roll(vectors, HD // 2, 1),
        )
        return vectors * cosine + turned * sine

    def far_copy(owner, part, way, target):
        return pltpu.make_async_remote_copy(
            src_ref=far.at[owner, part],
            dst_ref=far.at[owner, part],
            send_sem=far_send_sem.at[way, part],
            recv_sem=far_recv_sem.at[owner, part],
            device_id=(row, target),
            device_id_type=MESH,
        )

    def far_out(part):
        return pltpu.make_async_remote_copy(
            src_ref=piece_send.at[part],
            dst_ref=far.at[col, part],
            send_sem=far_out_sem.at[part],
            recv_sem=far_recv_sem.at[col, part],
            device_id=(farthest, col),
            device_id_type=MESH,
        )

    def share(part, act):
        act(far_copy(col, part, 0, side))
        act(far_copy(col, part, 1, across))

    def share_corner(part, act):
        if part == 0:
            act(far_copy(side, part, 2, across))
        else:
            act(far_copy(across, part, 2, side))

    def far_wait(owner, part):
        far_copy(owner, part, 0, side).wait_recv()

    def kv_copy(source, chunk, way, target):
        return pltpu.make_async_remote_copy(
            src_ref=kv.at[source, chunk],
            dst_ref=kv.at[source, chunk],
            send_sem=kv_send_sem.at[way, source, chunk],
            recv_sem=kv_recv_sem.at[source, chunk],
            device_id=(target, col),
            device_id_type=MESH,
        )

    def pass_on(source, chunk, right, left, act):
        if right:

            @pl.when(chip + 1 < chips)
            def _():
                act(kv_copy(source, chunk, 0, row + 2))

        if left:

            @pl.when(chip >= 1)
            def _():
                act(kv_copy(source, chunk, 1, row - 2))

        act(kv_copy(source, chunk, 2, partner))

    def start(copy):
        copy.start()

    def finish(copy):
        copy.wait_send()

    def keys_of(rows_in, source):
        cosine, sine = tables(source)
        projected = jnp.dot(rows_in, w_key[...], preferred_element_type=jnp.float32)
        for pair in range(pairs):
            kv[source, 0, pair] = rope(
                projected[:, pair * 128 : pair * 128 + 128], cosine, sine
            ).astype(jnp.bfloat16)

    def values_of(rows_in, source):
        projected = jnp.dot(rows_in, w_value[...], preferred_element_type=jnp.float32)
        for pair in range(pairs):
            kv[source, 1, pair] = projected[:, pair * 128 : pair * 128 + 128].astype(jnp.bfloat16)

    pl.semaphore_wait(barrier, greetings)

    @pl.when(outer)
    def _():
        for part in range(2):
            far_out(part).start()

    attn_in = normalize(hidden_ref[...])
    loads[0].wait()
    keys_of(attn_in, row)
    pass_on(row, 0, True, True, start)
    loads[1].wait()
    values_of(attn_in, row)
    pass_on(row, 1, True, True, start)

    def gain_copy(source, target):
        return pltpu.make_async_remote_copy(
            src_ref=gain_sums.at[source],
            dst_ref=gain_sums.at[source],
            send_sem=gain_send_sem.at[target],
            recv_sem=gain_recv_sem.at[source],
            device_id=(row, target),
            device_id_type=MESH,
        )

    others = [corner, side, across]
    loads[2].wait()
    cosine, sine = tables(row)
    projected = jnp.dot(attn_in, w_query[...], preferred_element_type=jnp.float32) * HD ** (-0.5)
    for pair in range(pairs):
        turned = rope(projected[:, pair * 128 : pair * 128 + 128], cosine, sine)
        query[pair, :count] = jnp.where(first_head, turned, 0.0).astype(jnp.bfloat16)
        query[pair, count:] = jnp.where(first_head, 0.0, turned).astype(jnp.bfloat16)
    bins = table_ref.shape[0]
    table[...] = jnp.zeros_like(table)
    table[:bins] = table_ref[...]
    slot_rows = rel_slots.shape[1]
    col_count = bins_ref.shape[1]
    slots = bins_ref.shape[0] // slot_rows

    def rel_copy(index):
        return pltpu.make_async_copy(
            rel_slots.at[index % 2],
            rel_hbm.at[pl.ds(pl.multiple_of(index * slot_rows, slot_rows), slot_rows)],
            rel_sem.at[index % 2],
        )

    def spell(begin, end):
        @pl.loop(begin, end)
        def _(index):
            @pl.when(index >= 2)
            def _():
                rel_copy(index - 2).wait()

            picked = bins_ref[pl.ds(pl.multiple_of(index * slot_rows, slot_rows), slot_rows)]
            codes = lax.broadcasted_iota(jnp.int32, (table.shape[0], col_count), 0)
            hot = jnp.concatenate(
                [
                    jnp.where(picked[i : i + 1, :] == codes, 1.0, 0.0).astype(jnp.bfloat16)
                    for i in range(slot_rows)
                ],
                1,
            )
            chosen = lax.dot_general(
                hot, table[...], (((0,), (0,)), ((), ())), preferred_element_type=jnp.float32
            )
            rel_slots[index % 2] = chosen.astype(jnp.bfloat16).reshape(rel_slots.shape[1:])
            rel_copy(index).start()

    totals[...] = jnp.zeros_like(totals)
    numerator[...] = jnp.zeros_like(numerator)

    def score(source, slot):
        for pair in range(pairs):
            keys = kv[pl.ds(2 * source, 2), 0, pair].reshape(2 * count, 128)
            weights = jnp.exp(
                lax.dot_general(
                    query[pair],
                    keys,
                    (((1,), (1,)), ((), ())),
                    preferred_element_type=jnp.float32,
                )
            )
            totals[pair] += weights[:, :count] + weights[:, count:]
            shares[slot, pair] = weights.astype(jnp.bfloat16)

    def mix(source, slot):
        for pair in range(pairs):
            values = kv[pl.ds(2 * source, 2), 1, pair].reshape(2 * count, 128)
            numerator[pair] += jnp.dot(
                shares[slot, pair], values, preferred_element_type=jnp.float32
            )

    def arrive(source, chunk):
        kv_copy(source, chunk, 2, partner).wait_recv()

    arrive(partner, 0)
    score(chip, 0)
    loads[4].wait()
    gain = final_gain_ref[...].reshape(1, -1)
    coarse = gain.astype(jnp.bfloat16)
    fine = (gain - coarse.astype(jnp.float32)).astype(jnp.bfloat16)
    gains = jnp.concatenate([jnp.broadcast_to(part, (16, features)) for part in (coarse, fine)], 0)
    gained = jnp.dot(gains, w_single[...], preferred_element_type=jnp.float32)
    gain_sums[col] = gained[:8] + gained[16:24]
    for target in others:
        gain_copy(col, target).start()

    arrive(partner, 1)
    mix(chip, 0)

    grouped = bins_ref[...].reshape(flags_ref.shape[0], -1, col_count)
    high = jnp.max(grouped, 1)
    low = jnp.min(grouped, 1)
    spot = lax.broadcasted_iota(jnp.int32, flags_ref.shape, 1)
    flags = jnp.full(flags_ref.shape, -1, jnp.int32)
    width = col_count // CHUNKS
    for index in range(CHUNKS):
        span = slice(index * width, (index + 1) * width)
        top = jnp.max(high[:, span], -1, keepdims=True)
        bottom = jnp.min(low[:, span], -1, keepdims=True)
        flags = jnp.where(spot == index, jnp.where(top == bottom, top, -1), flags)
    flags_ref[...] = flags
    early = jnp.where(outer, slots, 4)
    spell(0, 2)

    @pl.when(outer)
    def _():
        for part in range(2):
            far_wait(col, part)
            share(part, start)

    spell(2, early)

    @pl.when(outer)
    def _():
        far_wait(side, 0)
        share_corner(0, start)
        far_wait(across, 1)
        share_corner(1, start)


    def near(step, onward):
        from_left = chip - step >= 0
        from_right = chip + step < chips

        def receive(chunk):
            @pl.when(from_left)
            def _():
                arrive(row - 2 * step, chunk)
                pass_on(row - 2 * step, chunk, onward, False, start)

            @pl.when(from_right)
            def _():
                arrive(row + 2 * step, chunk)
                pass_on(row + 2 * step, chunk, False, onward, start)

        def use(chunk):
            @pl.when(from_left)
            def _():
                arrive(partner - 2 * step, chunk)
                (mix if chunk else score)(chip - step, 0)

            @pl.when(from_right)
            def _():
                arrive(partner + 2 * step, chunk)
                (mix if chunk else score)(chip + step, 1)

        receive(0)
        if onward:
            receive(1)
        use(0)
        if not onward:
            receive(1)
        use(1)

    for step in range(1, chips - 1):
        near(step, step < chips - 2)
        if step == 1:
            loads[5].wait()
            w_sides[...] = jnp.dot(
                w_second[...],
                jnp.concatenate([w_left_ref[...], w_right_ref[...]], 1),
                preferred_element_type=jnp.float32,
            ).astype(jnp.bfloat16)
            spell(early, slots)

            @pl.when(outer)
            def _():
                far_wait(side, 1)
                far_wait(across, 0)
                for part in range(2):
                    far_wait(corner, part)
                rows_in = far[...].reshape(count, model_width)
                keys_of(rows_in, farthest)
                pass_on(farthest, 0, False, False, start)
                values_of(rows_in, farthest)
                pass_on(farthest, 1, False, False, start)
                for chunk in range(2):
                    arrive(farthest + partner - row, chunk)
                    (mix if chunk else score)(chips - 1 - chip, 0)


    for pair in range(pairs):
        mixed = numerator[pair] / jnp.sum(totals[pair], -1, keepdims=True)
        context[:, pair * 128 : pair * 128 + 128] = jnp.where(
            first_head, mixed[:count], mixed[count:]
        ).astype(jnp.bfloat16)

    split = count // 2
    halves = [slice(0, split), slice(split, count)]
    firsts = (side, across)
    seconds = (across, side)

    def out_copy(slot, target):
        return pltpu.make_async_remote_copy(
            src_ref=out_send.at[slot],
            dst_ref=out_recv.at[slot],
            send_sem=out_send_sem.at[slot],
            recv_sem=out_recv_sem.at[slot],
            device_id=(row, target),
            device_id_type=MESH,
        )

    def out_part(target):
        columns = pl.ds(pl.multiple_of(target * features, 128), features)
        return jnp.dot(context[...], w_out[:, columns], preferred_element_type=jnp.float32)

    loads[3].wait()
    passing = out_part(corner).astype(jnp.bfloat16)
    for half in range(2):
        out_send[half] = passing[halves[half]]
        out_copy(half, firsts[half]).start()
    kept = [None, None]
    for half in range(2):
        passing = out_part(firsts[half])
        out_send[2 + half] = passing[halves[half]].astype(jnp.bfloat16)
        out_copy(2 + half, firsts[half]).start()
        kept[1 - half] = passing[halves[1 - half]]
    for half in range(2):
        out_copy(half, firsts[half]).wait_recv()
        out_send[4 + half] = (kept[half] + out_recv[half].astype(jnp.float32)).astype(jnp.bfloat16)
        out_copy(4 + half, seconds[half]).start()
    loads[6].wait()
    resid = own[...].astype(jnp.float32) + out_part(col)
    collected = []
    for half in range(2):
        out_copy(2 + half, firsts[half]).wait_recv()
        out_copy(4 + half, seconds[half]).wait_recv()
        collected.append(
            resid[halves[half]]
            + out_recv[2 + half].astype(jnp.float32)
            + out_recv[4 + half].astype(jnp.float32)
        )
    resid = jnp.concatenate(collected, 0)

    def stat_copy(source, target):
        return pltpu.make_async_remote_copy(
            src_ref=stat_send.at[target],
            dst_ref=stat_recv.at[source],
            send_sem=stat_send_sem.at[target],
            recv_sem=stat_recv_sem.at[source],
            device_id=(row, target),
            device_id_type=MESH,
        )

    middle = jnp.sum(resid, -1, keepdims=True) / features
    centred = resid - middle
    spread_sum = jnp.sum(centred * centred, -1, keepdims=True)
    stats = jnp.where(lane < 1, middle, spread_sum)
    for index in range(cols):
        stat_send[index] = stats[index * piece : (index + 1) * piece]
    for target in others:
        stat_copy(col, target).start()
    final = (centred * final_gain_ref[...].reshape(1, -1)).astype(jnp.bfloat16)

    def single_copy(source, target):
        return pltpu.make_async_remote_copy(
            src_ref=single_send.at[target],
            dst_ref=single_recv.at[source],
            send_sem=single_send_sem.at[target],
            recv_sem=single_recv_sem.at[source],
            device_id=(row, target),
            device_id_type=MESH,
        )

    part = jnp.dot(final, w_single[...], preferred_element_type=jnp.float32)
    for index in range(cols):
        block = part[index * piece : (index + 1) * piece]
        single_own[index] = block
        single_send[index] = block.astype(jnp.bfloat16)
    for target in others:
        single_copy(col, target).start()
    for source in others:
        stat_copy(source, source).wait_recv()
        gain_copy(source, source).wait_recv()
    stat_recv[col] = stat_send[col]
    middles = [stat_recv[index][:, 0:1] for index in range(cols)]
    average = sum(middles) / cols
    variance = sum(stat_recv[index][:, 1:2] for index in range(cols)) / model_width
    variance += sum((middles[index] - average) * (middles[index] - average) for index in range(cols)) / cols
    scale = lax.rsqrt(variance + epsilon)
    summed = single_own[col]
    for index in range(cols):
        summed += (middles[index] - average) * gain_sums[index][0:1]
    for source in others:
        single_copy(source, source).wait_recv()
        summed += single_recv[source].astype(jnp.float32)
    lifted = jnp.maximum(summed * scale, 0.0).astype(jnp.bfloat16)
    channels = w_left_ref.shape[1]
    both = jnp.dot(lifted, w_sides[...], preferred_element_type=jnp.float32).astype(jnp.bfloat16)

    def sides_copy(source, target):
        return pltpu.make_async_remote_copy(
            src_ref=sides.at[source],
            dst_ref=sides.at[source],
            send_sem=sides_send_sem.at[target],
            recv_sem=sides_recv_sem.at[source],
            device_id=(row, target),
            device_id_type=MESH,
        )

    def right_copy(slot, index, step):
        return pltpu.make_async_remote_copy(
            src_ref=right_own,
            dst_ref=right_all.at[slot, index],
            send_sem=right_send_sem.at[step],
            recv_sem=right_recv_sem.at[slot, index],
            device_id=((row + step) % rows, row // owners),
            device_id_type=MESH,
        )

    right_own[...] = both[:, channels:]
    for step in range(1, rows):
        right_copy(row % owners, col, step).start()

    @pl.when(jnp.logical_not(is_owner))
    def _():
        right_copy(row % owners, col, 0).start()

    sides[col] = both[:, :channels]
    for target in others:
        sides_copy(col, target).start()

    @pl.when(is_owner)
    def _():
        right_all[row % owners, col] = right_own[...]

    for source in others:
        sides_copy(source, source).wait_recv()
    for index in range(cols):
        left_ref[index * piece : (index + 1) * piece] = sides[index]
    for slot in range(owners):
        for index in range(cols):

            @pl.when(jnp.logical_or(row != col * owners + slot, col != index))
            def _():
                right_copy(slot, index, 1).wait_recv()

            start_row = slot * count + index * piece
            right_ref[start_row : start_row + piece] = right_all[slot, index]

    for chunk in range(2):
        pass_on(row, chunk, True, True, finish)
        for step in range(1, chips - 1):

            @pl.when(chip - step >= 0)
            def _():
                pass_on(row - 2 * step, chunk, step < chips - 2, False, finish)

            @pl.when(chip + step < chips)
            def _():
                pass_on(row + 2 * step, chunk, False, step < chips - 2, finish)

    @pl.when(outer)
    def _():
        for part in range(2):
            pass_on(farthest, part, False, False, finish)
            far_out(part).wait_send()
            share(part, finish)
            share_corner(part, finish)

    rel_copy(slots - 2).wait()
    rel_copy(slots - 1).wait()
    for half in range(2):
        out_copy(half, firsts[half]).wait_send()
        out_copy(2 + half, firsts[half]).wait_send()
        out_copy(4 + half, seconds[half]).wait_send()
    for target in others:
        stat_copy(col, target).wait_send()
        single_copy(col, target).wait_send()
        sides_copy(col, target).wait_send()
        gain_copy(col, target).wait_send()

    for step in range(1, rows):
        right_copy(row % owners, col, step).wait_send()

    @pl.when(jnp.logical_not(is_owner))
    def _():
        right_copy(row % owners, col, 0).wait_send()


def padded(array, axis, size, groups=1):
    width = array.shape[axis] // groups
    if width == size:
        return array
    shape = array.shape
    array = array.reshape(shape[:axis] + (groups, width) + shape[axis + 1 :])
    pads = [(0, 0)] * array.ndim
    pads[axis + 1] = (0, size - width)
    array = jnp.pad(array, pads)
    return array.reshape(shape[:axis] + (groups * size,) + shape[axis + 1 :])


def front_general(
    hidden,
    attn_gain,
    w_query,
    w_key,
    w_value,
    w_out,
    final_gain,
    w_single,
    w_second,
    w_left,
    w_right,
):
    rows = lax.axis_size("row")
    cols = lax.axis_size("col")
    count, model_width = hidden.shape
    width = -(-w_query.shape[1] // 128) * 128
    features = -(-w_single.shape[0] // 128) * 128
    pairs = width // 128
    piece = count // cols
    owners = rows // cols
    single_width = w_second.shape[0]
    channels = w_left.shape[1]
    positions = lax.axis_index("row") * count + jnp.arange(count, dtype=jnp.int32)
    frequency = jnp.exp(
        jnp.arange(HD // 2, dtype=jnp.float32) * (-2.0 * math.log(10000.0) / HD)
    )
    angles = positions.astype(jnp.float32)[:, None] * frequency[None, :]
    cosine = jnp.cos(angles)
    sine = jnp.sin(angles)
    cosine = jnp.concatenate([cosine] * 4, -1)
    sine = jnp.concatenate([-sine, sine, -sine, sine], -1)
    weights = (
        padded(w_query, 1, width),
        padded(w_key, 1, width),
        padded(w_value, 1, width),
        padded(padded(w_out, 0, width), 1, features, cols),
        padded(w_single, 0, features),
        w_second,
    )
    vmem = pl.BlockSpec(memory_space=pltpu.VMEM)
    anywhere = pl.BlockSpec(memory_space=pl.ANY)
    bf16 = jnp.bfloat16
    f32 = jnp.float32
    dma = pltpu.SemaphoreType.DMA
    return pl.pallas_call(
        functools.partial(front_kernel, rows, cols, model_width),
        out_shape=(
            jax.ShapeDtypeStruct((count, channels), bf16),
            jax.ShapeDtypeStruct((owners * count, channels), bf16),
        ),
        in_specs=[vmem, anywhere] + [vmem] * 4 + [anywhere] * 6 + [vmem] * 2,
        out_specs=(vmem, vmem),
        scratch_shapes=[pltpu.VMEM(weight.shape, bf16) for weight in weights]
        + [
            pltpu.VMEM((count, features), bf16),
            pltpu.VMEM((rows, 2, pairs, count, 128), bf16),
            pltpu.VMEM((pairs, 2 * count, 128), bf16),
            pltpu.VMEM((pairs, 2 * count, count), f32),
            pltpu.VMEM((pairs, 2 * count, 128), f32),
            pltpu.VMEM((count, width), bf16),
            pltpu.VMEM((cols, count, features), bf16),
            pltpu.VMEM((cols, count, features), bf16),
            pltpu.VMEM((8, count), f32),
            pltpu.VMEM((cols, 8, count), f32),
            pltpu.VMEM((cols, piece, single_width), f32),
            pltpu.VMEM((cols, piece, single_width), bf16),
            pltpu.VMEM((cols, piece, single_width), bf16),
            pltpu.VMEM((cols, piece, channels), bf16),
            pltpu.VMEM((piece, channels), bf16),
            pltpu.VMEM((owners, cols, piece, channels), bf16),
            dma((7,)),
            dma((3, rows, 2)),
            dma((rows, 2)),
            dma((cols,)),
            dma((cols,)),
            dma((cols,)),
            dma((cols,)),
            dma((cols,)),
            dma((cols,)),
            dma((cols,)),
            dma((cols,)),
            dma((rows,)),
            dma((owners, cols)),
        ],
        compiler_params=pltpu.CompilerParams(
            collective_id=0, has_side_effects=True, vmem_limit_bytes=56 << 20
        ),
    )(
        hidden,
        padded(hidden, 1, features, cols),
        attn_gain,
        cosine,
        sine,
        padded(final_gain, 0, features),
        *weights,
        w_left,
        w_right,
    )


def banded_kernel(
    flags,
    rel_ref,
    left_ref,
    right_ref,
    table_ref,
    gain_ref,
    expand_ref,
    contract_ref,
    out_ref,
    table,
    left_parts,
    right_parts,
    table_parts,
    left_wide,
    right_wide,
    table_wide,
):
    block_rows, col_count, channels = out_ref.shape
    bins = table_ref.shape[0]
    chunk = col_count // CHUNKS
    width = WINDOW * chunk
    sub = SUB

    @pl.when(pl.program_id(0) == 0)
    def _():
        table[...] = jnp.zeros_like(table)
        table[:bins] = table_ref[...]
        gain = gain_ref[...]
        weights = jnp.concatenate([expand_ref[...]] * 2, 0)
        for source, parts, wide in (
            (left_ref, left_parts, left_wide),
            (right_ref, right_parts, right_wide),
            (table, table_parts, table_wide),
        ):
            values = source[...].astype(jnp.float32)
            centred = values - jnp.sum(values, -1, keepdims=True) / channels
            parts[0] = values
            parts[1] = centred
            scaled = centred * gain
            coarse = scaled.astype(jnp.bfloat16)
            fine = (scaled - coarse.astype(jnp.float32)).astype(jnp.bfloat16)
            wide[...] = jnp.dot(
                jnp.concatenate([coarse, fine], 1), weights, preferred_element_type=jnp.float32
            )

    gain = gain_ref[...]

    def block(first, local, group, start, mixed_width, places):
        sums = []
        scales = []
        expanded = []
        targets = []
        if mixed_width:
            right = right_parts[0, pl.ds(start, mixed_width)]
            pair_in = jnp.concatenate(
                [
                    rel_ref[local + i, pl.ds(start, mixed_width)].astype(jnp.float32)
                    + (right + left_parts[0, pl.ds(first + i, 1)])
                    for i in range(sub)
                ],
                0,
            )
            average = jnp.sum(pair_in, -1, keepdims=True) / channels
            variance = (
                jnp.sum(pair_in * pair_in, -1, keepdims=True) / channels - average * average
            )
            normed = ((pair_in - average) * lax.rsqrt(variance + epsilon) * gain).astype(
                jnp.bfloat16
            )
            wide = jnp.dot(normed, expand_ref[...], preferred_element_type=jnp.float32)
            wide = jnp.maximum(wide.astype(jnp.bfloat16), 0)
            for i in range(sub):
                rows = slice(i * mixed_width, (i + 1) * mixed_width)
                targets.append((local + i, start, mixed_width))
                sums.append(pair_in[rows])
                scales.append(None)
                expanded.append(wide[rows])
        for place in places:
            begin = pl.multiple_of(place * chunk, chunk)
            span = pl.ds(begin, chunk)
            spot = pl.ds(flags[group, place], 1)
            right = right_parts[0, span]
            right_centred = right_parts[1, span]
            right_up = right_wide[span]
            for i in range(sub):
                one = pl.ds(first + i, 1)
                base = left_parts[0, one] + table_parts[0, spot]
                base_centred = left_parts[1, one] + table_parts[1, spot]
                base_up = left_wide[one] + table_wide[spot]
                centred = right_centred + base_centred
                variance = jnp.sum(centred * centred, -1, keepdims=True) / channels
                targets.append((local + i, begin, chunk))
                scales.append(lax.rsqrt(variance + epsilon))
                sums.append(right + base)
                expanded.append(jnp.maximum((right_up + base_up).astype(jnp.bfloat16), 0))
        update = jnp.dot(
            jnp.concatenate(expanded, 0), contract_ref[...], preferred_element_type=jnp.float32
        )
        row = 0
        for total, scale, (place, begin, size) in zip(sums, scales, targets):
            piece = update[row : row + size]
            if scale is not None:
                piece = piece * scale
            out_ref[place, pl.ds(begin, size)] = (total + piece).astype(out_ref.dtype)
            row += size

    @pl.loop(0, block_rows // sub)
    def _(step):
        local = pl.multiple_of(step * sub, sub)
        first = pl.multiple_of(pl.program_id(0) * block_rows + local, sub)
        group = pl.program_id(0) * (block_rows // sub) + step
        begin = jnp.int32(CHUNKS)
        end = jnp.int32(0)
        for index in range(CHUNKS):
            ragged = flags[group, index] < 0
            begin = jnp.where(jnp.logical_and(ragged, begin == CHUNKS), index, begin)
            end = jnp.where(ragged, index + 1, end)
        none = end == 0
        few = jnp.logical_and(end > 0, end - begin <= WINDOW)

        @pl.when(none)
        def _():
            block(first, local, group, 0, 0, range(CHUNKS))

        @pl.when(few)
        def _():
            window = jnp.minimum(begin, CHUNKS - WINDOW)
            places = [
                jnp.where(index < window, index, index + WINDOW)
                for index in range(CHUNKS - WINDOW)
            ]
            block(first, local, group, pl.multiple_of(window * chunk, chunk), width, places)

        @pl.when(end - begin > WINDOW)
        def _():
            block(first, local, group, 0, col_count, ())


def banded_stage(flags, rel, left, right, rel_table, pair_gain, w_expand, w_contract):
    row_count, col_count, _ = rel.shape
    channels = right.shape[1]
    hidden_width = w_expand.shape[1]
    block_rows = math.gcd(row_count, 32)
    bins_padded = -(-rel_table.shape[0] // 128) * 128
    whole = lambda array: pl.BlockSpec(array.shape, lambda i: (0, 0))
    gain = pair_gain.reshape(1, channels)
    operands = (flags, rel, left, right, rel_table, gain, w_expand, w_contract)
    tile = pl.BlockSpec((block_rows, col_count, channels), lambda i: (i, 0, 0))
    f32 = jnp.float32
    return pl.pallas_call(
        banded_kernel,
        grid=(row_count // block_rows,),
        in_specs=[pl.BlockSpec(memory_space=pltpu.SMEM), tile]
        + [whole(operand) for operand in operands[2:]],
        out_specs=tile,
        out_shape=jax.ShapeDtypeStruct((row_count, col_count, channels), jnp.bfloat16),
        scratch_shapes=[
            pltpu.VMEM((bins_padded, channels), jnp.bfloat16),
            pltpu.VMEM((2, row_count, channels), f32),
            pltpu.VMEM((2, col_count, channels), f32),
            pltpu.VMEM((2, bins_padded, channels), f32),
            pltpu.VMEM((row_count, hidden_width), f32),
            pltpu.VMEM((col_count, hidden_width), f32),
            pltpu.VMEM((bins_padded, hidden_width), f32),
        ],
        compiler_params=pltpu.CompilerParams(
            dimension_semantics=("arbitrary",), vmem_limit_bytes=56 << 20
        ),
    )(*operands)


def front_plane(
    hidden,
    attn_gain,
    w_query,
    w_key,
    w_value,
    w_out,
    final_gain,
    w_single,
    w_second,
    w_left,
    w_right,
    rel_bins,
    rel_table,
):
    rows = lax.axis_size("row")
    cols = lax.axis_size("col")
    count, model_width = hidden.shape
    width = -(-w_query.shape[1] // 128) * 128
    features = -(-w_single.shape[0] // 128) * 128
    pairs = width // 128
    piece = count // cols
    owners = rows // cols
    single_width = w_second.shape[0]
    channels = w_left.shape[1]
    frequency = np.exp(np.arange(HD // 2) * (-2.0 * math.log(10000.0) / HD))
    frequency = np.concatenate([frequency] * 4)[None, :]
    offsets = np.arange(count)[:, None] * frequency
    steps = (np.arange(rows) * count)[:, None] * frequency
    angles = [
        jnp.asarray(turn(angle), jnp.float32)
        for angle in (offsets, steps)
        for turn in (np.cos, np.sin)
    ]
    weights = (w_query, w_key, w_value, w_out, w_single, w_second)
    vmem = pl.BlockSpec(memory_space=pltpu.VMEM)
    anywhere = pl.BlockSpec(memory_space=pl.ANY)
    bf16 = jnp.bfloat16
    f32 = jnp.float32
    dma = pltpu.SemaphoreType.DMA
    return pl.pallas_call(
        functools.partial(plane_kernel, rows, cols, model_width),
        out_shape=(
            jax.ShapeDtypeStruct((count, channels), bf16),
            jax.ShapeDtypeStruct((owners * count, channels), bf16),
            jax.ShapeDtypeStruct(rel_bins.shape + (channels,), bf16),
            jax.ShapeDtypeStruct((rel_bins.shape[0] // SUB, 128), jnp.int32),
        ),
        in_specs=[vmem, anywhere] + [vmem] * 6 + [anywhere] * 6 + [vmem] * 4,
        out_specs=(vmem, vmem, anywhere, vmem),
        scratch_shapes=[pltpu.VMEM(weight.shape, bf16) for weight in weights]
        + [
            pltpu.VMEM((count, features), bf16),
            pltpu.VMEM((2, piece // 2, model_width), bf16),
            pltpu.VMEM((cols, 2, piece // 2, model_width), bf16),
            pltpu.VMEM((rows, 2, pairs, count, 128), bf16),
            pltpu.VMEM((pairs, 2 * count, 128), bf16),
            pltpu.VMEM((pairs, 2 * count, count), f32),
            pltpu.VMEM((2, pairs, 2 * count, 2 * count), bf16),
            pltpu.VMEM((pairs, 2 * count, 128), f32),
            pltpu.VMEM((single_width, 2 * channels), bf16),
            pltpu.VMEM((count, width), bf16),
            pltpu.VMEM((6, count // 2, features), bf16),
            pltpu.VMEM((6, count // 2, features), bf16),
            pltpu.VMEM((cols, piece, 128), f32),
            pltpu.VMEM((cols, piece, 128), f32),
            pltpu.VMEM((cols, 8, single_width), f32),
            pltpu.VMEM((cols, piece, single_width), f32),
            pltpu.VMEM((cols, piece, single_width), bf16),
            pltpu.VMEM((cols, piece, single_width), bf16),
            pltpu.VMEM((cols, piece, channels), bf16),
            pltpu.VMEM((piece, channels), bf16),
            pltpu.VMEM((owners, cols, piece, channels), bf16),
            pltpu.VMEM((-(-rel_table.shape[0] // 16) * 16, channels), bf16),
            pltpu.VMEM((2, rel_bins.shape[0] // 8, rel_bins.shape[1], channels), bf16),
            dma((7,)),
            dma((2,)),
            dma((3, 2)),
            dma((cols, 2)),
            dma((3, rows, 2)),
            dma((rows, 2)),
            dma((6,)),
            dma((6,)),
            dma((cols,)),
            dma((cols,)),
            dma((cols,)),
            dma((cols,)),
            dma((cols,)),
            dma((cols,)),
            dma((rows,)),
            dma((owners, cols)),
            dma((cols,)),
            dma((cols,)),
            dma((2,)),
        ],
        compiler_params=pltpu.CompilerParams(
            collective_id=0, has_side_effects=True, vmem_limit_bytes=56 << 20
        ),
    )(
        hidden,
        hidden,
        attn_gain,
        *angles,
        final_gain,
        *weights,
        w_left,
        w_right,
        rel_bins,
        rel_table,
    )


def local(
    hidden,
    rel_bins,
    attn_gain,
    w_query,
    w_key,
    w_value,
    w_out,
    final_gain,
    w_single,
    w_second,
    w_left,
    w_right,
    rel_table,
    pair_gain,
    w_expand,
    w_contract,
):
    rows = lax.axis_size("row")
    cols = lax.axis_size("col")
    aligned = w_query.shape[1] % 128 == 0 and hidden.shape[0] % (32 * cols) == 0
    operands = (
        hidden,
        attn_gain,
        w_query,
        w_key,
        w_value,
        w_out,
        final_gain,
        w_single,
        w_second,
        w_left,
        w_right,
    )
    if rows == 2 * cols and cols == 4 and aligned and rel_bins.shape[1] % (16 * CHUNKS) == 0:
        left, right, rel, flags = front_plane(*operands, rel_bins, rel_table)
        return banded_stage(
            flags, rel, left, right, rel_table, pair_gain, w_expand, w_contract
        )
    left, right = front_general(*operands)
    return pair_stage(rel_bins, left, right, rel_table, pair_gain, w_expand, w_contract)


def solution(mesh):
    in_specs = (
        P("row", None),
        P("row", "col"),
        P(),
        P(None, "col"),
        P(None, "col"),
        P(None, "col"),
        P("col", None),
        P("col"),
        P("col", None),
        P(),
        P(),
        P(),
        P(),
        P(),
        P(),
        P(),
    )
    out_specs = P("row", "col", None)
    return jax.shard_map(local, mesh=mesh, in_specs=in_specs, out_specs=out_specs, check_vma=False)
```

```python
import functools
import math

import jax
import jax.numpy as jnp
import numpy as np
from jax import lax
from jax.experimental import pallas as pl
from jax.experimental.pallas import tpu as pltpu
from jax.sharding import PartitionSpec as P

HD = 64
SUB = 16
CHUNKS = 8
WINDOW = 3
MESH = pl.DeviceIdType.MESH


epsilon = 1e-05


def pair_kernel(bins_ref, left_ref, right_ref, table_ref, gain_ref, expand_ref, contract_ref, out_ref, table):
    block_rows, col_count = bins_ref.shape
    channels = right_ref.shape[1]
    right = right_ref[...].astype(jnp.float32)
    bins = table_ref.shape[0]

    @pl.when(pl.program_id(0) == 0)
    def _():
        table[...] = jnp.zeros_like(table)
        table[:bins] = table_ref[...]

    codes = lax.broadcasted_iota(jnp.int32, (table.shape[0], col_count), 0)
    hot = jnp.concatenate(
        [
            jnp.where(bins_ref[i : i + 1, :] == codes, 1.0, 0.0).astype(jnp.bfloat16)
            for i in range(block_rows)
        ],
        1,
    )
    part = lax.dot_general(
        hot, table[...], (((0,), (0,)), ((), ())), preferred_element_type=jnp.float32
    )
    pair_in = jnp.concatenate(
        [
            part[i * col_count : (i + 1) * col_count]
            + (right + left_ref[i : i + 1, :].astype(jnp.float32))
            for i in range(block_rows)
        ],
        0,
    )
    average = jnp.sum(pair_in, -1, keepdims=True) / channels
    variance = jnp.sum(pair_in * pair_in, -1, keepdims=True) / channels - average * average
    normed = ((pair_in - average) * lax.rsqrt(variance + epsilon) * gain_ref[...]).astype(
        jnp.bfloat16
    )
    expanded = jnp.dot(normed, expand_ref[...], preferred_element_type=jnp.float32)
    expanded = jnp.maximum(expanded.astype(jnp.bfloat16), 0)
    update = jnp.dot(expanded, contract_ref[...], preferred_element_type=jnp.float32)
    out_ref[...] = (pair_in + update).astype(out_ref.dtype).reshape(out_ref.shape)


def pair_stage(rel_bins, left, right, rel_table, pair_gain, w_expand, w_contract):
    row_count, col_count = rel_bins.shape
    channels = right.shape[1]
    block_rows = math.gcd(row_count, 32)
    bins_padded = -(-rel_table.shape[0] // 128) * 128
    whole = lambda array: pl.BlockSpec(array.shape, lambda i: (0, 0))
    gain = pair_gain.reshape(1, channels)
    return pl.pallas_call(
        pair_kernel,
        grid=(row_count // block_rows,),
        in_specs=[
            pl.BlockSpec((block_rows, col_count), lambda i: (i, 0)),
            pl.BlockSpec((block_rows, channels), lambda i: (i, 0)),
            whole(right),
            whole(rel_table),
            whole(gain),
            whole(w_expand),
            whole(w_contract),
        ],
        out_specs=pl.BlockSpec((block_rows, col_count, channels), lambda i: (i, 0, 0)),
        out_shape=jax.ShapeDtypeStruct((row_count, col_count, channels), jnp.bfloat16),
        scratch_shapes=[pltpu.VMEM((bins_padded, channels), jnp.bfloat16)],
        compiler_params=pltpu.CompilerParams(
            dimension_semantics=("arbitrary",), vmem_limit_bytes=56 << 20
        ),
    )(rel_bins, left, right, rel_table, gain, w_expand, w_contract)


def front_kernel(
    rows,
    cols,
    model_width,
    hidden_ref,
    own_hbm,
    attn_gain_ref,
    cos_ref,
    sin_ref,
    final_gain_ref,
    w_query_hbm,
    w_key_hbm,
    w_value_hbm,
    w_out_hbm,
    w_single_hbm,
    w_second_hbm,
    w_left_ref,
    w_right_ref,
    left_ref,
    right_ref,
    w_query,
    w_key,
    w_value,
    w_out,
    w_single,
    w_second,
    own,
    kv,
    query,
    totals,
    numerator,
    context,
    out_send,
    out_recv,
    stat_send,
    stat_recv,
    single_own,
    single_send,
    single_recv,
    sides,
    right_own,
    right_all,
    weight_sem,
    kv_send_sem,
    kv_recv_sem,
    out_send_sem,
    out_recv_sem,
    stat_send_sem,
    stat_recv_sem,
    single_send_sem,
    single_recv_sem,
    sides_send_sem,
    sides_recv_sem,
    right_send_sem,
    right_recv_sem,
):
    row = lax.axis_index("row")
    col = lax.axis_index("col")
    count = hidden_ref.shape[0]
    pairs = query.shape[0]
    features = w_single.shape[0]
    piece = single_own.shape[1]
    owners = rows // cols
    chips = rows // 2
    chip = row // 2
    core = row % 2
    partner = row + 1 - 2 * core

    own_columns = pl.ds(pl.multiple_of(col * features, 128), features)
    loads = []
    for index, (source, target) in enumerate(
        (
            (w_key_hbm, w_key),
            (w_value_hbm, w_value),
            (w_query_hbm, w_query),
            (w_out_hbm, w_out),
            (w_single_hbm, w_single),
            (w_second_hbm, w_second),
            (own_hbm.at[:, own_columns], own),
        )
    ):
        load = pltpu.make_async_copy(source, target, weight_sem.at[index])
        load.start()
        loads.append(load)

    barrier = pltpu.get_barrier_semaphore()
    is_owner = row // owners == col

    def greet(target_row, target_col):
        pl.semaphore_signal(
            barrier, inc=1, device_id=(target_row, target_col), device_id_type=MESH
        )

    greet(partner, col)

    @pl.when(chip + 1 < chips)
    def _():
        greet(row + 2, col)

    @pl.when(chip >= 1)
    def _():
        greet(row - 2, col)

    for slot in range(owners):
        for index in range(cols):

            @pl.when(jnp.logical_or(row != col * owners + slot, col != index))
            def _():
                greet(col * owners + slot, index)

    greetings = cols + rows
    greetings += jnp.where(chip + 1 < chips, 1, 0) + jnp.where(chip >= 1, 1, 0)
    greetings -= jnp.where(is_owner, 1, 0)
    for step in range(1, cols):
        pl.semaphore_signal(
            barrier, inc=1, device_id=(row, (col + step) % cols), device_id_type=MESH
        )

    stream = hidden_ref[...].astype(jnp.float32)
    average = jnp.sum(stream, -1, keepdims=True) / model_width
    variance = jnp.sum(stream * stream, -1, keepdims=True) / model_width - average * average
    attn_in = (
        (stream - average) * lax.rsqrt(variance + epsilon) * attn_gain_ref[...].reshape(1, -1)
    ).astype(jnp.bfloat16)
    cosine = cos_ref[...]
    sine = sin_ref[...]
    lane = lax.broadcasted_iota(jnp.int32, (count, 128), 1)
    first_half = lane % HD < HD // 2
    first_head = lane < HD

    def rope(vectors):
        turned = jnp.where(
            first_half,
            pltpu.roll(vectors, 128 - HD // 2, 1),
            pltpu.roll(vectors, HD // 2, 1),
        )
        return vectors * cosine + turned * sine

    def kv_copy(source, chunk, way, target):
        return pltpu.make_async_remote_copy(
            src_ref=kv.at[source, chunk],
            dst_ref=kv.at[source, chunk],
            send_sem=kv_send_sem.at[way, source, chunk],
            recv_sem=kv_recv_sem.at[source, chunk],
            device_id=(target, col),
            device_id_type=MESH,
        )

    def pass_on(source, chunk, right, left, act):
        if right:

            @pl.when(chip + 1 < chips)
            def _():
                act(kv_copy(source, chunk, 0, row + 2))

        if left:

            @pl.when(chip >= 1)
            def _():
                act(kv_copy(source, chunk, 1, row - 2))

        act(kv_copy(source, chunk, 2, partner))

    def start(copy):
        copy.start()

    def finish(copy):
        copy.wait_send()

    loads[0].wait()
    projected = jnp.dot(attn_in, w_key[...], preferred_element_type=jnp.float32)
    for pair in range(pairs):
        kv[row, 0, pair] = rope(projected[:, pair * 128 : pair * 128 + 128]).astype(jnp.bfloat16)
    pl.semaphore_wait(barrier, greetings)
    pass_on(row, 0, True, True, start)
    loads[1].wait()
    projected = jnp.dot(attn_in, w_value[...], preferred_element_type=jnp.float32)
    for pair in range(pairs):
        kv[row, 1, pair] = projected[:, pair * 128 : pair * 128 + 128].astype(jnp.bfloat16)
    pass_on(row, 1, True, True, start)
    loads[2].wait()
    projected = jnp.dot(attn_in, w_query[...], preferred_element_type=jnp.float32) * HD ** (-0.5)
    for pair in range(pairs):
        turned = rope(projected[:, pair * 128 : pair * 128 + 128])
        query[pair, :count] = jnp.where(first_head, turned, 0.0).astype(jnp.bfloat16)
        query[pair, count:] = jnp.where(first_head, 0.0, turned).astype(jnp.bfloat16)
    totals[...] = jnp.zeros_like(totals)
    numerator[...] = jnp.zeros_like(numerator)

    def attend(source):
        for pair in range(pairs):
            scores = lax.dot_general(
                query[pair],
                kv[source, 0, pair],
                (((1,), (1,)), ((), ())),
                preferred_element_type=jnp.float32,
            )
            weights = jnp.exp(scores)
            totals[pair] += weights
            numerator[pair] += jnp.dot(
                weights.astype(jnp.bfloat16),
                kv[source, 1, pair],
                preferred_element_type=jnp.float32,
            )

    def arrive(source):
        for chunk in range(2):
            kv_copy(source, chunk, 2, partner).wait_recv()

    attend(row)
    arrive(partner)
    attend(partner)

    @pl.loop(1, chips)
    def _(step):
        from_left = chip - step >= 0
        from_right = chip + step < chips
        for chunk in range(2):

            @pl.when(from_left)
            def _():
                source = row - 2 * step
                kv_copy(source, chunk, 2, partner).wait_recv()
                pass_on(source, chunk, True, False, start)

            @pl.when(from_right)
            def _():
                source = row + 2 * step
                kv_copy(source, chunk, 2, partner).wait_recv()
                pass_on(source, chunk, False, True, start)

        @pl.when(from_left)
        def _():
            attend(row - 2 * step)
            arrive(partner - 2 * step)
            attend(partner - 2 * step)

        @pl.when(from_right)
        def _():
            attend(row + 2 * step)
            arrive(partner + 2 * step)
            attend(partner + 2 * step)

    for pair in range(pairs):
        shares = numerator[pair] / jnp.sum(totals[pair], -1, keepdims=True)
        context[:, pair * 128 : pair * 128 + 128] = jnp.where(
            first_head, shares[:count], shares[count:]
        ).astype(jnp.bfloat16)

    def out_copy(source, target):
        return pltpu.make_async_remote_copy(
            src_ref=out_send.at[target],
            dst_ref=out_recv.at[source],
            send_sem=out_send_sem.at[target],
            recv_sem=out_recv_sem.at[source],
            device_id=(row, target),
            device_id_type=MESH,
        )

    def out_part(target):
        columns = pl.ds(pl.multiple_of(target * features, 128), features)
        return jnp.dot(context[...], w_out[:, columns], preferred_element_type=jnp.float32)

    others = [(col + step) % cols for step in range(1, cols)]
    loads[3].wait()
    for target in others:
        out_send[target] = out_part(target).astype(jnp.bfloat16)
        out_copy(col, target).start()
    loads[6].wait()
    resid = own[...].astype(jnp.float32) + out_part(col)
    for source in others:
        out_copy(source, source).wait_recv()
        resid += out_recv[source].astype(jnp.float32)

    def stat_copy(source, target):
        return pltpu.make_async_remote_copy(
            src_ref=stat_send,
            dst_ref=stat_recv.at[source],
            send_sem=stat_send_sem.at[target],
            recv_sem=stat_recv_sem.at[source],
            device_id=(row, target),
            device_id_type=MESH,
        )

    sum_first = jnp.sum(resid, -1, keepdims=True)
    sum_second = jnp.sum(resid * resid, -1, keepdims=True)
    sums = jnp.transpose(jnp.where(lane < 4, sum_first, sum_second))[:8]
    stat_send[...] = sums
    for target in others:
        stat_copy(col, target).start()
    for source in others:
        stat_copy(source, source).wait_recv()
        sums += stat_recv[source]
    sums = jnp.transpose(jnp.concatenate([sums] * 16, 0))
    average = sums[:, 0:1] / model_width
    variance = sums[:, 4:5] / model_width - average * average
    final = (
        (resid - average) * lax.rsqrt(variance + epsilon) * final_gain_ref[...].reshape(1, -1)
    ).astype(jnp.bfloat16)

    def single_copy(source, target):
        return pltpu.make_async_remote_copy(
            src_ref=single_send.at[target],
            dst_ref=single_recv.at[source],
            send_sem=single_send_sem.at[target],
            recv_sem=single_recv_sem.at[source],
            device_id=(row, target),
            device_id_type=MESH,
        )

    loads[4].wait()
    part = jnp.dot(final, w_single[...], preferred_element_type=jnp.float32)
    for index in range(cols):
        block = part[index * piece : (index + 1) * piece]
        single_own[index] = block
        single_send[index] = block.astype(jnp.bfloat16)
    for target in others:
        single_copy(col, target).start()
    summed = single_own[col]
    for source in others:
        single_copy(source, source).wait_recv()
        summed += single_recv[source].astype(jnp.float32)
    lifted = jnp.maximum(summed, 0.0).astype(jnp.bfloat16)
    loads[5].wait()
    single = jnp.dot(lifted, w_second[...], preferred_element_type=jnp.float32)
    single = single.astype(jnp.bfloat16)

    def sides_copy(source, target):
        return pltpu.make_async_remote_copy(
            src_ref=sides.at[source],
            dst_ref=sides.at[source],
            send_sem=sides_send_sem.at[target],
            recv_sem=sides_recv_sem.at[source],
            device_id=(row, target),
            device_id_type=MESH,
        )

    def right_copy(slot, index, step):
        return pltpu.make_async_remote_copy(
            src_ref=right_own,
            dst_ref=right_all.at[slot, index],
            send_sem=right_send_sem.at[step],
            recv_sem=right_recv_sem.at[slot, index],
            device_id=((row + step) % rows, row // owners),
            device_id_type=MESH,
        )

    right_own[...] = jnp.dot(
        single, w_right_ref[...], preferred_element_type=jnp.float32
    ).astype(jnp.bfloat16)
    for step in range(1, rows):
        right_copy(row % owners, col, step).start()

    @pl.when(jnp.logical_not(is_owner))
    def _():
        right_copy(row % owners, col, 0).start()

    sides[col] = jnp.dot(single, w_left_ref[...], preferred_element_type=jnp.float32).astype(
        jnp.bfloat16
    )
    for target in others:
        sides_copy(col, target).start()

    @pl.when(is_owner)
    def _():
        right_all[row % owners, col] = right_own[...]

    for source in others:
        sides_copy(source, source).wait_recv()
    for index in range(cols):
        left_ref[index * piece : (index + 1) * piece] = sides[index]
    for slot in range(owners):
        for index in range(cols):

            @pl.when(jnp.logical_or(row != col * owners + slot, col != index))
            def _():
                right_copy(slot, index, 1).wait_recv()

            start_row = slot * count + index * piece
            right_ref[start_row : start_row + piece] = right_all[slot, index]

    for chunk in range(2):
        pass_on(row, chunk, True, True, finish)

    @pl.loop(1, chips)
    def _(step):
        for chunk in range(2):

            @pl.when(chip - step >= 0)
            def _():
                pass_on(row - 2 * step, chunk, True, False, finish)

            @pl.when(chip + step < chips)
            def _():
                pass_on(row + 2 * step, chunk, False, True, finish)

    for target in others:
        out_copy(col, target).wait_send()
        stat_copy(col, target).wait_send()
        single_copy(col, target).wait_send()
        sides_copy(col, target).wait_send()

    for step in range(1, rows):
        right_copy(row % owners, col, step).wait_send()

    @pl.when(jnp.logical_not(is_owner))
    def _():
        right_copy(row % owners, col, 0).wait_send()


def plane_kernel(
    rows,
    cols,
    model_width,
    hidden_ref,
    own_hbm,
    attn_gain_ref,
    cos_ref,
    sin_ref,
    cos_step_ref,
    sin_step_ref,
    final_gain_ref,
    w_query_hbm,
    w_key_hbm,
    w_value_hbm,
    w_out_hbm,
    w_single_hbm,
    w_second_hbm,
    w_left_ref,
    w_right_ref,
    bins_ref,
    table_ref,
    left_ref,
    right_ref,
    rel_hbm,
    flags_ref,
    w_query,
    w_key,
    w_value,
    w_out,
    w_single,
    w_second,
    own,
    piece_send,
    far,
    kv,
    query,
    totals,
    shares,
    numerator,
    w_sides,
    context,
    out_send,
    out_recv,
    stat_send,
    stat_recv,
    gain_sums,
    single_own,
    single_send,
    single_recv,
    sides,
    right_own,
    right_all,
    table,
    rel_slots,
    weight_sem,
    far_out_sem,
    far_send_sem,
    far_recv_sem,
    kv_send_sem,
    kv_recv_sem,
    out_send_sem,
    out_recv_sem,
    stat_send_sem,
    stat_recv_sem,
    single_send_sem,
    single_recv_sem,
    sides_send_sem,
    sides_recv_sem,
    right_send_sem,
    right_recv_sem,
    gain_send_sem,
    gain_recv_sem,
    rel_sem,
):
    row = lax.axis_index("row")
    col = lax.axis_index("col")
    count = hidden_ref.shape[0]
    pairs = query.shape[0]
    features = w_single.shape[0]
    piece = single_own.shape[1]
    owners = rows // cols
    chips = rows // 2
    chip = row // 2
    core = row % 2
    partner = row + 1 - 2 * core
    outer = jnp.logical_or(chip == 0, chip == chips - 1)
    farthest = (chips - 1 - chip) * 2 + core
    side = col + 1 - 2 * (col % 2)
    across = (col + 2) % cols
    corner = cols - 1 - col

    own_columns = pl.ds(pl.multiple_of(col * features, 128), features)
    loads = []
    for index, (source, target) in enumerate(
        (
            (w_key_hbm, w_key),
            (w_value_hbm, w_value),
            (w_query_hbm, w_query),
            (w_out_hbm, w_out),
            (w_single_hbm, w_single),
            (w_second_hbm, w_second),
            (own_hbm.at[:, own_columns], own),
        )
    ):
        load = pltpu.make_async_copy(source, target, weight_sem.at[index])
        load.start()
        loads.append(load)

    barrier = pltpu.get_barrier_semaphore()
    is_owner = row // owners == col

    def greet(target_row, target_col):
        pl.semaphore_signal(
            barrier, inc=1, device_id=(target_row, target_col), device_id_type=MESH
        )

    greet(partner, col)

    @pl.when(chip + 1 < chips)
    def _():
        greet(row + 2, col)

    @pl.when(chip >= 1)
    def _():
        greet(row - 2, col)

    @pl.when(outer)
    def _():
        greet(farthest, col)

    greetings = cols + jnp.where(outer, 1, 0)
    greetings += jnp.where(chip + 1 < chips, 1, 0) + jnp.where(chip >= 1, 1, 0)
    for step in range(1, cols):
        pl.semaphore_signal(
            barrier, inc=1, device_id=(row, (col + step) % cols), device_id_type=MESH
        )

    def normalize(values):
        stream = values.astype(jnp.float32)
        average = jnp.sum(stream, -1, keepdims=True) / model_width
        variance = jnp.sum(stream * stream, -1, keepdims=True) / model_width - average * average
        return (
            (stream - average) * lax.rsqrt(variance + epsilon) * attn_gain_ref[...].reshape(1, -1)
        ).astype(jnp.bfloat16)

    half = piece // 2

    @pl.when(outer)
    def _():
        for part in range(2):
            first = pl.multiple_of(col * piece + part * half, half)
            piece_send[part] = normalize(hidden_ref[pl.ds(first, half)])

    lane = lax.broadcasted_iota(jnp.int32, (count, 128), 1)
    first_half = lane % HD < HD // 2
    first_head = lane < HD

    def tables(source):
        cosine = cos_ref[...]
        sine = sin_ref[...]
        cos_step = cos_step_ref[pl.ds(source, 1), :]
        sin_step = sin_step_ref[pl.ds(source, 1), :]
        turned = sine * cos_step + cosine * sin_step
        return cosine * cos_step - sine * sin_step, jnp.where(first_half, -turned, turned)

    def rope(vectors, cosine, sine):
        turned = jnp.where(
            first_half,
            pltpu.roll(vectors, 128 - HD // 2, 1),
            pltpu.roll(vectors, HD // 2, 1),
        )
        return vectors * cosine + turned * sine

    def far_copy(owner, part, way, target):
        return pltpu.make_async_remote_copy(
            src_ref=far.at[owner, part],
            dst_ref=far.at[owner, part],
            send_sem=far_send_sem.at[way, part],
            recv_sem=far_recv_sem.at[owner, part],
            device_id=(row, target),
            device_id_type=MESH,
        )

    def far_out(part):
        return pltpu.make_async_remote_copy(
            src_ref=piece_send.at[part],
            dst_ref=far.at[col, part],
            send_sem=far_out_sem.at[part],
            recv_sem=far_recv_sem.at[col, part],
            device_id=(farthest, col),
            device_id_type=MESH,
        )

    def share(part, act):
        act(far_copy(col, part, 0, side))
        act(far_copy(col, part, 1, across))

    def share_corner(part, act):
        if part == 0:
            act(far_copy(side, part, 2, across))
        else:
            act(far_copy(across, part, 2, side))

    def far_wait(owner, part):
        far_copy(owner, part, 0, side).wait_recv()

    def kv_copy(source, chunk, way, target):
        return pltpu.make_async_remote_copy(
            src_ref=kv.at[source, chunk],
            dst_ref=kv.at[source, chunk],
            send_sem=kv_send_sem.at[way, source, chunk],
            recv_sem=kv_recv_sem.at[source, chunk],
            device_id=(target, col),
            device_id_type=MESH,
        )

    def pass_on(source, chunk, right, left, act):
        if right:

            @pl.when(chip + 1 < chips)
            def _():
                act(kv_copy(source, chunk, 0, row + 2))

        if left:

            @pl.when(chip >= 1)
            def _():
                act(kv_copy(source, chunk, 1, row - 2))

        act(kv_copy(source, chunk, 2, partner))

    def start(copy):
        copy.start()

    def finish(copy):
        copy.wait_send()

    def keys_of(rows_in, source):
        cosine, sine = tables(source)
        projected = jnp.dot(rows_in, w_key[...], preferred_element_type=jnp.float32)
        for pair in range(pairs):
            kv[source, 0, pair] = rope(
                projected[:, pair * 128 : pair * 128 + 128], cosine, sine
            ).astype(jnp.bfloat16)

    def values_of(rows_in, source):
        projected = jnp.dot(rows_in, w_value[...], preferred_element_type=jnp.float32)
        for pair in range(pairs):
            kv[source, 1, pair] = projected[:, pair * 128 : pair * 128 + 128].astype(jnp.bfloat16)

    pl.semaphore_wait(barrier, greetings)

    @pl.when(outer)
    def _():
        for part in range(2):
            far_out(part).start()

    attn_in = normalize(hidden_ref[...])
    loads[0].wait()
    keys_of(attn_in, row)
    pass_on(row, 0, True, True, start)
    loads[1].wait()
    values_of(attn_in, row)
    pass_on(row, 1, True, True, start)

    def gain_copy(source, target):
        return pltpu.make_async_remote_copy(
            src_ref=gain_sums.at[source],
            dst_ref=gain_sums.at[source],
            send_sem=gain_send_sem.at[target],
            recv_sem=gain_recv_sem.at[source],
            device_id=(row, target),
            device_id_type=MESH,
        )

    others = [corner, side, across]
    loads[2].wait()
    cosine, sine = tables(row)
    projected = jnp.dot(attn_in, w_query[...], preferred_element_type=jnp.float32) * HD ** (-0.5)
    for pair in range(pairs):
        turned = rope(projected[:, pair * 128 : pair * 128 + 128], cosine, sine)
        query[pair, :count] = jnp.where(first_head, turned, 0.0).astype(jnp.bfloat16)
        query[pair, count:] = jnp.where(first_head, 0.0, turned).astype(jnp.bfloat16)
    bins = table_ref.shape[0]
    table[...] = jnp.zeros_like(table)
    table[:bins] = table_ref[...]
    slot_rows = rel_slots.shape[1]
    col_count = bins_ref.shape[1]
    slots = bins_ref.shape[0] // slot_rows

    def rel_copy(index):
        return pltpu.make_async_copy(
            rel_slots.at[index % 2],
            rel_hbm.at[pl.ds(pl.multiple_of(index * slot_rows, slot_rows), slot_rows)],
            rel_sem.at[index % 2],
        )

    def spell(begin, end):
        @pl.loop(begin, end)
        def _(index):
            @pl.when(index >= 2)
            def _():
                rel_copy(index - 2).wait()

            picked = bins_ref[pl.ds(pl.multiple_of(index * slot_rows, slot_rows), slot_rows)]
            codes = lax.broadcasted_iota(jnp.int32, (table.shape[0], col_count), 0)
            hot = jnp.concatenate(
                [
                    jnp.where(picked[i : i + 1, :] == codes, 1.0, 0.0).astype(jnp.bfloat16)
                    for i in range(slot_rows)
                ],
                1,
            )
            chosen = lax.dot_general(
                hot, table[...], (((0,), (0,)), ((), ())), preferred_element_type=jnp.float32
            )
            rel_slots[index % 2] = chosen.astype(jnp.bfloat16).reshape(rel_slots.shape[1:])
            rel_copy(index).start()

    totals[...] = jnp.zeros_like(totals)
    numerator[...] = jnp.zeros_like(numerator)

    def score(source, slot):
        for pair in range(pairs):
            keys = kv[pl.ds(2 * source, 2), 0, pair].reshape(2 * count, 128)
            weights = jnp.exp(
                lax.dot_general(
                    query[pair],
                    keys,
                    (((1,), (1,)), ((), ())),
                    preferred_element_type=jnp.float32,
                )
            )
            totals[pair] += weights[:, :count] + weights[:, count:]
            shares[slot, pair] = weights.astype(jnp.bfloat16)

    def mix(source, slot):
        for pair in range(pairs):
            values = kv[pl.ds(2 * source, 2), 1, pair].reshape(2 * count, 128)
            numerator[pair] += jnp.dot(
                shares[slot, pair], values, preferred_element_type=jnp.float32
            )

    def arrive(source, chunk):
        kv_copy(source, chunk, 2, partner).wait_recv()

    arrive(partner, 0)
    score(chip, 0)
    loads[4].wait()
    gain = final_gain_ref[...].reshape(1, -1)
    coarse = gain.astype(jnp.bfloat16)
    fine = (gain - coarse.astype(jnp.float32)).astype(jnp.bfloat16)
    gains = jnp.concatenate([jnp.broadcast_to(part, (16, features)) for part in (coarse, fine)], 0)
    gained = jnp.dot(gains, w_single[...], preferred_element_type=jnp.float32)
    gain_sums[col] = gained[:8] + gained[16:24]
    for target in others:
        gain_copy(col, target).start()

    arrive(partner, 1)
    mix(chip, 0)

    grouped = bins_ref[...].reshape(flags_ref.shape[0], -1, col_count)
    high = jnp.max(grouped, 1)
    low = jnp.min(grouped, 1)
    spot = lax.broadcasted_iota(jnp.int32, flags_ref.shape, 1)
    flags = jnp.full(flags_ref.shape, -1, jnp.int32)
    width = col_count // CHUNKS
    for index in range(CHUNKS):
        span = slice(index * width, (index + 1) * width)
        top = jnp.max(high[:, span], -1, keepdims=True)
        bottom = jnp.min(low[:, span], -1, keepdims=True)
        flags = jnp.where(spot == index, jnp.where(top == bottom, top, -1), flags)
    flags_ref[...] = flags
    early = jnp.where(outer, slots, 4)
    spell(0, 2)

    @pl.when(outer)
    def _():
        for part in range(2):
            far_wait(col, part)
            share(part, start)

    spell(2, early)

    @pl.when(outer)
    def _():
        far_wait(side, 0)
        share_corner(0, start)
        far_wait(across, 1)
        share_corner(1, start)


    def near(step, onward):
        from_left = chip - step >= 0
        from_right = chip + step < chips

        def receive(chunk):
            @pl.when(from_left)
            def _():
                arrive(row - 2 * step, chunk)
                pass_on(row - 2 * step, chunk, onward, False, start)

            @pl.when(from_right)
            def _():
                arrive(row + 2 * step, chunk)
                pass_on(row + 2 * step, chunk, False, onward, start)

        def use(chunk):
            @pl.when(from_left)
            def _():
                arrive(partner - 2 * step, chunk)
                (mix if chunk else score)(chip - step, 0)

            @pl.when(from_right)
            def _():
                arrive(partner + 2 * step, chunk)
                (mix if chunk else score)(chip + step, 1)

        receive(0)
        if onward:
            receive(1)
        use(0)
        if not onward:
            receive(1)
        use(1)

    for step in range(1, chips - 1):
        near(step, step < chips - 2)
        if step == 1:
            loads[5].wait()
            w_sides[...] = jnp.dot(
                w_second[...],
                jnp.concatenate([w_left_ref[...], w_right_ref[...]], 1),
                preferred_element_type=jnp.float32,
            ).astype(jnp.bfloat16)
            spell(early, slots)

            @pl.when(outer)
            def _():
                far_wait(side, 1)
                far_wait(across, 0)
                for part in range(2):
                    far_wait(corner, part)
                rows_in = far[...].reshape(count, model_width)
                keys_of(rows_in, farthest)
                pass_on(farthest, 0, False, False, start)
                values_of(rows_in, farthest)
                pass_on(farthest, 1, False, False, start)
                for chunk in range(2):
                    arrive(farthest + partner - row, chunk)
                    (mix if chunk else score)(chips - 1 - chip, 0)


    for pair in range(pairs):
        mixed = numerator[pair] / jnp.sum(totals[pair], -1, keepdims=True)
        context[:, pair * 128 : pair * 128 + 128] = jnp.where(
            first_head, mixed[:count], mixed[count:]
        ).astype(jnp.bfloat16)

    split = count // 2
    halves = [slice(0, split), slice(split, count)]
    firsts = (side, across)
    seconds = (across, side)

    def out_copy(slot, target):
        return pltpu.make_async_remote_copy(
            src_ref=out_send.at[slot],
            dst_ref=out_recv.at[slot],
            send_sem=out_send_sem.at[slot],
            recv_sem=out_recv_sem.at[slot],
            device_id=(row, target),
            device_id_type=MESH,
        )

    def out_part(target):
        columns = pl.ds(pl.multiple_of(target * features, 128), features)
        return jnp.dot(context[...], w_out[:, columns], preferred_element_type=jnp.float32)

    loads[3].wait()
    passing = out_part(corner).astype(jnp.bfloat16)
    for half in range(2):
        out_send[half] = passing[halves[half]]
        out_copy(half, firsts[half]).start()
    kept = [None, None]
    for half in range(2):
        passing = out_part(firsts[half])
        out_send[2 + half] = passing[halves[half]].astype(jnp.bfloat16)
        out_copy(2 + half, firsts[half]).start()
        kept[1 - half] = passing[halves[1 - half]]
    for half in range(2):
        out_copy(half, firsts[half]).wait_recv()
        out_send[4 + half] = (kept[half] + out_recv[half].astype(jnp.float32)).astype(jnp.bfloat16)
        out_copy(4 + half, seconds[half]).start()
    loads[6].wait()
    resid = own[...].astype(jnp.float32) + out_part(col)
    collected = []
    for half in range(2):
        out_copy(2 + half, firsts[half]).wait_recv()
        out_copy(4 + half, seconds[half]).wait_recv()
        collected.append(
            resid[halves[half]]
            + out_recv[2 + half].astype(jnp.float32)
            + out_recv[4 + half].astype(jnp.float32)
        )
    resid = jnp.concatenate(collected, 0)

    def stat_copy(source, target):
        return pltpu.make_async_remote_copy(
            src_ref=stat_send.at[target],
            dst_ref=stat_recv.at[source],
            send_sem=stat_send_sem.at[target],
            recv_sem=stat_recv_sem.at[source],
            device_id=(row, target),
            device_id_type=MESH,
        )

    middle = jnp.sum(resid, -1, keepdims=True) / features
    centred = resid - middle
    spread_sum = jnp.sum(centred * centred, -1, keepdims=True)
    stats = jnp.where(lane < 1, middle, spread_sum)
    for index in range(cols):
        stat_send[index] = stats[index * piece : (index + 1) * piece]
    for target in others:
        stat_copy(col, target).start()
    final = (centred * final_gain_ref[...].reshape(1, -1)).astype(jnp.bfloat16)

    def single_copy(source, target):
        return pltpu.make_async_remote_copy(
            src_ref=single_send.at[target],
            dst_ref=single_recv.at[source],
            send_sem=single_send_sem.at[target],
            recv_sem=single_recv_sem.at[source],
            device_id=(row, target),
            device_id_type=MESH,
        )

    part = jnp.dot(final, w_single[...], preferred_element_type=jnp.float32)
    for index in range(cols):
        block = part[index * piece : (index + 1) * piece]
        single_own[index] = block
        single_send[index] = block.astype(jnp.bfloat16)
    for target in others:
        single_copy(col, target).start()
    for source in others:
        stat_copy(source, source).wait_recv()
        gain_copy(source, source).wait_recv()
    stat_recv[col] = stat_send[col]
    middles = [stat_recv[index][:, 0:1] for index in range(cols)]
    average = sum(middles) / cols
    variance = sum(stat_recv[index][:, 1:2] for index in range(cols)) / model_width
    variance += sum((middles[index] - average) * (middles[index] - average) for index in range(cols)) / cols
    scale = lax.rsqrt(variance + epsilon)
    summed = single_own[col]
    for index in range(cols):
        summed += (middles[index] - average) * gain_sums[index][0:1]
    for source in others:
        single_copy(source, source).wait_recv()
        summed += single_recv[source].astype(jnp.float32)
    lifted = jnp.maximum(summed * scale, 0.0).astype(jnp.bfloat16)
    channels = w_left_ref.shape[1]
    both = jnp.dot(lifted, w_sides[...], preferred_element_type=jnp.float32).astype(jnp.bfloat16)

    def sides_copy(source, target):
        return pltpu.make_async_remote_copy(
            src_ref=sides.at[source],
            dst_ref=sides.at[source],
            send_sem=sides_send_sem.at[target],
            recv_sem=sides_recv_sem.at[source],
            device_id=(row, target),
            device_id_type=MESH,
        )

    def right_copy(slot, index, step):
        return pltpu.make_async_remote_copy(
            src_ref=right_own,
            dst_ref=right_all.at[slot, index],
            send_sem=right_send_sem.at[step],
            recv_sem=right_recv_sem.at[slot, index],
            device_id=((row + step) % rows, row // owners),
            device_id_type=MESH,
        )

    right_own[...] = both[:, channels:]
    for step in range(1, rows):
        right_copy(row % owners, col, step).start()

    @pl.when(jnp.logical_not(is_owner))
    def _():
        right_copy(row % owners, col, 0).start()

    sides[col] = both[:, :channels]
    for target in others:
        sides_copy(col, target).start()

    @pl.when(is_owner)
    def _():
        right_all[row % owners, col] = right_own[...]

    for source in others:
        sides_copy(source, source).wait_recv()
    for index in range(cols):
        left_ref[index * piece : (index + 1) * piece] = sides[index]
    for slot in range(owners):
        for index in range(cols):

            @pl.when(jnp.logical_or(row != col * owners + slot, col != index))
            def _():
                right_copy(slot, index, 1).wait_recv()

            start_row = slot * count + index * piece
            right_ref[start_row : start_row + piece] = right_all[slot, index]

    for chunk in range(2):
        pass_on(row, chunk, True, True, finish)
        for step in range(1, chips - 1):

            @pl.when(chip - step >= 0)
            def _():
                pass_on(row - 2 * step, chunk, step < chips - 2, False, finish)

            @pl.when(chip + step < chips)
            def _():
                pass_on(row + 2 * step, chunk, False, step < chips - 2, finish)

    @pl.when(outer)
    def _():
        for part in range(2):
            pass_on(farthest, part, False, False, finish)
            far_out(part).wait_send()
            share(part, finish)
            share_corner(part, finish)

    rel_copy(slots - 2).wait()
    rel_copy(slots - 1).wait()
    for half in range(2):
        out_copy(half, firsts[half]).wait_send()
        out_copy(2 + half, firsts[half]).wait_send()
        out_copy(4 + half, seconds[half]).wait_send()
    for target in others:
        stat_copy(col, target).wait_send()
        single_copy(col, target).wait_send()
        sides_copy(col, target).wait_send()
        gain_copy(col, target).wait_send()

    for step in range(1, rows):
        right_copy(row % owners, col, step).wait_send()

    @pl.when(jnp.logical_not(is_owner))
    def _():
        right_copy(row % owners, col, 0).wait_send()


def padded(array, axis, size, groups=1):
    width = array.shape[axis] // groups
    if width == size:
        return array
    shape = array.shape
    array = array.reshape(shape[:axis] + (groups, width) + shape[axis + 1 :])
    pads = [(0, 0)] * array.ndim
    pads[axis + 1] = (0, size - width)
    array = jnp.pad(array, pads)
    return array.reshape(shape[:axis] + (groups * size,) + shape[axis + 1 :])


def front_general(
    hidden,
    attn_gain,
    w_query,
    w_key,
    w_value,
    w_out,
    final_gain,
    w_single,
    w_second,
    w_left,
    w_right,
):
    rows = lax.axis_size("row")
    cols = lax.axis_size("col")
    count, model_width = hidden.shape
    width = -(-w_query.shape[1] // 128) * 128
    features = -(-w_single.shape[0] // 128) * 128
    pairs = width // 128
    piece = count // cols
    owners = rows // cols
    single_width = w_second.shape[0]
    channels = w_left.shape[1]
    positions = lax.axis_index("row") * count + jnp.arange(count, dtype=jnp.int32)
    frequency = jnp.exp(
        jnp.arange(HD // 2, dtype=jnp.float32) * (-2.0 * math.log(10000.0) / HD)
    )
    angles = positions.astype(jnp.float32)[:, None] * frequency[None, :]
    cosine = jnp.cos(angles)
    sine = jnp.sin(angles)
    cosine = jnp.concatenate([cosine] * 4, -1)
    sine = jnp.concatenate([-sine, sine, -sine, sine], -1)
    weights = (
        padded(w_query, 1, width),
        padded(w_key, 1, width),
        padded(w_value, 1, width),
        padded(padded(w_out, 0, width), 1, features, cols),
        padded(w_single, 0, features),
        w_second,
    )
    vmem = pl.BlockSpec(memory_space=pltpu.VMEM)
    anywhere = pl.BlockSpec(memory_space=pl.ANY)
    bf16 = jnp.bfloat16
    f32 = jnp.float32
    dma = pltpu.SemaphoreType.DMA
    return pl.pallas_call(
        functools.partial(front_kernel, rows, cols, model_width),
        out_shape=(
            jax.ShapeDtypeStruct((count, channels), bf16),
            jax.ShapeDtypeStruct((owners * count, channels), bf16),
        ),
        in_specs=[vmem, anywhere] + [vmem] * 4 + [anywhere] * 6 + [vmem] * 2,
        out_specs=(vmem, vmem),
        scratch_shapes=[pltpu.VMEM(weight.shape, bf16) for weight in weights]
        + [
            pltpu.VMEM((count, features), bf16),
            pltpu.VMEM((rows, 2, pairs, count, 128), bf16),
            pltpu.VMEM((pairs, 2 * count, 128), bf16),
            pltpu.VMEM((pairs, 2 * count, count), f32),
            pltpu.VMEM((pairs, 2 * count, 128), f32),
            pltpu.VMEM((count, width), bf16),
            pltpu.VMEM((cols, count, features), bf16),
            pltpu.VMEM((cols, count, features), bf16),
            pltpu.VMEM((8, count), f32),
            pltpu.VMEM((cols, 8, count), f32),
            pltpu.VMEM((cols, piece, single_width), f32),
            pltpu.VMEM((cols, piece, single_width), bf16),
            pltpu.VMEM((cols, piece, single_width), bf16),
            pltpu.VMEM((cols, piece, channels), bf16),
            pltpu.VMEM((piece, channels), bf16),
            pltpu.VMEM((owners, cols, piece, channels), bf16),
            dma((7,)),
            dma((3, rows, 2)),
            dma((rows, 2)),
            dma((cols,)),
            dma((cols,)),
            dma((cols,)),
            dma((cols,)),
            dma((cols,)),
            dma((cols,)),
            dma((cols,)),
            dma((cols,)),
            dma((rows,)),
            dma((owners, cols)),
        ],
        compiler_params=pltpu.CompilerParams(
            collective_id=0, has_side_effects=True, vmem_limit_bytes=56 << 20
        ),
    )(
        hidden,
        padded(hidden, 1, features, cols),
        attn_gain,
        cosine,
        sine,
        padded(final_gain, 0, features),
        *weights,
        w_left,
        w_right,
    )


def banded_kernel(
    flags,
    rel_ref,
    left_ref,
    right_ref,
    table_ref,
    gain_ref,
    expand_ref,
    contract_ref,
    out_ref,
    table,
    left_parts,
    right_parts,
    table_parts,
    left_wide,
    right_wide,
    table_wide,
):
    block_rows, col_count, channels = out_ref.shape
    bins = table_ref.shape[0]
    chunk = col_count // CHUNKS
    width = WINDOW * chunk
    sub = SUB

    @pl.when(pl.program_id(0) == 0)
    def _():
        table[...] = jnp.zeros_like(table)
        table[:bins] = table_ref[...]
        gain = gain_ref[...]
        weights = jnp.concatenate([expand_ref[...]] * 2, 0)
        for source, parts, wide in (
            (left_ref, left_parts, left_wide),
            (right_ref, right_parts, right_wide),
            (table, table_parts, table_wide),
        ):
            values = source[...].astype(jnp.float32)
            centred = values - jnp.sum(values, -1, keepdims=True) / channels
            parts[0] = values
            parts[1] = centred
            scaled = centred * gain
            coarse = scaled.astype(jnp.bfloat16)
            fine = (scaled - coarse.astype(jnp.float32)).astype(jnp.bfloat16)
            wide[...] = jnp.dot(
                jnp.concatenate([coarse, fine], 1), weights, preferred_element_type=jnp.float32
            )

    gain = gain_ref[...]

    def block(first, local, group, start, mixed_width, places):
        sums = []
        scales = []
        expanded = []
        targets = []
        if mixed_width:
            right = right_parts[0, pl.ds(start, mixed_width)]
            pair_in = jnp.concatenate(
                [
                    rel_ref[local + i, pl.ds(start, mixed_width)].astype(jnp.float32)
                    + (right + left_parts[0, pl.ds(first + i, 1)])
                    for i in range(sub)
                ],
                0,
            )
            average = jnp.sum(pair_in, -1, keepdims=True) / channels
            variance = (
                jnp.sum(pair_in * pair_in, -1, keepdims=True) / channels - average * average
            )
            normed = ((pair_in - average) * lax.rsqrt(variance + epsilon) * gain).astype(
                jnp.bfloat16
            )
            wide = jnp.dot(normed, expand_ref[...], preferred_element_type=jnp.float32)
            wide = jnp.maximum(wide.astype(jnp.bfloat16), 0)
            for i in range(sub):
                rows = slice(i * mixed_width, (i + 1) * mixed_width)
                targets.append((local + i, start, mixed_width))
                sums.append(pair_in[rows])
                scales.append(None)
                expanded.append(wide[rows])
        for place in places:
            begin = pl.multiple_of(place * chunk, chunk)
            span = pl.ds(begin, chunk)
            spot = pl.ds(flags[group, place], 1)
            right = right_parts[0, span]
            right_centred = right_parts[1, span]
            right_up = right_wide[span]
            for i in range(sub):
                one = pl.ds(first + i, 1)
                base = left_parts[0, one] + table_parts[0, spot]
                base_centred = left_parts[1, one] + table_parts[1, spot]
                base_up = left_wide[one] + table_wide[spot]
                centred = right_centred + base_centred
                variance = jnp.sum(centred * centred, -1, keepdims=True) / channels
                targets.append((local + i, begin, chunk))
                scales.append(lax.rsqrt(variance + epsilon))
                sums.append(right + base)
                expanded.append(jnp.maximum((right_up + base_up).astype(jnp.bfloat16), 0))
        update = jnp.dot(
            jnp.concatenate(expanded, 0), contract_ref[...], preferred_element_type=jnp.float32
        )
        row = 0
        for total, scale, (place, begin, size) in zip(sums, scales, targets):
            piece = update[row : row + size]
            if scale is not None:
                piece = piece * scale
            out_ref[place, pl.ds(begin, size)] = (total + piece).astype(out_ref.dtype)
            row += size

    @pl.loop(0, block_rows // sub)
    def _(step):
        local = pl.multiple_of(step * sub, sub)
        first = pl.multiple_of(pl.program_id(0) * block_rows + local, sub)
        group = pl.program_id(0) * (block_rows // sub) + step
        begin = jnp.int32(CHUNKS)
        end = jnp.int32(0)
        for index in range(CHUNKS):
            ragged = flags[group, index] < 0
            begin = jnp.where(jnp.logical_and(ragged, begin == CHUNKS), index, begin)
            end = jnp.where(ragged, index + 1, end)
        none = end == 0
        few = jnp.logical_and(end > 0, end - begin <= WINDOW)

        @pl.when(none)
        def _():
            block(first, local, group, 0, 0, range(CHUNKS))

        @pl.when(few)
        def _():
            window = jnp.minimum(begin, CHUNKS - WINDOW)
            places = [
                jnp.where(index < window, index, index + WINDOW)
                for index in range(CHUNKS - WINDOW)
            ]
            block(first, local, group, pl.multiple_of(window * chunk, chunk), width, places)

        @pl.when(end - begin > WINDOW)
        def _():
            block(first, local, group, 0, col_count, ())


def banded_stage(flags, rel, left, right, rel_table, pair_gain, w_expand, w_contract):
    row_count, col_count, _ = rel.shape
    channels = right.shape[1]
    hidden_width = w_expand.shape[1]
    block_rows = math.gcd(row_count, SUB)
    bins_padded = -(-rel_table.shape[0] // 128) * 128
    whole = lambda array: pl.BlockSpec(array.shape, lambda i: (0, 0))
    gain = pair_gain.reshape(1, channels)
    operands = (flags, rel, left, right, rel_table, gain, w_expand, w_contract)
    tile = pl.BlockSpec((block_rows, col_count, channels), lambda i: (i, 0, 0))
    f32 = jnp.float32
    return pl.pallas_call(
        banded_kernel,
        grid=(row_count // block_rows,),
        in_specs=[pl.BlockSpec(memory_space=pltpu.SMEM), tile]
        + [whole(operand) for operand in operands[2:]],
        out_specs=tile,
        out_shape=jax.ShapeDtypeStruct((row_count, col_count, channels), jnp.bfloat16),
        scratch_shapes=[
            pltpu.VMEM((bins_padded, channels), jnp.bfloat16),
            pltpu.VMEM((2, row_count, channels), f32),
            pltpu.VMEM((2, col_count, channels), f32),
            pltpu.VMEM((2, bins_padded, channels), f32),
            pltpu.VMEM((row_count, hidden_width), f32),
            pltpu.VMEM((col_count, hidden_width), f32),
            pltpu.VMEM((bins_padded, hidden_width), f32),
        ],
        compiler_params=pltpu.CompilerParams(
            dimension_semantics=("arbitrary",), vmem_limit_bytes=56 << 20
        ),
    )(*operands)


def front_plane(
    hidden,
    attn_gain,
    w_query,
    w_key,
    w_value,
    w_out,
    final_gain,
    w_single,
    w_second,
    w_left,
    w_right,
    rel_bins,
    rel_table,
):
    rows = lax.axis_size("row")
    cols = lax.axis_size("col")
    count, model_width = hidden.shape
    width = -(-w_query.shape[1] // 128) * 128
    features = -(-w_single.shape[0] // 128) * 128
    pairs = width // 128
    piece = count // cols
    owners = rows // cols
    single_width = w_second.shape[0]
    channels = w_left.shape[1]
    frequency = np.exp(np.arange(HD // 2) * (-2.0 * math.log(10000.0) / HD))
    frequency = np.concatenate([frequency] * 4)[None, :]
    offsets = np.arange(count)[:, None] * frequency
    steps = (np.arange(rows) * count)[:, None] * frequency
    angles = [
        jnp.asarray(turn(angle), jnp.float32)
        for angle in (offsets, steps)
        for turn in (np.cos, np.sin)
    ]
    weights = (w_query, w_key, w_value, w_out, w_single, w_second)
    vmem = pl.BlockSpec(memory_space=pltpu.VMEM)
    anywhere = pl.BlockSpec(memory_space=pl.ANY)
    bf16 = jnp.bfloat16
    f32 = jnp.float32
    dma = pltpu.SemaphoreType.DMA
    return pl.pallas_call(
        functools.partial(plane_kernel, rows, cols, model_width),
        out_shape=(
            jax.ShapeDtypeStruct((count, channels), bf16),
            jax.ShapeDtypeStruct((owners * count, channels), bf16),
            jax.ShapeDtypeStruct(rel_bins.shape + (channels,), bf16),
            jax.ShapeDtypeStruct((rel_bins.shape[0] // SUB, 128), jnp.int32),
        ),
        in_specs=[vmem, anywhere] + [vmem] * 6 + [anywhere] * 6 + [vmem] * 4,
        out_specs=(vmem, vmem, anywhere, vmem),
        scratch_shapes=[pltpu.VMEM(weight.shape, bf16) for weight in weights]
        + [
            pltpu.VMEM((count, features), bf16),
            pltpu.VMEM((2, piece // 2, model_width), bf16),
            pltpu.VMEM((cols, 2, piece // 2, model_width), bf16),
            pltpu.VMEM((rows, 2, pairs, count, 128), bf16),
            pltpu.VMEM((pairs, 2 * count, 128), bf16),
            pltpu.VMEM((pairs, 2 * count, count), f32),
            pltpu.VMEM((2, pairs, 2 * count, 2 * count), bf16),
            pltpu.VMEM((pairs, 2 * count, 128), f32),
            pltpu.VMEM((single_width, 2 * channels), bf16),
            pltpu.VMEM((count, width), bf16),
            pltpu.VMEM((6, count // 2, features), bf16),
            pltpu.VMEM((6, count // 2, features), bf16),
            pltpu.VMEM((cols, piece, 128), f32),
            pltpu.VMEM((cols, piece, 128), f32),
            pltpu.VMEM((cols, 8, single_width), f32),
            pltpu.VMEM((cols, piece, single_width), f32),
            pltpu.VMEM((cols, piece, single_width), bf16),
            pltpu.VMEM((cols, piece, single_width), bf16),
            pltpu.VMEM((cols, piece, channels), bf16),
            pltpu.VMEM((piece, channels), bf16),
            pltpu.VMEM((owners, cols, piece, channels), bf16),
            pltpu.VMEM((-(-rel_table.shape[0] // 16) * 16, channels), bf16),
            pltpu.VMEM((2, rel_bins.shape[0] // 8, rel_bins.shape[1], channels), bf16),
            dma((7,)),
            dma((2,)),
            dma((3, 2)),
            dma((cols, 2)),
            dma((3, rows, 2)),
            dma((rows, 2)),
            dma((6,)),
            dma((6,)),
            dma((cols,)),
            dma((cols,)),
            dma((cols,)),
            dma((cols,)),
            dma((cols,)),
            dma((cols,)),
            dma((rows,)),
            dma((owners, cols)),
            dma((cols,)),
            dma((cols,)),
            dma((2,)),
        ],
        compiler_params=pltpu.CompilerParams(
            collective_id=0, has_side_effects=True, vmem_limit_bytes=56 << 20
        ),
    )(
        hidden,
        hidden,
        attn_gain,
        *angles,
        final_gain,
        *weights,
        w_left,
        w_right,
        rel_bins,
        rel_table,
    )


def local(
    hidden,
    rel_bins,
    attn_gain,
    w_query,
    w_key,
    w_value,
    w_out,
    final_gain,
    w_single,
    w_second,
    w_left,
    w_right,
    rel_table,
    pair_gain,
    w_expand,
    w_contract,
):
    rows = lax.axis_size("row")
    cols = lax.axis_size("col")
    aligned = w_query.shape[1] % 128 == 0 and hidden.shape[0] % (32 * cols) == 0
    operands = (
        hidden,
        attn_gain,
        w_query,
        w_key,
        w_value,
        w_out,
        final_gain,
        w_single,
        w_second,
        w_left,
        w_right,
    )
    if rows == 2 * cols and cols == 4 and aligned and rel_bins.shape[1] % (16 * CHUNKS) == 0:
        left, right, rel, flags = front_plane(*operands, rel_bins, rel_table)
        return banded_stage(
            flags, rel, left, right, rel_table, pair_gain, w_expand, w_contract
        )
    left, right = front_general(*operands)
    return pair_stage(rel_bins, left, right, rel_table, pair_gain, w_expand, w_contract)


def solution(mesh):
    in_specs = (
        P("row", None),
        P("row", "col"),
        P(),
        P(None, "col"),
        P(None, "col"),
        P(None, "col"),
        P("col", None),
        P("col"),
        P("col", None),
        P(),
        P(),
        P(),
        P(),
        P(),
        P(),
        P(),
    )
    out_specs = P("row", "col", None)
    return jax.shard_map(local, mesh=mesh, in_specs=in_specs, out_specs=out_specs, check_vma=False)
```

```python
import functools
import math

import jax
import jax.numpy as jnp
import numpy as np
from jax import lax
from jax.experimental import pallas as pl
from jax.experimental.pallas import tpu as pltpu
from jax.sharding import PartitionSpec as P

HD = 64
SUB = 16
CHUNKS = 8
WINDOW = 3
MESH = pl.DeviceIdType.MESH


epsilon = 1e-05


def pair_kernel(bins_ref, left_ref, right_ref, table_ref, gain_ref, expand_ref, contract_ref, out_ref, table):
    block_rows, col_count = bins_ref.shape
    channels = right_ref.shape[1]
    right = right_ref[...].astype(jnp.float32)
    bins = table_ref.shape[0]

    @pl.when(pl.program_id(0) == 0)
    def _():
        table[...] = jnp.zeros_like(table)
        table[:bins] = table_ref[...]

    codes = lax.broadcasted_iota(jnp.int32, (table.shape[0], col_count), 0)
    hot = jnp.concatenate(
        [
            jnp.where(bins_ref[i : i + 1, :] == codes, 1.0, 0.0).astype(jnp.bfloat16)
            for i in range(block_rows)
        ],
        1,
    )
    part = lax.dot_general(
        hot, table[...], (((0,), (0,)), ((), ())), preferred_element_type=jnp.float32
    )
    pair_in = jnp.concatenate(
        [
            part[i * col_count : (i + 1) * col_count]
            + (right + left_ref[i : i + 1, :].astype(jnp.float32))
            for i in range(block_rows)
        ],
        0,
    )
    average = jnp.sum(pair_in, -1, keepdims=True) / channels
    variance = jnp.sum(pair_in * pair_in, -1, keepdims=True) / channels - average * average
    normed = ((pair_in - average) * lax.rsqrt(variance + epsilon) * gain_ref[...]).astype(
        jnp.bfloat16
    )
    expanded = jnp.dot(normed, expand_ref[...], preferred_element_type=jnp.float32)
    expanded = jnp.maximum(expanded.astype(jnp.bfloat16), 0)
    update = jnp.dot(expanded, contract_ref[...], preferred_element_type=jnp.float32)
    out_ref[...] = (pair_in + update).astype(out_ref.dtype).reshape(out_ref.shape)


def pair_stage(rel_bins, left, right, rel_table, pair_gain, w_expand, w_contract):
    row_count, col_count = rel_bins.shape
    channels = right.shape[1]
    block_rows = math.gcd(row_count, 32)
    bins_padded = -(-rel_table.shape[0] // 128) * 128
    whole = lambda array: pl.BlockSpec(array.shape, lambda i: (0, 0))
    gain = pair_gain.reshape(1, channels)
    return pl.pallas_call(
        pair_kernel,
        grid=(row_count // block_rows,),
        in_specs=[
            pl.BlockSpec((block_rows, col_count), lambda i: (i, 0)),
            pl.BlockSpec((block_rows, channels), lambda i: (i, 0)),
            whole(right),
            whole(rel_table),
            whole(gain),
            whole(w_expand),
            whole(w_contract),
        ],
        out_specs=pl.BlockSpec((block_rows, col_count, channels), lambda i: (i, 0, 0)),
        out_shape=jax.ShapeDtypeStruct((row_count, col_count, channels), jnp.bfloat16),
        scratch_shapes=[pltpu.VMEM((bins_padded, channels), jnp.bfloat16)],
        compiler_params=pltpu.CompilerParams(
            dimension_semantics=("arbitrary",), vmem_limit_bytes=56 << 20
        ),
    )(rel_bins, left, right, rel_table, gain, w_expand, w_contract)


def front_kernel(
    rows,
    cols,
    model_width,
    hidden_ref,
    own_hbm,
    attn_gain_ref,
    cos_ref,
    sin_ref,
    final_gain_ref,
    w_query_hbm,
    w_key_hbm,
    w_value_hbm,
    w_out_hbm,
    w_single_hbm,
    w_second_hbm,
    w_left_ref,
    w_right_ref,
    left_ref,
    right_ref,
    w_query,
    w_key,
    w_value,
    w_out,
    w_single,
    w_second,
    own,
    kv,
    query,
    totals,
    numerator,
    context,
    out_send,
    out_recv,
    stat_send,
    stat_recv,
    single_own,
    single_send,
    single_recv,
    sides,
    right_own,
    right_all,
    weight_sem,
    kv_send_sem,
    kv_recv_sem,
    out_send_sem,
    out_recv_sem,
    stat_send_sem,
    stat_recv_sem,
    single_send_sem,
    single_recv_sem,
    sides_send_sem,
    sides_recv_sem,
    right_send_sem,
    right_recv_sem,
):
    row = lax.axis_index("row")
    col = lax.axis_index("col")
    count = hidden_ref.shape[0]
    pairs = query.shape[0]
    features = w_single.shape[0]
    piece = single_own.shape[1]
    owners = rows // cols
    chips = rows // 2
    chip = row // 2
    core = row % 2
    partner = row + 1 - 2 * core

    own_columns = pl.ds(pl.multiple_of(col * features, 128), features)
    loads = []
    for index, (source, target) in enumerate(
        (
            (w_key_hbm, w_key),
            (w_value_hbm, w_value),
            (w_query_hbm, w_query),
            (w_out_hbm, w_out),
            (w_single_hbm, w_single),
            (w_second_hbm, w_second),
            (own_hbm.at[:, own_columns], own),
        )
    ):
        load = pltpu.make_async_copy(source, target, weight_sem.at[index])
        load.start()
        loads.append(load)

    barrier = pltpu.get_barrier_semaphore()
    is_owner = row // owners == col

    def greet(target_row, target_col):
        pl.semaphore_signal(
            barrier, inc=1, device_id=(target_row, target_col), device_id_type=MESH
        )

    greet(partner, col)

    @pl.when(chip + 1 < chips)
    def _():
        greet(row + 2, col)

    @pl.when(chip >= 1)
    def _():
        greet(row - 2, col)

    for slot in range(owners):
        for index in range(cols):

            @pl.when(jnp.logical_or(row != col * owners + slot, col != index))
            def _():
                greet(col * owners + slot, index)

    greetings = cols + rows
    greetings += jnp.where(chip + 1 < chips, 1, 0) + jnp.where(chip >= 1, 1, 0)
    greetings -= jnp.where(is_owner, 1, 0)
    for step in range(1, cols):
        pl.semaphore_signal(
            barrier, inc=1, device_id=(row, (col + step) % cols), device_id_type=MESH
        )

    stream = hidden_ref[...].astype(jnp.float32)
    average = jnp.sum(stream, -1, keepdims=True) / model_width
    variance = jnp.sum(stream * stream, -1, keepdims=True) / model_width - average * average
    attn_in = (
        (stream - average) * lax.rsqrt(variance + epsilon) * attn_gain_ref[...].reshape(1, -1)
    ).astype(jnp.bfloat16)
    cosine = cos_ref[...]
    sine = sin_ref[...]
    lane = lax.broadcasted_iota(jnp.int32, (count, 128), 1)
    first_half = lane % HD < HD // 2
    first_head = lane < HD

    def rope(vectors):
        turned = jnp.where(
            first_half,
            pltpu.roll(vectors, 128 - HD // 2, 1),
            pltpu.roll(vectors, HD // 2, 1),
        )
        return vectors * cosine + turned * sine

    def kv_copy(source, chunk, way, target):
        return pltpu.make_async_remote_copy(
            src_ref=kv.at[source, chunk],
            dst_ref=kv.at[source, chunk],
            send_sem=kv_send_sem.at[way, source, chunk],
            recv_sem=kv_recv_sem.at[source, chunk],
            device_id=(target, col),
            device_id_type=MESH,
        )

    def pass_on(source, chunk, right, left, act):
        if right:

            @pl.when(chip + 1 < chips)
            def _():
                act(kv_copy(source, chunk, 0, row + 2))

        if left:

            @pl.when(chip >= 1)
            def _():
                act(kv_copy(source, chunk, 1, row - 2))

        act(kv_copy(source, chunk, 2, partner))

    def start(copy):
        copy.start()

    def finish(copy):
        copy.wait_send()

    loads[0].wait()
    projected = jnp.dot(attn_in, w_key[...], preferred_element_type=jnp.float32)
    for pair in range(pairs):
        kv[row, 0, pair] = rope(projected[:, pair * 128 : pair * 128 + 128]).astype(jnp.bfloat16)
    pl.semaphore_wait(barrier, greetings)
    pass_on(row, 0, True, True, start)
    loads[1].wait()
    projected = jnp.dot(attn_in, w_value[...], preferred_element_type=jnp.float32)
    for pair in range(pairs):
        kv[row, 1, pair] = projected[:, pair * 128 : pair * 128 + 128].astype(jnp.bfloat16)
    pass_on(row, 1, True, True, start)
    loads[2].wait()
    projected = jnp.dot(attn_in, w_query[...], preferred_element_type=jnp.float32) * HD ** (-0.5)
    for pair in range(pairs):
        turned = rope(projected[:, pair * 128 : pair * 128 + 128])
        query[pair, :count] = jnp.where(first_head, turned, 0.0).astype(jnp.bfloat16)
        query[pair, count:] = jnp.where(first_head, 0.0, turned).astype(jnp.bfloat16)
    totals[...] = jnp.zeros_like(totals)
    numerator[...] = jnp.zeros_like(numerator)

    def attend(source):
        for pair in range(pairs):
            scores = lax.dot_general(
                query[pair],
                kv[source, 0, pair],
                (((1,), (1,)), ((), ())),
                preferred_element_type=jnp.float32,
            )
            weights = jnp.exp(scores)
            totals[pair] += weights
            numerator[pair] += jnp.dot(
                weights.astype(jnp.bfloat16),
                kv[source, 1, pair],
                preferred_element_type=jnp.float32,
            )

    def arrive(source):
        for chunk in range(2):
            kv_copy(source, chunk, 2, partner).wait_recv()

    attend(row)
    arrive(partner)
    attend(partner)

    @pl.loop(1, chips)
    def _(step):
        from_left = chip - step >= 0
        from_right = chip + step < chips
        for chunk in range(2):

            @pl.when(from_left)
            def _():
                source = row - 2 * step
                kv_copy(source, chunk, 2, partner).wait_recv()
                pass_on(source, chunk, True, False, start)

            @pl.when(from_right)
            def _():
                source = row + 2 * step
                kv_copy(source, chunk, 2, partner).wait_recv()
                pass_on(source, chunk, False, True, start)

        @pl.when(from_left)
        def _():
            attend(row - 2 * step)
            arrive(partner - 2 * step)
            attend(partner - 2 * step)

        @pl.when(from_right)
        def _():
            attend(row + 2 * step)
            arrive(partner + 2 * step)
            attend(partner + 2 * step)

    for pair in range(pairs):
        shares = numerator[pair] / jnp.sum(totals[pair], -1, keepdims=True)
        context[:, pair * 128 : pair * 128 + 128] = jnp.where(
            first_head, shares[:count], shares[count:]
        ).astype(jnp.bfloat16)

    def out_copy(source, target):
        return pltpu.make_async_remote_copy(
            src_ref=out_send.at[target],
            dst_ref=out_recv.at[source],
            send_sem=out_send_sem.at[target],
            recv_sem=out_recv_sem.at[source],
            device_id=(row, target),
            device_id_type=MESH,
        )

    def out_part(target):
        columns = pl.ds(pl.multiple_of(target * features, 128), features)
        return jnp.dot(context[...], w_out[:, columns], preferred_element_type=jnp.float32)

    others = [(col + step) % cols for step in range(1, cols)]
    loads[3].wait()
    for target in others:
        out_send[target] = out_part(target).astype(jnp.bfloat16)
        out_copy(col, target).start()
    loads[6].wait()
    resid = own[...].astype(jnp.float32) + out_part(col)
    for source in others:
        out_copy(source, source).wait_recv()
        resid += out_recv[source].astype(jnp.float32)

    def stat_copy(source, target):
        return pltpu.make_async_remote_copy(
            src_ref=stat_send,
            dst_ref=stat_recv.at[source],
            send_sem=stat_send_sem.at[target],
            recv_sem=stat_recv_sem.at[source],
            device_id=(row, target),
            device_id_type=MESH,
        )

    sum_first = jnp.sum(resid, -1, keepdims=True)
    sum_second = jnp.sum(resid * resid, -1, keepdims=True)
    sums = jnp.transpose(jnp.where(lane < 4, sum_first, sum_second))[:8]
    stat_send[...] = sums
    for target in others:
        stat_copy(col, target).start()
    for source in others:
        stat_copy(source, source).wait_recv()
        sums += stat_recv[source]
    sums = jnp.transpose(jnp.concatenate([sums] * 16, 0))
    average = sums[:, 0:1] / model_width
    variance = sums[:, 4:5] / model_width - average * average
    final = (
        (resid - average) * lax.rsqrt(variance + epsilon) * final_gain_ref[...].reshape(1, -1)
    ).astype(jnp.bfloat16)

    def single_copy(source, target):
        return pltpu.make_async_remote_copy(
            src_ref=single_send.at[target],
            dst_ref=single_recv.at[source],
            send_sem=single_send_sem.at[target],
            recv_sem=single_recv_sem.at[source],
            device_id=(row, target),
            device_id_type=MESH,
        )

    loads[4].wait()
    part = jnp.dot(final, w_single[...], preferred_element_type=jnp.float32)
    for index in range(cols):
        block = part[index * piece : (index + 1) * piece]
        single_own[index] = block
        single_send[index] = block.astype(jnp.bfloat16)
    for target in others:
        single_copy(col, target).start()
    summed = single_own[col]
    for source in others:
        single_copy(source, source).wait_recv()
        summed += single_recv[source].astype(jnp.float32)
    lifted = jnp.maximum(summed, 0.0).astype(jnp.bfloat16)
    loads[5].wait()
    single = jnp.dot(lifted, w_second[...], preferred_element_type=jnp.float32)
    single = single.astype(jnp.bfloat16)

    def sides_copy(source, target):
        return pltpu.make_async_remote_copy(
            src_ref=sides.at[source],
            dst_ref=sides.at[source],
            send_sem=sides_send_sem.at[target],
            recv_sem=sides_recv_sem.at[source],
            device_id=(row, target),
            device_id_type=MESH,
        )

    def right_copy(slot, index, step):
        return pltpu.make_async_remote_copy(
            src_ref=right_own,
            dst_ref=right_all.at[slot, index],
            send_sem=right_send_sem.at[step],
            recv_sem=right_recv_sem.at[slot, index],
            device_id=((row + step) % rows, row // owners),
            device_id_type=MESH,
        )

    right_own[...] = jnp.dot(
        single, w_right_ref[...], preferred_element_type=jnp.float32
    ).astype(jnp.bfloat16)
    for step in range(1, rows):
        right_copy(row % owners, col, step).start()

    @pl.when(jnp.logical_not(is_owner))
    def _():
        right_copy(row % owners, col, 0).start()

    sides[col] = jnp.dot(single, w_left_ref[...], preferred_element_type=jnp.float32).astype(
        jnp.bfloat16
    )
    for target in others:
        sides_copy(col, target).start()

    @pl.when(is_owner)
    def _():
        right_all[row % owners, col] = right_own[...]

    for source in others:
        sides_copy(source, source).wait_recv()
    for index in range(cols):
        left_ref[index * piece : (index + 1) * piece] = sides[index]
    for slot in range(owners):
        for index in range(cols):

            @pl.when(jnp.logical_or(row != col * owners + slot, col != index))
            def _():
                right_copy(slot, index, 1).wait_recv()

            start_row = slot * count + index * piece
            right_ref[start_row : start_row + piece] = right_all[slot, index]

    for chunk in range(2):
        pass_on(row, chunk, True, True, finish)

    @pl.loop(1, chips)
    def _(step):
        for chunk in range(2):

            @pl.when(chip - step >= 0)
            def _():
                pass_on(row - 2 * step, chunk, True, False, finish)

            @pl.when(chip + step < chips)
            def _():
                pass_on(row + 2 * step, chunk, False, True, finish)

    for target in others:
        out_copy(col, target).wait_send()
        stat_copy(col, target).wait_send()
        single_copy(col, target).wait_send()
        sides_copy(col, target).wait_send()

    for step in range(1, rows):
        right_copy(row % owners, col, step).wait_send()

    @pl.when(jnp.logical_not(is_owner))
    def _():
        right_copy(row % owners, col, 0).wait_send()


def plane_kernel(
    rows,
    cols,
    model_width,
    hidden_ref,
    own_hbm,
    attn_gain_ref,
    cos_ref,
    sin_ref,
    cos_step_ref,
    sin_step_ref,
    final_gain_ref,
    w_query_hbm,
    w_key_hbm,
    w_value_hbm,
    w_out_hbm,
    w_single_hbm,
    w_second_hbm,
    w_left_ref,
    w_right_ref,
    bins_ref,
    table_ref,
    left_ref,
    right_ref,
    rel_hbm,
    flags_ref,
    w_query,
    w_key,
    w_value,
    w_out,
    w_single,
    w_second,
    own,
    piece_send,
    far,
    kv,
    query,
    totals,
    shares,
    numerator,
    w_sides,
    context,
    out_send,
    out_recv,
    stat_send,
    stat_recv,
    gain_sums,
    single_own,
    single_send,
    single_recv,
    sides,
    right_own,
    right_all,
    table,
    rel_slots,
    weight_sem,
    far_out_sem,
    far_send_sem,
    far_recv_sem,
    kv_send_sem,
    kv_recv_sem,
    out_send_sem,
    out_recv_sem,
    stat_send_sem,
    stat_recv_sem,
    single_send_sem,
    single_recv_sem,
    sides_send_sem,
    sides_recv_sem,
    right_send_sem,
    right_recv_sem,
    gain_send_sem,
    gain_recv_sem,
    rel_sem,
):
    row = lax.axis_index("row")
    col = lax.axis_index("col")
    count = hidden_ref.shape[0]
    pairs = query.shape[0]
    features = w_single.shape[0]
    piece = single_own.shape[1]
    owners = rows // cols
    chips = rows // 2
    chip = row // 2
    core = row % 2
    partner = row + 1 - 2 * core
    outer = jnp.logical_or(chip == 0, chip == chips - 1)
    farthest = (chips - 1 - chip) * 2 + core
    side = col + 1 - 2 * (col % 2)
    across = (col + 2) % cols
    corner = cols - 1 - col

    own_columns = pl.ds(pl.multiple_of(col * features, 128), features)
    loads = []
    for index, (source, target) in enumerate(
        (
            (w_key_hbm, w_key),
            (w_value_hbm, w_value),
            (w_query_hbm, w_query),
            (w_out_hbm, w_out),
            (w_single_hbm, w_single),
            (w_second_hbm, w_second),
            (own_hbm.at[:, own_columns], own),
        )
    ):
        load = pltpu.make_async_copy(source, target, weight_sem.at[index])
        load.start()
        loads.append(load)

    barrier = pltpu.get_barrier_semaphore()
    is_owner = row // owners == col

    def greet(target_row, target_col):
        pl.semaphore_signal(
            barrier, inc=1, device_id=(target_row, target_col), device_id_type=MESH
        )

    greet(partner, col)

    @pl.when(chip + 1 < chips)
    def _():
        greet(row + 2, col)

    @pl.when(chip >= 1)
    def _():
        greet(row - 2, col)

    @pl.when(outer)
    def _():
        greet(farthest, col)

    greetings = cols + jnp.where(outer, 1, 0)
    greetings += jnp.where(chip + 1 < chips, 1, 0) + jnp.where(chip >= 1, 1, 0)
    for step in range(1, cols):
        pl.semaphore_signal(
            barrier, inc=1, device_id=(row, (col + step) % cols), device_id_type=MESH
        )

    def normalize(values):
        stream = values.astype(jnp.float32)
        average = jnp.sum(stream, -1, keepdims=True) / model_width
        variance = jnp.sum(stream * stream, -1, keepdims=True) / model_width - average * average
        return (
            (stream - average) * lax.rsqrt(variance + epsilon) * attn_gain_ref[...].reshape(1, -1)
        ).astype(jnp.bfloat16)

    half = piece // 2

    @pl.when(outer)
    def _():
        for part in range(2):
            first = pl.multiple_of(col * piece + part * half, half)
            piece_send[part] = normalize(hidden_ref[pl.ds(first, half)])

    lane = lax.broadcasted_iota(jnp.int32, (count, 128), 1)
    first_half = lane % HD < HD // 2
    first_head = lane < HD

    def tables(source):
        cosine = cos_ref[...]
        sine = sin_ref[...]
        cos_step = cos_step_ref[pl.ds(source, 1), :]
        sin_step = sin_step_ref[pl.ds(source, 1), :]
        turned = sine * cos_step + cosine * sin_step
        return cosine * cos_step - sine * sin_step, jnp.where(first_half, -turned, turned)

    def rope(vectors, cosine, sine):
        turned = jnp.where(
            first_half,
            pltpu.roll(vectors, 128 - HD // 2, 1),
            pltpu.roll(vectors, HD // 2, 1),
        )
        return vectors * cosine + turned * sine

    def far_copy(owner, part, way, target):
        return pltpu.make_async_remote_copy(
            src_ref=far.at[owner, part],
            dst_ref=far.at[owner, part],
            send_sem=far_send_sem.at[way, part],
            recv_sem=far_recv_sem.at[owner, part],
            device_id=(row, target),
            device_id_type=MESH,
        )

    def far_out(part):
        return pltpu.make_async_remote_copy(
            src_ref=piece_send.at[part],
            dst_ref=far.at[col, part],
            send_sem=far_out_sem.at[part],
            recv_sem=far_recv_sem.at[col, part],
            device_id=(farthest, col),
            device_id_type=MESH,
        )

    def share(part, act):
        act(far_copy(col, part, 0, side))
        act(far_copy(col, part, 1, across))

    def share_corner(part, act):
        if part == 0:
            act(far_copy(side, part, 2, across))
        else:
            act(far_copy(across, part, 2, side))

    def far_wait(owner, part):
        far_copy(owner, part, 0, side).wait_recv()

    def kv_copy(source, chunk, way, target):
        return pltpu.make_async_remote_copy(
            src_ref=kv.at[source, chunk],
            dst_ref=kv.at[source, chunk],
            send_sem=kv_send_sem.at[way, source, chunk],
            recv_sem=kv_recv_sem.at[source, chunk],
            device_id=(target, col),
            device_id_type=MESH,
        )

    def pass_on(source, chunk, right, left, act):
        if right:

            @pl.when(chip + 1 < chips)
            def _():
                act(kv_copy(source, chunk, 0, row + 2))

        if left:

            @pl.when(chip >= 1)
            def _():
                act(kv_copy(source, chunk, 1, row - 2))

        act(kv_copy(source, chunk, 2, partner))

    def start(copy):
        copy.start()

    def finish(copy):
        copy.wait_send()

    def keys_of(rows_in, source):
        cosine, sine = tables(source)
        projected = jnp.dot(rows_in, w_key[...], preferred_element_type=jnp.float32)
        for pair in range(pairs):
            kv[source, 0, pair] = rope(
                projected[:, pair * 128 : pair * 128 + 128], cosine, sine
            ).astype(jnp.bfloat16)

    def values_of(rows_in, source):
        projected = jnp.dot(rows_in, w_value[...], preferred_element_type=jnp.float32)
        for pair in range(pairs):
            kv[source, 1, pair] = projected[:, pair * 128 : pair * 128 + 128].astype(jnp.bfloat16)

    pl.semaphore_wait(barrier, greetings)

    @pl.when(outer)
    def _():
        for part in range(2):
            far_out(part).start()

    attn_in = normalize(hidden_ref[...])
    loads[0].wait()
    keys_of(attn_in, row)
    pass_on(row, 0, True, True, start)
    loads[1].wait()
    values_of(attn_in, row)
    pass_on(row, 1, True, True, start)

    def gain_copy(source, target):
        return pltpu.make_async_remote_copy(
            src_ref=gain_sums.at[source],
            dst_ref=gain_sums.at[source],
            send_sem=gain_send_sem.at[target],
            recv_sem=gain_recv_sem.at[source],
            device_id=(row, target),
            device_id_type=MESH,
        )

    others = [corner, side, across]
    loads[2].wait()
    cosine, sine = tables(row)
    projected = jnp.dot(attn_in, w_query[...], preferred_element_type=jnp.float32) * HD ** (-0.5)
    for pair in range(pairs):
        turned = rope(projected[:, pair * 128 : pair * 128 + 128], cosine, sine)
        query[pair, :count] = jnp.where(first_head, turned, 0.0).astype(jnp.bfloat16)
        query[pair, count:] = jnp.where(first_head, 0.0, turned).astype(jnp.bfloat16)
    bins = table_ref.shape[0]
    table[...] = jnp.zeros_like(table)
    table[:bins] = table_ref[...]
    slot_rows = rel_slots.shape[1]
    col_count = bins_ref.shape[1]
    slots = bins_ref.shape[0] // slot_rows

    def rel_copy(index):
        return pltpu.make_async_copy(
            rel_slots.at[index % 2],
            rel_hbm.at[pl.ds(pl.multiple_of(index * slot_rows, slot_rows), slot_rows)],
            rel_sem.at[index % 2],
        )

    def spell(begin, end):
        @pl.loop(begin, end)
        def _(index):
            @pl.when(index >= 2)
            def _():
                rel_copy(index - 2).wait()

            picked = bins_ref[pl.ds(pl.multiple_of(index * slot_rows, slot_rows), slot_rows)]
            codes = lax.broadcasted_iota(jnp.int32, (table.shape[0], col_count), 0)
            hot = jnp.concatenate(
                [
                    jnp.where(picked[i : i + 1, :] == codes, 1.0, 0.0).astype(jnp.bfloat16)
                    for i in range(slot_rows)
                ],
                1,
            )
            chosen = lax.dot_general(
                hot, table[...], (((0,), (0,)), ((), ())), preferred_element_type=jnp.float32
            )
            rel_slots[index % 2] = chosen.astype(jnp.bfloat16).reshape(rel_slots.shape[1:])
            rel_copy(index).start()

    totals[...] = jnp.zeros_like(totals)
    numerator[...] = jnp.zeros_like(numerator)

    def score(source, slot):
        for pair in range(pairs):
            keys = kv[pl.ds(2 * source, 2), 0, pair].reshape(2 * count, 128)
            weights = jnp.exp(
                lax.dot_general(
                    query[pair],
                    keys,
                    (((1,), (1,)), ((), ())),
                    preferred_element_type=jnp.float32,
                )
            )
            totals[pair] += weights[:, :count] + weights[:, count:]
            shares[slot, pair] = weights.astype(jnp.bfloat16)

    def mix(source, slot):
        for pair in range(pairs):
            values = kv[pl.ds(2 * source, 2), 1, pair].reshape(2 * count, 128)
            numerator[pair] += jnp.dot(
                shares[slot, pair], values, preferred_element_type=jnp.float32
            )

    def arrive(source, chunk):
        kv_copy(source, chunk, 2, partner).wait_recv()

    arrive(partner, 0)
    score(chip, 0)
    loads[4].wait()
    gain = final_gain_ref[...].reshape(1, -1)
    coarse = gain.astype(jnp.bfloat16)
    fine = (gain - coarse.astype(jnp.float32)).astype(jnp.bfloat16)
    gains = jnp.concatenate([jnp.broadcast_to(part, (16, features)) for part in (coarse, fine)], 0)
    gained = jnp.dot(gains, w_single[...], preferred_element_type=jnp.float32)
    gain_sums[col] = gained[:8] + gained[16:24]
    for target in others:
        gain_copy(col, target).start()

    arrive(partner, 1)
    mix(chip, 0)

    grouped = bins_ref[...].reshape(flags_ref.shape[0], -1, col_count)
    high = jnp.max(grouped, 1)
    low = jnp.min(grouped, 1)
    spot = lax.broadcasted_iota(jnp.int32, flags_ref.shape, 1)
    flags = jnp.full(flags_ref.shape, -1, jnp.int32)
    width = col_count // CHUNKS
    for index in range(CHUNKS):
        span = slice(index * width, (index + 1) * width)
        top = jnp.max(high[:, span], -1, keepdims=True)
        bottom = jnp.min(low[:, span], -1, keepdims=True)
        flags = jnp.where(spot == index, jnp.where(top == bottom, top, -1), flags)
    flags_ref[...] = flags
    early = jnp.where(outer, slots, 4)
    spell(0, 2)

    @pl.when(outer)
    def _():
        for part in range(2):
            far_wait(col, part)
            share(part, start)

    spell(2, early)

    @pl.when(outer)
    def _():
        far_wait(side, 0)
        share_corner(0, start)
        far_wait(across, 1)
        share_corner(1, start)


    def near(step, onward):
        from_left = chip - step >= 0
        from_right = chip + step < chips

        def receive(chunk):
            @pl.when(from_left)
            def _():
                arrive(row - 2 * step, chunk)
                pass_on(row - 2 * step, chunk, onward, False, start)

            @pl.when(from_right)
            def _():
                arrive(row + 2 * step, chunk)
                pass_on(row + 2 * step, chunk, False, onward, start)

        def use(chunk):
            @pl.when(from_left)
            def _():
                arrive(partner - 2 * step, chunk)
                (mix if chunk else score)(chip - step, 0)

            @pl.when(from_right)
            def _():
                arrive(partner + 2 * step, chunk)
                (mix if chunk else score)(chip + step, 1)

        receive(0)
        if onward:
            receive(1)
        use(0)
        if not onward:
            receive(1)
        use(1)

    for step in range(1, chips - 1):
        near(step, step < chips - 2)
        if step == 1:
            loads[5].wait()
            w_sides[...] = jnp.dot(
                w_second[...],
                jnp.concatenate([w_left_ref[...], w_right_ref[...]], 1),
                preferred_element_type=jnp.float32,
            ).astype(jnp.bfloat16)
            spell(early, slots)

            @pl.when(outer)
            def _():
                far_wait(side, 1)
                far_wait(across, 0)
                for part in range(2):
                    far_wait(corner, part)
                rows_in = far[...].reshape(count, model_width)
                keys_of(rows_in, farthest)
                pass_on(farthest, 0, False, False, start)
                values_of(rows_in, farthest)
                pass_on(farthest, 1, False, False, start)
                for chunk in range(2):
                    arrive(farthest + partner - row, chunk)
                    (mix if chunk else score)(chips - 1 - chip, 0)


    for pair in range(pairs):
        mixed = numerator[pair] / jnp.sum(totals[pair], -1, keepdims=True)
        context[:, pair * 128 : pair * 128 + 128] = jnp.where(
            first_head, mixed[:count], mixed[count:]
        ).astype(jnp.bfloat16)

    split = count // 2
    halves = [slice(0, split), slice(split, count)]
    firsts = (side, across)
    seconds = (across, side)

    def out_copy(slot, target):
        return pltpu.make_async_remote_copy(
            src_ref=out_send.at[slot],
            dst_ref=out_recv.at[slot],
            send_sem=out_send_sem.at[slot],
            recv_sem=out_recv_sem.at[slot],
            device_id=(row, target),
            device_id_type=MESH,
        )

    def out_part(target):
        columns = pl.ds(pl.multiple_of(target * features, 128), features)
        return jnp.dot(context[...], w_out[:, columns], preferred_element_type=jnp.float32)

    loads[3].wait()
    passing = out_part(corner).astype(jnp.bfloat16)
    for half in range(2):
        out_send[half] = passing[halves[half]]
        out_copy(half, firsts[half]).start()
    kept = [None, None]
    for half in range(2):
        passing = out_part(firsts[half])
        out_send[2 + half] = passing[halves[half]].astype(jnp.bfloat16)
        out_copy(2 + half, firsts[half]).start()
        kept[1 - half] = passing[halves[1 - half]]
    for half in range(2):
        out_copy(half, firsts[half]).wait_recv()
        out_send[4 + half] = (kept[half] + out_recv[half].astype(jnp.float32)).astype(jnp.bfloat16)
        out_copy(4 + half, seconds[half]).start()
    loads[6].wait()
    resid = own[...].astype(jnp.float32) + out_part(col)
    collected = []
    for half in range(2):
        out_copy(2 + half, firsts[half]).wait_recv()
        out_copy(4 + half, seconds[half]).wait_recv()
        collected.append(
            resid[halves[half]]
            + out_recv[2 + half].astype(jnp.float32)
            + out_recv[4 + half].astype(jnp.float32)
        )
    resid = jnp.concatenate(collected, 0)

    def stat_copy(source, target):
        return pltpu.make_async_remote_copy(
            src_ref=stat_send.at[target],
            dst_ref=stat_recv.at[source],
            send_sem=stat_send_sem.at[target],
            recv_sem=stat_recv_sem.at[source],
            device_id=(row, target),
            device_id_type=MESH,
        )

    middle = jnp.sum(resid, -1, keepdims=True) / features
    centred = resid - middle
    spread_sum = jnp.sum(centred * centred, -1, keepdims=True)
    stats = jnp.where(lane < 1, middle, spread_sum)
    for index in range(cols):
        stat_send[index] = stats[index * piece : (index + 1) * piece]
    for target in others:
        stat_copy(col, target).start()
    final = (centred * final_gain_ref[...].reshape(1, -1)).astype(jnp.bfloat16)

    def single_copy(source, target):
        return pltpu.make_async_remote_copy(
            src_ref=single_send.at[target],
            dst_ref=single_recv.at[source],
            send_sem=single_send_sem.at[target],
            recv_sem=single_recv_sem.at[source],
            device_id=(row, target),
            device_id_type=MESH,
        )

    part = jnp.dot(final, w_single[...], preferred_element_type=jnp.float32)
    for index in range(cols):
        block = part[index * piece : (index + 1) * piece]
        single_own[index] = block
        single_send[index] = block.astype(jnp.bfloat16)
    for target in others:
        single_copy(col, target).start()
    for source in others:
        stat_copy(source, source).wait_recv()
        gain_copy(source, source).wait_recv()
    stat_recv[col] = stat_send[col]
    middles = [stat_recv[index][:, 0:1] for index in range(cols)]
    average = sum(middles) / cols
    variance = sum(stat_recv[index][:, 1:2] for index in range(cols)) / model_width
    variance += sum((middles[index] - average) * (middles[index] - average) for index in range(cols)) / cols
    scale = lax.rsqrt(variance + epsilon)
    summed = single_own[col]
    for index in range(cols):
        summed += (middles[index] - average) * gain_sums[index][0:1]
    for source in others:
        single_copy(source, source).wait_recv()
        summed += single_recv[source].astype(jnp.float32)
    lifted = jnp.maximum(summed * scale, 0.0).astype(jnp.bfloat16)
    channels = w_left_ref.shape[1]
    both = jnp.dot(lifted, w_sides[...], preferred_element_type=jnp.float32).astype(jnp.bfloat16)

    def sides_copy(source, target):
        return pltpu.make_async_remote_copy(
            src_ref=sides.at[source],
            dst_ref=sides.at[source],
            send_sem=sides_send_sem.at[target],
            recv_sem=sides_recv_sem.at[source],
            device_id=(row, target),
            device_id_type=MESH,
        )

    def right_copy(slot, index, step):
        return pltpu.make_async_remote_copy(
            src_ref=right_own,
            dst_ref=right_all.at[slot, index],
            send_sem=right_send_sem.at[step],
            recv_sem=right_recv_sem.at[slot, index],
            device_id=((row + step) % rows, row // owners),
            device_id_type=MESH,
        )

    right_own[...] = both[:, channels:]
    for step in sorted(range(1, rows), key=lambda step: abs(2 * step - rows)):
        right_copy(row % owners, col, step).start()

    @pl.when(jnp.logical_not(is_owner))
    def _():
        right_copy(row % owners, col, 0).start()

    sides[col] = both[:, :channels]
    for target in others:
        sides_copy(col, target).start()

    @pl.when(is_owner)
    def _():
        right_all[row % owners, col] = right_own[...]

    for source in others:
        sides_copy(source, source).wait_recv()
    for index in range(cols):
        left_ref[index * piece : (index + 1) * piece] = sides[index]
    for slot in range(owners):
        for index in range(cols):

            @pl.when(jnp.logical_or(row != col * owners + slot, col != index))
            def _():
                right_copy(slot, index, 1).wait_recv()

            start_row = slot * count + index * piece
            right_ref[start_row : start_row + piece] = right_all[slot, index]

    for chunk in range(2):
        pass_on(row, chunk, True, True, finish)
        for step in range(1, chips - 1):

            @pl.when(chip - step >= 0)
            def _():
                pass_on(row - 2 * step, chunk, step < chips - 2, False, finish)

            @pl.when(chip + step < chips)
            def _():
                pass_on(row + 2 * step, chunk, False, step < chips - 2, finish)

    @pl.when(outer)
    def _():
        for part in range(2):
            pass_on(farthest, part, False, False, finish)
            far_out(part).wait_send()
            share(part, finish)
            share_corner(part, finish)

    rel_copy(slots - 2).wait()
    rel_copy(slots - 1).wait()
    for half in range(2):
        out_copy(half, firsts[half]).wait_send()
        out_copy(2 + half, firsts[half]).wait_send()
        out_copy(4 + half, seconds[half]).wait_send()
    for target in others:
        stat_copy(col, target).wait_send()
        single_copy(col, target).wait_send()
        sides_copy(col, target).wait_send()
        gain_copy(col, target).wait_send()

    for step in range(1, rows):
        right_copy(row % owners, col, step).wait_send()

    @pl.when(jnp.logical_not(is_owner))
    def _():
        right_copy(row % owners, col, 0).wait_send()


def padded(array, axis, size, groups=1):
    width = array.shape[axis] // groups
    if width == size:
        return array
    shape = array.shape
    array = array.reshape(shape[:axis] + (groups, width) + shape[axis + 1 :])
    pads = [(0, 0)] * array.ndim
    pads[axis + 1] = (0, size - width)
    array = jnp.pad(array, pads)
    return array.reshape(shape[:axis] + (groups * size,) + shape[axis + 1 :])


def front_general(
    hidden,
    attn_gain,
    w_query,
    w_key,
    w_value,
    w_out,
    final_gain,
    w_single,
    w_second,
    w_left,
    w_right,
):
    rows = lax.axis_size("row")
    cols = lax.axis_size("col")
    count, model_width = hidden.shape
    width = -(-w_query.shape[1] // 128) * 128
    features = -(-w_single.shape[0] // 128) * 128
    pairs = width // 128
    piece = count // cols
    owners = rows // cols
    single_width = w_second.shape[0]
    channels = w_left.shape[1]
    positions = lax.axis_index("row") * count + jnp.arange(count, dtype=jnp.int32)
    frequency = jnp.exp(
        jnp.arange(HD // 2, dtype=jnp.float32) * (-2.0 * math.log(10000.0) / HD)
    )
    angles = positions.astype(jnp.float32)[:, None] * frequency[None, :]
    cosine = jnp.cos(angles)
    sine = jnp.sin(angles)
    cosine = jnp.concatenate([cosine] * 4, -1)
    sine = jnp.concatenate([-sine, sine, -sine, sine], -1)
    weights = (
        padded(w_query, 1, width),
        padded(w_key, 1, width),
        padded(w_value, 1, width),
        padded(padded(w_out, 0, width), 1, features, cols),
        padded(w_single, 0, features),
        w_second,
    )
    vmem = pl.BlockSpec(memory_space=pltpu.VMEM)
    anywhere = pl.BlockSpec(memory_space=pl.ANY)
    bf16 = jnp.bfloat16
    f32 = jnp.float32
    dma = pltpu.SemaphoreType.DMA
    return pl.pallas_call(
        functools.partial(front_kernel, rows, cols, model_width),
        out_shape=(
            jax.ShapeDtypeStruct((count, channels), bf16),
            jax.ShapeDtypeStruct((owners * count, channels), bf16),
        ),
        in_specs=[vmem, anywhere] + [vmem] * 4 + [anywhere] * 6 + [vmem] * 2,
        out_specs=(vmem, vmem),
        scratch_shapes=[pltpu.VMEM(weight.shape, bf16) for weight in weights]
        + [
            pltpu.VMEM((count, features), bf16),
            pltpu.VMEM((rows, 2, pairs, count, 128), bf16),
            pltpu.VMEM((pairs, 2 * count, 128), bf16),
            pltpu.VMEM((pairs, 2 * count, count), f32),
            pltpu.VMEM((pairs, 2 * count, 128), f32),
            pltpu.VMEM((count, width), bf16),
            pltpu.VMEM((cols, count, features), bf16),
            pltpu.VMEM((cols, count, features), bf16),
            pltpu.VMEM((8, count), f32),
            pltpu.VMEM((cols, 8, count), f32),
            pltpu.VMEM((cols, piece, single_width), f32),
            pltpu.VMEM((cols, piece, single_width), bf16),
            pltpu.VMEM((cols, piece, single_width), bf16),
            pltpu.VMEM((cols, piece, channels), bf16),
            pltpu.VMEM((piece, channels), bf16),
            pltpu.VMEM((owners, cols, piece, channels), bf16),
            dma((7,)),
            dma((3, rows, 2)),
            dma((rows, 2)),
            dma((cols,)),
            dma((cols,)),
            dma((cols,)),
            dma((cols,)),
            dma((cols,)),
            dma((cols,)),
            dma((cols,)),
            dma((cols,)),
            dma((rows,)),
            dma((owners, cols)),
        ],
        compiler_params=pltpu.CompilerParams(
            collective_id=0, has_side_effects=True, vmem_limit_bytes=56 << 20
        ),
    )(
        hidden,
        padded(hidden, 1, features, cols),
        attn_gain,
        cosine,
        sine,
        padded(final_gain, 0, features),
        *weights,
        w_left,
        w_right,
    )


def banded_kernel(
    flags,
    rel_ref,
    left_ref,
    right_ref,
    table_ref,
    gain_ref,
    expand_ref,
    contract_ref,
    out_ref,
    table,
    left_parts,
    right_parts,
    table_parts,
    left_wide,
    right_wide,
    table_wide,
):
    block_rows, col_count, channels = out_ref.shape
    bins = table_ref.shape[0]
    chunk = col_count // CHUNKS
    width = WINDOW * chunk
    sub = SUB

    @pl.when(pl.program_id(0) == 0)
    def _():
        table[...] = jnp.zeros_like(table)
        table[:bins] = table_ref[...]
        gain = gain_ref[...]
        weights = jnp.concatenate([expand_ref[...]] * 2, 0)
        for source, parts, wide in (
            (left_ref, left_parts, left_wide),
            (right_ref, right_parts, right_wide),
            (table, table_parts, table_wide),
        ):
            values = source[...].astype(jnp.float32)
            centred = values - jnp.sum(values, -1, keepdims=True) / channels
            parts[0] = values
            parts[1] = centred
            scaled = centred * gain
            coarse = scaled.astype(jnp.bfloat16)
            fine = (scaled - coarse.astype(jnp.float32)).astype(jnp.bfloat16)
            wide[...] = jnp.dot(
                jnp.concatenate([coarse, fine], 1), weights, preferred_element_type=jnp.float32
            )

    gain = gain_ref[...]

    def block(first, local, group, start, mixed_width, places):
        sums = []
        scales = []
        expanded = []
        targets = []
        if mixed_width:
            right = right_parts[0, pl.ds(start, mixed_width)]
            pair_in = jnp.concatenate(
                [
                    rel_ref[local + i, pl.ds(start, mixed_width)].astype(jnp.float32)
                    + (right + left_parts[0, pl.ds(first + i, 1)])
                    for i in range(sub)
                ],
                0,
            )
            average = jnp.sum(pair_in, -1, keepdims=True) / channels
            variance = (
                jnp.sum(pair_in * pair_in, -1, keepdims=True) / channels - average * average
            )
            normed = ((pair_in - average) * lax.rsqrt(variance + epsilon) * gain).astype(
                jnp.bfloat16
            )
            wide = jnp.dot(normed, expand_ref[...], preferred_element_type=jnp.float32)
            wide = jnp.maximum(wide.astype(jnp.bfloat16), 0)
            for i in range(sub):
                rows = slice(i * mixed_width, (i + 1) * mixed_width)
                targets.append((local + i, start, mixed_width))
                sums.append(pair_in[rows])
                scales.append(None)
                expanded.append(wide[rows])
        for place in places:
            begin = pl.multiple_of(place * chunk, chunk)
            span = pl.ds(begin, chunk)
            spot = pl.ds(flags[group, place], 1)
            right = right_parts[0, span]
            right_centred = right_parts[1, span]
            right_up = right_wide[span]
            for i in range(sub):
                one = pl.ds(first + i, 1)
                base = left_parts[0, one] + table_parts[0, spot]
                base_centred = left_parts[1, one] + table_parts[1, spot]
                base_up = left_wide[one] + table_wide[spot]
                centred = right_centred + base_centred
                variance = jnp.sum(centred * centred, -1, keepdims=True) / channels
                targets.append((local + i, begin, chunk))
                scales.append(lax.rsqrt(variance + epsilon))
                sums.append(right + base)
                expanded.append(jnp.maximum((right_up + base_up).astype(jnp.bfloat16), 0))
        update = jnp.dot(
            jnp.concatenate(expanded, 0), contract_ref[...], preferred_element_type=jnp.float32
        )
        row = 0
        for total, scale, (place, begin, size) in zip(sums, scales, targets):
            piece = update[row : row + size]
            if scale is not None:
                piece = piece * scale
            out_ref[place, pl.ds(begin, size)] = (total + piece).astype(out_ref.dtype)
            row += size

    @pl.loop(0, block_rows // sub)
    def _(step):
        local = pl.multiple_of(step * sub, sub)
        first = pl.multiple_of(pl.program_id(0) * block_rows + local, sub)
        group = pl.program_id(0) * (block_rows // sub) + step
        begin = jnp.int32(CHUNKS)
        end = jnp.int32(0)
        for index in range(CHUNKS):
            ragged = flags[group, index] < 0
            begin = jnp.where(jnp.logical_and(ragged, begin == CHUNKS), index, begin)
            end = jnp.where(ragged, index + 1, end)
        none = end == 0
        few = jnp.logical_and(end > 0, end - begin <= WINDOW)

        @pl.when(none)
        def _():
            block(first, local, group, 0, 0, range(CHUNKS))

        @pl.when(few)
        def _():
            window = jnp.minimum(begin, CHUNKS - WINDOW)
            places = [
                jnp.where(index < window, index, index + WINDOW)
                for index in range(CHUNKS - WINDOW)
            ]
            block(first, local, group, pl.multiple_of(window * chunk, chunk), width, places)

        @pl.when(end - begin > WINDOW)
        def _():
            block(first, local, group, 0, col_count, ())


def banded_stage(flags, rel, left, right, rel_table, pair_gain, w_expand, w_contract):
    row_count, col_count, _ = rel.shape
    channels = right.shape[1]
    hidden_width = w_expand.shape[1]
    block_rows = math.gcd(row_count, SUB)
    bins_padded = -(-rel_table.shape[0] // 16) * 16
    whole = lambda array: pl.BlockSpec(array.shape, lambda i: (0, 0))
    gain = pair_gain.reshape(1, channels)
    operands = (flags, rel, left, right, rel_table, gain, w_expand, w_contract)
    tile = pl.BlockSpec((block_rows, col_count, channels), lambda i: (i, 0, 0))
    f32 = jnp.float32
    return pl.pallas_call(
        banded_kernel,
        grid=(row_count // block_rows,),
        in_specs=[pl.BlockSpec(memory_space=pltpu.SMEM), tile]
        + [whole(operand) for operand in operands[2:]],
        out_specs=tile,
        out_shape=jax.ShapeDtypeStruct((row_count, col_count, channels), jnp.bfloat16),
        scratch_shapes=[
            pltpu.VMEM((bins_padded, channels), jnp.bfloat16),
            pltpu.VMEM((2, row_count, channels), f32),
            pltpu.VMEM((2, col_count, channels), f32),
            pltpu.VMEM((2, bins_padded, channels), f32),
            pltpu.VMEM((row_count, hidden_width), f32),
            pltpu.VMEM((col_count, hidden_width), f32),
            pltpu.VMEM((bins_padded, hidden_width), f32),
        ],
        compiler_params=pltpu.CompilerParams(
            dimension_semantics=("arbitrary",), vmem_limit_bytes=56 << 20
        ),
    )(*operands)


def front_plane(
    hidden,
    attn_gain,
    w_query,
    w_key,
    w_value,
    w_out,
    final_gain,
    w_single,
    w_second,
    w_left,
    w_right,
    rel_bins,
    rel_table,
):
    rows = lax.axis_size("row")
    cols = lax.axis_size("col")
    count, model_width = hidden.shape
    width = -(-w_query.shape[1] // 128) * 128
    features = -(-w_single.shape[0] // 128) * 128
    pairs = width // 128
    piece = count // cols
    owners = rows // cols
    single_width = w_second.shape[0]
    channels = w_left.shape[1]
    frequency = np.exp(np.arange(HD // 2) * (-2.0 * math.log(10000.0) / HD))
    frequency = np.concatenate([frequency] * 4)[None, :]
    offsets = np.arange(count)[:, None] * frequency
    steps = (np.arange(rows) * count)[:, None] * frequency
    angles = [
        jnp.asarray(turn(angle), jnp.float32)
        for angle in (offsets, steps)
        for turn in (np.cos, np.sin)
    ]
    weights = (w_query, w_key, w_value, w_out, w_single, w_second)
    vmem = pl.BlockSpec(memory_space=pltpu.VMEM)
    anywhere = pl.BlockSpec(memory_space=pl.ANY)
    bf16 = jnp.bfloat16
    f32 = jnp.float32
    dma = pltpu.SemaphoreType.DMA
    return pl.pallas_call(
        functools.partial(plane_kernel, rows, cols, model_width),
        out_shape=(
            jax.ShapeDtypeStruct((count, channels), bf16),
            jax.ShapeDtypeStruct((owners * count, channels), bf16),
            jax.ShapeDtypeStruct(rel_bins.shape + (channels,), bf16),
            jax.ShapeDtypeStruct((rel_bins.shape[0] // SUB, 128), jnp.int32),
        ),
        in_specs=[vmem, anywhere] + [vmem] * 6 + [anywhere] * 6 + [vmem] * 4,
        out_specs=(vmem, vmem, anywhere, vmem),
        scratch_shapes=[pltpu.VMEM(weight.shape, bf16) for weight in weights]
        + [
            pltpu.VMEM((count, features), bf16),
            pltpu.VMEM((2, piece // 2, model_width), bf16),
            pltpu.VMEM((cols, 2, piece // 2, model_width), bf16),
            pltpu.VMEM((rows, 2, pairs, count, 128), bf16),
            pltpu.VMEM((pairs, 2 * count, 128), bf16),
            pltpu.VMEM((pairs, 2 * count, count), f32),
            pltpu.VMEM((2, pairs, 2 * count, 2 * count), bf16),
            pltpu.VMEM((pairs, 2 * count, 128), f32),
            pltpu.VMEM((single_width, 2 * channels), bf16),
            pltpu.VMEM((count, width), bf16),
            pltpu.VMEM((6, count // 2, features), bf16),
            pltpu.VMEM((6, count // 2, features), bf16),
            pltpu.VMEM((cols, piece, 128), f32),
            pltpu.VMEM((cols, piece, 128), f32),
            pltpu.VMEM((cols, 8, single_width), f32),
            pltpu.VMEM((cols, piece, single_width), f32),
            pltpu.VMEM((cols, piece, single_width), bf16),
            pltpu.VMEM((cols, piece, single_width), bf16),
            pltpu.VMEM((cols, piece, channels), bf16),
            pltpu.VMEM((piece, channels), bf16),
            pltpu.VMEM((owners, cols, piece, channels), bf16),
            pltpu.VMEM((-(-rel_table.shape[0] // 16) * 16, channels), bf16),
            pltpu.VMEM((2, rel_bins.shape[0] // 8, rel_bins.shape[1], channels), bf16),
            dma((7,)),
            dma((2,)),
            dma((3, 2)),
            dma((cols, 2)),
            dma((3, rows, 2)),
            dma((rows, 2)),
            dma((6,)),
            dma((6,)),
            dma((cols,)),
            dma((cols,)),
            dma((cols,)),
            dma((cols,)),
            dma((cols,)),
            dma((cols,)),
            dma((rows,)),
            dma((owners, cols)),
            dma((cols,)),
            dma((cols,)),
            dma((2,)),
        ],
        compiler_params=pltpu.CompilerParams(
            collective_id=0, has_side_effects=True, vmem_limit_bytes=56 << 20
        ),
    )(
        hidden,
        hidden,
        attn_gain,
        *angles,
        final_gain,
        *weights,
        w_left,
        w_right,
        rel_bins,
        rel_table,
    )


def local(
    hidden,
    rel_bins,
    attn_gain,
    w_query,
    w_key,
    w_value,
    w_out,
    final_gain,
    w_single,
    w_second,
    w_left,
    w_right,
    rel_table,
    pair_gain,
    w_expand,
    w_contract,
):
    rows = lax.axis_size("row")
    cols = lax.axis_size("col")
    aligned = w_query.shape[1] % 128 == 0 and hidden.shape[0] % (32 * cols) == 0
    operands = (
        hidden,
        attn_gain,
        w_query,
        w_key,
        w_value,
        w_out,
        final_gain,
        w_single,
        w_second,
        w_left,
        w_right,
    )
    if rows == 2 * cols and cols == 4 and aligned and rel_bins.shape[1] % (16 * CHUNKS) == 0:
        left, right, rel, flags = front_plane(*operands, rel_bins, rel_table)
        return banded_stage(
            flags, rel, left, right, rel_table, pair_gain, w_expand, w_contract
        )
    left, right = front_general(*operands)
    return pair_stage(rel_bins, left, right, rel_table, pair_gain, w_expand, w_contract)


def solution(mesh):
    in_specs = (
        P("row", None),
        P("row", "col"),
        P(),
        P(None, "col"),
        P(None, "col"),
        P(None, "col"),
        P("col", None),
        P("col"),
        P("col", None),
        P(),
        P(),
        P(),
        P(),
        P(),
        P(),
        P(),
    )
    out_specs = P("row", "col", None)
    return jax.shard_map(local, mesh=mesh, in_specs=in_specs, out_specs=out_specs, check_vma=False)
```
